32 devices in a mesh: dp: 4 (over y, x), expert: 8 (over z, core).
Axes of the slice: x: 2, y: 2, z: 4, core: 2. Of those that a mesh axis runs over, the one named last changes fastest.
Arguments:
- tokens: bfloat16 [32768, 768], P(('dp', 'expert')), may hold values from -6 to 6
- cotangent: bfloat16 [32768, 768], P(('dp', 'expert')), may hold values from -6 to 6
- seg_start: int32 [32768], P(('dp', 'expert')), may hold values from 0 to 1023, as said below
- dispatch_slot: int32 [32768], P(('dp', 'expert')), may hold values from 0 to 2048, as said below
- ln1_gain: float32 [768], replicated, may hold values from 0.25 to 1.75
- ln1_shift: float32 [768], replicated, may hold values from -3 to 3
- w_qkv: bfloat16 [768, 2304], replicated, may hold values from -0.21875 to 0.21875
- w_attn_out: bfloat16 [768, 768], replicated, may hold values from -0.875 to 0.875
- ln2_gain: float32 [768], replicated, may hold values from 0.25 to 1.75
- ln2_shift: float32 [768], replicated, may hold values from -3 to 3
- w_in: bfloat16 [2, 768, 3072], replicated, may hold values from -0.21875 to 0.21875
- w_out: bfloat16 [2, 3072, 768], replicated, may hold values from -0.109375 to 0.109375
Outputs:
- result_out: bfloat16 [32768, 768], P(('dp', 'expert'))
- grad_tokens: float32 [32768, 768], P(('dp', 'expert'))
- grad_ln1_gain: float32 [768], replicated
- grad_ln1_shift: float32 [768], replicated
- grad_w_qkv: float32 [768, 2304], replicated
- grad_w_attn_out: float32 [768, 768], replicated
- grad_ln2_gain: float32 [768], replicated
- grad_ln2_shift: float32 [768], replicated
- grad_w_in: float32 [2, 768, 3072], P(None, None, 'expert')
- grad_w_out: float32 [2, 3072, 768], P(None, 'expert')
- expert_counts: int32 [2], replicated
The draws below stay inside these ranges and needn't reach their ends.
Inputs may be any that keep to these rules, and one draw needn't show every extreme that they name: A row is an image row or a caption row. An image row's first 985 slots hold 5 images of 197 patches each, its other slots are padding, each padding token a segment of its own; a caption row is filled with captions. A token attends only to tokens of its own row with the same seg_start. `dispatch_slot`: slot s sends the token to the device at expert index s // 256 of its dp index, at place s % 256. Image tokens go to expert indices below 4, caption tokens to the others; no two tokens of one device share a slot; padding tokens, and only they, have s = 2048.
All inputs are finite; a program needn't handle non-finite values.
Results may differ from the reference program's by a relative error of at most 0.012.
Values may be sent and summed in bfloat16 or wider, within the bound.
No kernel may reach another device: no remote copies, remote signals or barrier semaphores. Data moves between devices by JAX's collectives and lax.ppermute only.
A program may use at most 320 MiB of HBM per device.

```python
import math
import jax
import jax.numpy as jnp
from jax import lax

D = 768
HEADS = 12
DH = 64
FF = 3072
EXPERTS = 2
LEN = 1024
IMAGES = 5
PATCHES = 197
CAPTION = 24
ROWS_DEV = 1
TOK_DEV = 1024
TOKENS = 32768
HALF = 4
CAP = 256
SLOTS = 2048
N_EXPERT = 8


def layout(key):
    devices = TOKENS // TOK_DEV
    row_total = TOKENS // LEN
    key_rows, key_caps, key_offs = jax.random.split(key, 3)
    row_index = jnp.arange(row_total, dtype=jnp.int32)
    row_picks = jax.random.randint(key_rows, (row_total,), 0, 4 * row_total)
    owner_dev = row_index // ROWS_DEV
    image_row = row_picks < row_total + 2 * row_index
    image_row = jnp.where(owner_dev == 0, False, image_row)
    image_row = jnp.where(owner_dev == devices - 1, True, image_row)
    position = jnp.arange(LEN, dtype=jnp.int32)
    in_image = position < IMAGES * PATCHES
    image_seg = jnp.where(in_image, position // PATCHES * PATCHES, position)
    starts = jax.random.randint(key_caps, (row_total, LEN), 0, CAPTION) == 0
    starts = jnp.logical_or(starts, position[None, :] == 0)
    caption_seg = lax.cummax(jnp.where(starts, position[None, :], 0), axis=1)
    seg_ids = jnp.where(image_row[:, None], image_seg[None, :], caption_seg)
    is_real = jnp.logical_or(jnp.logical_not(image_row)[:, None], in_image[None, :])
    modality = jnp.broadcast_to(jnp.where(image_row, 0, 1)[:, None], (row_total, LEN)).astype(jnp.int32)
    is_real = is_real.reshape(devices, TOK_DEV)
    modality = modality.reshape(devices, TOK_DEV)
    vision = jnp.logical_and(is_real, modality == 0).astype(jnp.int32)
    language = jnp.logical_and(is_real, modality == 1).astype(jnp.int32)
    token_rank = jnp.where(modality == 0, jnp.cumsum(vision, axis=1) - vision, jnp.cumsum(language, axis=1) - language)
    offsets = jax.random.randint(key_offs, (devices, 2), 0, HALF)
    peer_offset = jnp.where(modality == 0, offsets[:, 0:1], offsets[:, 1:2])
    peer_index = modality * HALF + (token_rank + peer_offset) % HALF
    slot_index = jnp.where(is_real, peer_index * CAP + token_rank // HALF, SLOTS)
    return (seg_ids.reshape(TOKENS).astype(jnp.int32), slot_index.reshape(TOKENS).astype(jnp.int32))


def draw_seg_start(key, part):
    return layout(jax.random.fold_in(key, 11))[0]


def draw_dispatch_slot(key, part):
    return layout(jax.random.fold_in(key, 11))[1]


def shard_levels(own_key, extent, cuts, low, high):
    level, own = 1.0, jax.random.fold_in(own_key, 6)
    for dim, shards_of in cuts:
        steps = jnp.exp(jax.random.uniform(jax.random.fold_in(own, dim), (shards_of,), jnp.float32, low / len(cuts), high / len(cuts)))
        level = level * jnp.repeat(steps, extent[dim] // shards_of).reshape([-1 if axis == dim else 1 for axis in range(len(extent))])
    return level


def normal_values(own_key, extent, spread, most, cuts=(), kind=jnp.bfloat16):
    array = spread * jax.random.normal(own_key, extent, jnp.float32)
    if cuts:
        array = array * shard_levels(own_key, extent, cuts, -0.22, 0.18)
    return jnp.clip(array, -most, most).astype(kind)


def setup_inputs(seed: int = 0) -> dict:
    splits = jax.random.split(jax.random.key(seed), 13)
    return {
        "tokens": normal_values(splits[0], (TOKENS, D), 1.0, 6.0, ((0, 32),)),
        "cotangent": normal_values(splits[1], (TOKENS, D), 1.0, 6.0, ((0, 32),)),
        "seg_start": draw_seg_start(jax.random.fold_in(splits[12], 71), 0),
        "dispatch_slot": draw_dispatch_slot(jax.random.fold_in(splits[12], 71), 0),
        "ln1_gain": jnp.clip(1.0 + 0.15 * jax.random.normal(splits[4], (D,), jnp.float32), 0.25, 1.75),
        "ln1_shift": normal_values(splits[5], (D,), 0.5, 3.0, (), jnp.float32),
        "w_qkv": normal_values(splits[6], (D, 3 * D), D ** -0.5, 0.21875),
        "w_attn_out": normal_values(splits[7], (D, D), (D // 16) ** -0.5, 0.875),
        "ln2_gain": jnp.clip(1.0 + 0.15 * jax.random.normal(splits[8], (D,), jnp.float32), 0.25, 1.75),
        "ln2_shift": normal_values(splits[9], (D,), 0.5, 3.0, (), jnp.float32),
        "w_in": normal_values(splits[10], (EXPERTS, D, FF), D ** -0.5, 0.21875),
        "w_out": normal_values(splits[11], (EXPERTS, FF, D), FF ** -0.5, 0.109375),
    }


@jax.custom_vjp
def low(v):
    return lax.optimization_barrier(v.astype(jnp.bfloat16)).astype(jnp.float32)

@jax.custom_vjp
def low_back(v):
    return v

def low_keep(v):
    return (low(v), None)

def low_pass(kept, grad):
    return (grad,)

def back_keep(v):
    return (v, None)

def back_low(kept, grad):
    return (low(grad),)
low.defvjp(low_keep, low_pass)
low_back.defvjp(back_keep, back_low)
EPS = 1e-05
NEG = -1e+30
HIGH = lax.Precision.HIGHEST

def layer_norm(values, gain_vec, shift_vec):
    row_mean = lax.optimization_barrier(jnp.mean(values, axis=-1, keepdims=True))
    centred = values - row_mean
    variance = lax.optimization_barrier(jnp.mean(centred * centred, axis=-1, keepdims=True))
    return centred * lax.rsqrt(variance + EPS) * gain_vec + shift_vec

def reference(tokens, cotangent, seg_start, dispatch_slot, ln1_gain, ln1_shift, w_qkv, w_attn_out, ln2_gain, ln2_shift, w_in, w_out):
    source_count = TOKENS // TOK_DEV
    row_total = TOKENS // LEN
    seg_rows = seg_start.reshape(row_total, LEN)
    owner_dev = jnp.arange(TOKENS, dtype=jnp.int32) // TOK_DEV
    target = jnp.where(dispatch_slot < SLOTS, owner_dev * SLOTS + dispatch_slot, source_count * SLOTS).astype(jnp.int32)
    score_scale = 1.0 / math.sqrt(DH)
    peer_expert = (jnp.arange(N_EXPERT, dtype=jnp.int32) // HALF).astype(jnp.int32)

    def attend_row(pieces):
        qkv_row, seg_row = pieces
        split_qkv = qkv_row.reshape(LEN, 3, HEADS, DH)
        scores = jnp.einsum('qhd,khd->hqk', split_qkv[:, 0], split_qkv[:, 1], precision=HIGH) * score_scale
        scores = low_back(scores)
        allowed = seg_row[:, None] == seg_row[None, :]
        scores = jnp.where(allowed[None], scores, NEG)
        attn_probs = low(jax.nn.softmax(scores, axis=-1))
        return jnp.einsum('hqk,khd->qhd', attn_probs, split_qkv[:, 2], precision=HIGH).reshape(LEN, D)

    def expert_apply(row_block, weight_first, weight_second):
        pre_act = low_back(jnp.dot(row_block, weight_first, precision=HIGH))
        hidden = low(jax.nn.gelu(pre_act, approximate=False))
        return low(low_back(jnp.dot(hidden, weight_second, precision=HIGH)))

    def forward(inputs, gain_one, shift_one, weight_qkv, weight_attn, gain_two, shift_two, weight_in, weight_out):
        normed_one = low(layer_norm(inputs, gain_one, shift_one))
        qkv_all = low(low_back(jnp.dot(normed_one, weight_qkv, precision=HIGH)))
        mixed_out = lax.map(jax.checkpoint(attend_row), (qkv_all.reshape(row_total, LEN, 3 * D), seg_rows))
        mixed_out = low(low_back(mixed_out.reshape(TOKENS, D)))
        residual = inputs + low_back(jnp.dot(mixed_out, weight_attn, precision=HIGH))
        normed_two = low(low_back(layer_norm(residual, gain_two, shift_two)))
        buffer = jnp.zeros((source_count * SLOTS, D), jnp.float32).at[target].set(normed_two, mode='drop')
        buffer = buffer.reshape(source_count, N_EXPERT, CAP, D).transpose(1, 0, 2, 3).reshape(N_EXPERT, source_count * CAP, D)

        def peer_apply(pieces):
            row_block, which = pieces
            first = lax.dynamic_index_in_dim(weight_in, which, 0, keepdims=False)
            second = lax.dynamic_index_in_dim(weight_out, which, 0, keepdims=False)
            return expert_apply(row_block, first, second)
        expert_rows = lax.map(jax.checkpoint(peer_apply), (buffer, peer_expert))
        expert_rows = expert_rows.reshape(N_EXPERT, source_count, CAP, D).transpose(1, 0, 2, 3).reshape(source_count * SLOTS, D)
        expert_rows = jnp.concatenate([expert_rows, jnp.zeros((1, D), jnp.float32)], axis=0)
        return residual + jnp.take(expert_rows, target, axis=0)
    inputs = tokens.astype(jnp.float32)
    result, pullback = jax.vjp(forward, inputs, ln1_gain, ln1_shift, w_qkv.astype(jnp.float32), w_attn_out.astype(jnp.float32), ln2_gain, ln2_shift, w_in.astype(jnp.float32), w_out.astype(jnp.float32))
    grads = pullback(cotangent.astype(jnp.float32))
    expert_ids = jnp.arange(EXPERTS, dtype=jnp.int32)
    modality = dispatch_slot // CAP // HALF
    counts = lax.optimization_barrier(jnp.sum((modality[:, None] == expert_ids[None, :]).astype(jnp.int32), axis=0))
    count_f = counts.astype(jnp.float32)
    factor = jnp.sum(count_f) / (EXPERTS * count_f)
    return (result.astype(jnp.bfloat16), grads[0], grads[1], grads[2], grads[3], grads[4], grads[5], grads[6], grads[7] * factor[:, None, None], grads[8] * factor[:, None, None], counts)
```

```python
import functools
import math

import jax
import jax.numpy as jnp
from jax import lax
from jax.experimental import pallas as pl
from jax.experimental.pallas import tpu as pltpu
from jax.sharding import PartitionSpec as P

HEADS = 12
DH = 64
LEN = 1024
NEG = -1e30
EPS = 1e-05
PAIR = 128
LOG2E = math.log2(math.e)
bf16 = jnp.bfloat16
f32 = jnp.float32
VMEM_BYTES = 56 << 20


def dot_nn(a, b):
    return lax.dot_general(a, b, (((1,), (0,)), ((), ())), preferred_element_type=f32)


def dot_nt(a, b):
    return lax.dot_general(a, b, (((1,), (1,)), ((), ())), preferred_element_type=f32)


def dot_tn(a, b):
    return lax.dot_general(a, b, (((0,), (0,)), ((), ())), preferred_element_type=f32)


def block_meta(seg, qb, win):
    nq=LEN//qb
    rows=seg.reshape(nq,qb)
    lo_s=jnp.min(rows,axis=1)[:,None]; hi_s=jnp.max(rows,axis=1)[:,None]
    pos=jnp.arange(LEN,dtype=jnp.int32)[None]
    hit=(seg[None]>=lo_s)&(seg[None]<=hi_s)
    first=jnp.min(jnp.where(hit,pos,LEN),axis=1)
    last=jnp.max(jnp.where(hit,pos+1,0),axis=1)
    lo=jnp.minimum(first//128*128, LEN-win)
    count=(last-lo+win-1)//win
    single=jnp.broadcast_to((jnp.max(count)==1).astype(jnp.int32),count.shape)
    return jnp.stack([lo,count,single])

def window(lo_ref, i, t, win, seg_col_ref):
    base=lo_ref[0,i]+t*win
    start=pl.multiple_of(jnp.minimum(base,LEN-win),128)
    seg_k=seg_col_ref[pl.ds(start,win),:]
    pos=start+lax.broadcasted_iota(jnp.int32,(win,PAIR),0)
    return start, jnp.where(pos>=base,seg_k,-1)

def fwd_kernel(qb, win, lo_ref, q_ref, k_ref, v_ref, seg_col_ref, seg_row_ref, o_ref, lse_ref, vt_ref):
    vt_ref[...]=v_ref[...].T
    c=LOG2E/math.sqrt(DH)
    def block(i,_,fast=False):
        r0=i*qb if fast else pl.multiple_of(i*qb,qb)
        q=q_ref[pl.ds(r0,qb),:]
        low=lax.broadcasted_iota(jnp.int32,(qb,PAIR),1)<DH
        zero=jnp.zeros_like(q)
        qs=(jnp.where(low,q,zero),jnp.where(low,zero,q))
        seg_q=seg_row_ref[:,pl.ds(r0,qb)]
        def one():
            start,seg_k=window(lo_ref,i,0,win,seg_col_ref)
            ok=jnp.concatenate([seg_k]*(qb//PAIR),axis=1)==seg_q
            kw=k_ref[pl.ds(start,win),:]
            res=[]
            for h in range(2):
                s=jnp.where(ok,dot_nt(kw,qs[h])*c,NEG)
                m=jnp.max(s,axis=0,keepdims=True)
                p=jnp.exp2(s-m)
                l=jnp.sum(p,axis=0,keepdims=True)
                vtw=vt_ref[h*DH:(h+1)*DH,pl.ds(start,win)]
                res.append((m,l,dot_nn(vtw,p.astype(bf16))))
            return res
        def win_step(t,carry):
            start,seg_k=window(lo_ref,i,t,win,seg_col_ref)
            ok=jnp.concatenate([seg_k]*(qb//PAIR),axis=1)==seg_q
            kw=k_ref[pl.ds(start,win),:]
            out=[]
            for h in range(2):
                m,l,acc=carry[h]
                s=jnp.where(ok,dot_nt(kw,qs[h])*c,NEG)
                mn=jnp.maximum(m,jnp.max(s,axis=0,keepdims=True))
                al=jnp.exp2(m-mn)
                p=jnp.exp2(s-mn)
                l=l*al+jnp.sum(p,axis=0,keepdims=True)
                vtw=vt_ref[h*DH:(h+1)*DH,pl.ds(start,win)]
                acc=acc*al+dot_nn(vtw,p.astype(bf16))
                out.append((mn,l,acc))
            return tuple(out)
        init=(jnp.full((1,qb),NEG,f32),jnp.zeros((1,qb),f32),jnp.zeros((DH,qb),f32))
        res=one() if fast else lax.fori_loop(0,lo_ref[1,i],win_step,(init,init))
        ot=jnp.concatenate([a/l for m,l,a in res],axis=0)
        o_ref[pl.ds(r0,qb),:]=ot.T.astype(bf16)
        lse_ref[0,:,pl.ds(r0,qb)]=jnp.concatenate([m+jnp.log2(l) for m,l,a in res],axis=0)
        return 0
    single=lo_ref[2,0]==1
    @pl.when(single)
    def _():
        low=lax.broadcasted_iota(jnp.int32,(qb,PAIR),1)<DH
        def scores(i,h):
            q=q_ref[i*qb:(i+1)*qb,:]
            zero=jnp.zeros_like(q)
            qh=jnp.where(low,q,zero) if h==0 else jnp.where(low,zero,q)
            start=pl.multiple_of(lo_ref[0,i],128)
            ok=jnp.concatenate([seg_col_ref[pl.ds(start,win),:]]*(qb//PAIR),axis=1)==seg_row_ref[:,i*qb:(i+1)*qb]
            return jnp.where(ok,dot_nt(k_ref[pl.ds(start,win),:],qh)*c,NEG)
        units=[(i,h) for i in range(LEN//qb) for h in range(2)]
        ahead=3
        queue=[scores(*u) for u in units[:ahead]]
        done={}
        for n,(i,h) in enumerate(units):
            s=queue.pop(0)
            m=jnp.max(s,axis=0,keepdims=True)
            if n+ahead<len(units): queue.append(scores(*units[n+ahead]))
            p=jnp.exp2(s-m)
            l=jnp.sum(p,axis=0,keepdims=True)
            start=pl.multiple_of(lo_ref[0,i],128)
            acc=dot_nn(vt_ref[h*DH:(h+1)*DH,pl.ds(start,win)],p.astype(bf16))
            done[h]=(acc/l,m+jnp.log2(l))
            if h==1:
                o_ref[i*qb:(i+1)*qb,:]=jnp.concatenate([done[0][0],done[1][0]],axis=0).T.astype(bf16)
                lse_ref[0,:,i*qb:(i+1)*qb]=jnp.concatenate([done[0][1],done[1][1]],axis=0)
    @pl.when(jnp.logical_not(single))
    def _():
        lax.fori_loop(0,LEN//qb,block,0)

def attn_fwd(qkv, meta, seg_col, seg_row, qb=256, win=512):
    nh=HEADS//2
    return pl.pallas_call(
        functools.partial(fwd_kernel,qb,win),
        out_shape=(jax.ShapeDtypeStruct((LEN,HEADS*DH),bf16),jax.ShapeDtypeStruct((nh,2,LEN),f32)),
        grid_spec=pltpu.PrefetchScalarGridSpec(num_scalar_prefetch=1,grid=(nh,),
            in_specs=[pl.BlockSpec((LEN,PAIR),lambda h,*_:(0,h)),
                      pl.BlockSpec((LEN,PAIR),lambda h,*_:(0,nh+h)),
                      pl.BlockSpec((LEN,PAIR),lambda h,*_:(0,2*nh+h)),
                      pl.BlockSpec((LEN,PAIR),lambda h,*_:(0,0)),
                      pl.BlockSpec((1,LEN),lambda h,*_:(0,0))],
            out_specs=[pl.BlockSpec((LEN,PAIR),lambda h,*_:(0,h)),
                       pl.BlockSpec((1,2,LEN),lambda h,*_:(h,0,0))],
            scratch_shapes=[pltpu.VMEM((PAIR,LEN),bf16)]),
        compiler_params=pltpu.CompilerParams(vmem_limit_bytes=VMEM_BYTES),
        name="attn_fwd",
    )(meta,qkv,qkv,qkv,seg_col,seg_row)

def bwd_kernel(qb, win, lo_ref, q_ref, k_ref, v_ref, dm_ref, o_ref, lse_ref, seg_col_ref, seg_row_ref, dq_ref, dk_ref, dv_ref, kt_ref, dka, dva):
    kt_ref[...]=k_ref[...].T
    dka[...]=jnp.zeros_like(dka); dva[...]=jnp.zeros_like(dva)
    c=LOG2E/math.sqrt(DH); scale=1.0/math.sqrt(DH)
    def block(i,_,fast=False):
        r0=i*qb if fast else pl.multiple_of(i*qb,qb)
        q=q_ref[pl.ds(r0,qb),:]; dm=dm_ref[pl.ds(r0,qb),:]
        low=lax.broadcasted_iota(jnp.int32,(qb,PAIR),1)<DH
        zero=jnp.zeros_like(q)
        qs=(jnp.where(low,q,zero),jnp.where(low,zero,q))
        dms=(jnp.where(low,dm,zero),jnp.where(low,zero,dm))
        seg_q=seg_row_ref[:,pl.ds(r0,qb)]
        prod=(dm.astype(f32)*o_ref[pl.ds(r0,qb),:].astype(f32)).T
        delta=[jnp.sum(prod[h*DH:(h+1)*DH],axis=0,keepdims=True) for h in range(2)]
        lse=[lse_ref[0,h:h+1,pl.ds(r0,qb)] for h in range(2)]
        def win_step(t,carry):
            start,seg_k=window(lo_ref,i,t,win,seg_col_ref)
            ok=jnp.concatenate([seg_k]*(qb//PAIR),axis=1)==seg_q
            kw=k_ref[pl.ds(start,win),:]; vw=v_ref[pl.ds(start,win),:]
            out=[]
            dk=dka[pl.ds(start,win),:]; dv=dva[pl.ds(start,win),:]
            for h in range(2):
                s=dot_nt(kw,qs[h])
                p=jnp.where(ok,jnp.exp2(s*c-lse[h]),0.0)
                dp=dot_nt(vw,dms[h])
                ds=(p*(dp-delta[h])).astype(bf16)
                dv=dv+dot_nn(p.astype(bf16),dms[h])
                dk=dk+dot_nn(ds,qs[h])
                out.append(carry[h]+dot_nn(kt_ref[h*DH:(h+1)*DH,pl.ds(start,win)],ds))
            dka[pl.ds(start,win),:]=dk; dva[pl.ds(start,win),:]=dv
            return tuple(out)
        init=jnp.zeros((DH,qb),f32)
        res=win_step(0,(init,init)) if fast else lax.fori_loop(0,lo_ref[1,i],win_step,(init,init))
        dq_ref[pl.ds(r0,qb),:]=(jnp.concatenate(res,axis=0)*scale).T.astype(bf16)
        return 0
    single=lo_ref[2,0]==1
    @pl.when(single)
    def _():
        low=lax.broadcasted_iota(jnp.int32,(qb,PAIR),1)<DH
        def half(x,h):
            zero=jnp.zeros_like(x)
            return jnp.where(low,x,zero) if h==0 else jnp.where(low,zero,x)
        def products(i,h):
            start=pl.multiple_of(lo_ref[0,i],128)
            qh=half(q_ref[i*qb:(i+1)*qb,:],h); dmh=half(dm_ref[i*qb:(i+1)*qb,:],h)
            return dot_nt(k_ref[pl.ds(start,win),:],qh),dot_nt(v_ref[pl.ds(start,win),:],dmh),qh,dmh
        units=[(i,h) for i in range(LEN//qb) for h in range(2)]
        ahead=2
        queue=[products(*u) for u in units[:ahead]]
        dqs={}
        for n,(i,h) in enumerate(units):
            s,dp,qh,dmh=queue.pop(0)
            if n+ahead<len(units): queue.append(products(*units[n+ahead]))
            start=pl.multiple_of(lo_ref[0,i],128)
            rows=slice(i*qb,(i+1)*qb)
            if h==0:
                prod=(dm_ref[rows,:].astype(f32)*o_ref[rows,:].astype(f32)).T
                ok=jnp.concatenate([seg_col_ref[pl.ds(start,win),:]]*(qb//PAIR),axis=1)==seg_row_ref[:,rows]
            delta=jnp.sum(prod[h*DH:(h+1)*DH],axis=0,keepdims=True)
            p=jnp.where(ok,jnp.exp2(s*c-lse_ref[0,h:h+1,rows]),0.0)
            ds=(p*(dp-delta)).astype(bf16)
            dva[pl.ds(start,win),:]+=dot_nn(p.astype(bf16),dmh)
            dka[pl.ds(start,win),:]+=dot_nn(ds,qh)
            dqs[h]=dot_nn(kt_ref[h*DH:(h+1)*DH,pl.ds(start,win)],ds)
            if h==1:
                dq_ref[rows,:]=(jnp.concatenate([dqs[0],dqs[1]],axis=0)*scale).T.astype(bf16)
    @pl.when(jnp.logical_not(single))
    def _():
        lax.fori_loop(0,LEN//qb,block,0)
    dk_ref[...]=(dka[...]*scale).astype(bf16)
    dv_ref[...]=dva[...].astype(bf16)

def attn_bwd(qkv, dmixed, mixed, lse, meta, seg_col, seg_row, qb=256, win=512, h0=0, nh=6):
    np_=HEADS//2
    col=lambda off: pl.BlockSpec((LEN,PAIR),lambda h,*_:(0,off+h0+h))
    out=pl.BlockSpec((LEN,PAIR),lambda h,*_:(0,h))
    sh=jax.ShapeDtypeStruct((LEN,nh*PAIR),bf16)
    return pl.pallas_call(
        functools.partial(bwd_kernel,qb,win),
        out_shape=(sh,sh,sh),
        grid_spec=pltpu.PrefetchScalarGridSpec(num_scalar_prefetch=1,grid=(nh,),
            in_specs=[col(0),col(np_),col(2*np_),col(0),col(0),
                      pl.BlockSpec((1,2,LEN),lambda h,*_:(h0+h,0,0)),
                      pl.BlockSpec((LEN,PAIR),lambda h,*_:(0,0)),
                      pl.BlockSpec((1,LEN),lambda h,*_:(0,0))],
            out_specs=[out,out,out],
            scratch_shapes=[pltpu.VMEM((PAIR,LEN),bf16),pltpu.VMEM((LEN,PAIR),f32),pltpu.VMEM((LEN,PAIR),f32)]),
        compiler_params=pltpu.CompilerParams(vmem_limit_bytes=VMEM_BYTES),
        name="attn_bwd",
    )(meta,qkv,qkv,qkv,dmixed,mixed,lse,seg_col,seg_row)

ROWS = 256


def full(*shape):
    return pl.BlockSpec(shape, lambda *_: (0,) * len(shape))


def rows_of(width):
    return pl.BlockSpec((ROWS, width), lambda i, *_: (i, 0))


def normalise(x):
    centred = x - jnp.mean(x, axis=-1, keepdims=True)
    rstd = lax.rsqrt(jnp.mean(centred * centred, axis=-1, keepdims=True) + EPS)
    return centred * rstd, rstd


def norm_back(u, gain, n, rstd):
    ug = u * gain
    return rstd * (
        ug - jnp.mean(ug, axis=-1, keepdims=True) - n * jnp.mean(ug * n, axis=-1, keepdims=True)
    )


def params():
    return pltpu.CompilerParams(vmem_limit_bytes=VMEM_BYTES)


def qkv_kernel(x_ref, gain_ref, shift_ref, w_ref, h1_ref, qkv_ref):
    n, _ = normalise(x_ref[...].astype(f32))
    h1 = (n * gain_ref[...] + shift_ref[...]).astype(bf16)
    h1_ref[...] = h1
    qkv_ref[...] = dot_nn(h1, w_ref[...]).astype(bf16)


def ln_qkv(tokens, gain, shift, w_qkv):
    t, d = tokens.shape
    return pl.pallas_call(
        qkv_kernel,
        grid=(t // ROWS,),
        in_specs=[rows_of(d), full(1, d), full(1, d), full(d, 3 * d)],
        out_specs=[rows_of(d), rows_of(3 * d)],
        out_shape=(
            jax.ShapeDtypeStruct((t, d), bf16),
            jax.ShapeDtypeStruct((t, 3 * d), bf16),
        ),
        compiler_params=params(),
        name="ln_qkv",
    )(tokens, gain, shift, w_qkv)


def proj_kernel(n_slots, x_ref, mixed_ref, cot_ref, slot_ref, w_ref, gain_ref, shift_ref,
                resid_ref, h2_ref, cotm_ref):
    resid = x_ref[...].astype(f32) + dot_nn(mixed_ref[...], w_ref[...])
    resid_ref[...] = resid
    n, _ = normalise(resid)
    h2_ref[...] = (n * gain_ref[...] + shift_ref[...]).astype(bf16)
    routed = slot_ref[...] < n_slots
    cotm_ref[...] = jnp.where(routed, cot_ref[...].astype(f32), 0.0).astype(bf16)


def proj_ln(tokens, mixed, cotangent, slot_col, w_attn_out, gain, shift, n_slots):
    t, d = tokens.shape
    return pl.pallas_call(
        functools.partial(proj_kernel, n_slots),
        grid=(t // ROWS,),
        in_specs=[rows_of(d), rows_of(d), rows_of(d), rows_of(1), full(d, d), full(1, d), full(1, d)],
        out_specs=[rows_of(d), rows_of(d), rows_of(d)],
        out_shape=(
            jax.ShapeDtypeStruct((t, d), f32),
            jax.ShapeDtypeStruct((t, d), bf16),
            jax.ShapeDtypeStruct((t, d), bf16),
        ),
        compiler_params=params(),
        name="proj_ln",
    )(tokens, mixed, cotangent, slot_col, w_attn_out, gain, shift)


def gelu_parts(v):
    half = 0.5 * (1.0 + lax.erf(v * math.sqrt(0.5)))
    bell = jnp.exp(-0.5 * v * v) * (1.0 / math.sqrt(2.0 * math.pi))
    return v * half, half + v * bell


def ffn_kernel(which_ref, h2_ref, cot_ref, win_ref, wout_ref, ffn_ref, dh2_ref, gin_ref, gout_ref):
    h2 = h2_ref[...]
    cot = cot_ref[...]
    win = win_ref[0]
    wout = wout_ref[0]
    pre = dot_nn(h2, win)
    d_hidden = dot_nt(cot, wout)
    hidden, slope = gelu_parts(pre)
    hidden = hidden.astype(bf16)
    d_pre = (d_hidden * slope).astype(bf16)
    gout_ref[...] = dot_tn(hidden, cot).astype(gout_ref.dtype)
    gin_ref[...] = dot_tn(d_pre, h2).astype(gin_ref.dtype)
    ffn = dot_nn(hidden, wout)
    dh2 = dot_nt(d_pre, win)

    @pl.when(pl.program_id(0) == 0)
    def _():
        ffn_ref[...] = ffn
        dh2_ref[...] = dh2

    @pl.when(pl.program_id(0) > 0)
    def _():
        ffn_ref[...] += ffn
        dh2_ref[...] += dh2


def ffn_both(which, h2, cot, w_in, w_out, chunk):
    t, d = h2.shape
    ff = w_in.shape[2]
    piece = pl.BlockSpec((chunk, d), lambda i, *_: (i, 0))
    return pl.pallas_call(
        ffn_kernel,
        grid_spec=pltpu.PrefetchScalarGridSpec(
            num_scalar_prefetch=1,
            grid=(ff // chunk,),
            in_specs=[
                full(t, d),
                full(t, d),
                pl.BlockSpec((1, d, chunk), lambda i, w: (w[0], 0, i)),
                pl.BlockSpec((1, chunk, d), lambda i, w: (w[0], i, 0)),
            ],
            out_specs=[full(t, d), full(t, d), piece, piece],
        ),
        out_shape=(
            jax.ShapeDtypeStruct((t, d), f32),
            jax.ShapeDtypeStruct((t, d), f32),
            jax.ShapeDtypeStruct((ff, d), bf16),
            jax.ShapeDtypeStruct((ff, d), bf16),
        ),
        compiler_params=params(),
        name="ffn_both",
    )(which, h2, cot, w_in, w_out)


def post_kernel(n_slots, ffn_ref, dh2_ref, resid_ref, cot_ref, slot_ref, mixed_ref, w_ref, gain_ref,
                out_ref, dres_ref, dmix_ref, gw_ref, gvec_ref):
    routed = slot_ref[...] < n_slots
    resid = resid_ref[...]
    ffn = jnp.where(routed, ffn_ref[...], 0.0).astype(bf16).astype(f32)
    out_ref[...] = (resid + ffn).astype(bf16)
    u = dh2_ref[...].astype(bf16).astype(f32)
    n, rstd = normalise(resid)
    d_resid = cot_ref[...].astype(f32) + norm_back(u, gain_ref[...], n, rstd)
    dres_ref[...] = d_resid
    d_branch = d_resid.astype(bf16)
    dmix_ref[...] = dot_nt(d_branch, w_ref[...]).astype(bf16)
    gw = dot_tn(mixed_ref[...], d_branch)
    gg = jnp.sum(u * n, axis=0, keepdims=True)
    gs = jnp.sum(u, axis=0, keepdims=True)

    @pl.when(pl.program_id(0) == 0)
    def _():
        gw_ref[...] = gw
        gvec_ref[0:1, :] = gg
        gvec_ref[1:2, :] = gs

    @pl.when(pl.program_id(0) > 0)
    def _():
        gw_ref[...] += gw
        gvec_ref[0:1, :] += gg
        gvec_ref[1:2, :] += gs


def post_ffn(ffn, dh2, resid, cotangent, slot_col, mixed, w_attn_out, gain, n_slots):
    t, d = resid.shape
    return pl.pallas_call(
        functools.partial(post_kernel, n_slots),
        grid=(t // ROWS,),
        in_specs=[rows_of(d)] * 4 + [rows_of(1), rows_of(d), full(d, d), full(1, d)],
        out_specs=[rows_of(d), rows_of(d), rows_of(d), full(d, d), full(2, d)],
        out_shape=(
            jax.ShapeDtypeStruct((t, d), bf16),
            jax.ShapeDtypeStruct((t, d), f32),
            jax.ShapeDtypeStruct((t, d), bf16),
            jax.ShapeDtypeStruct((d, d), f32),
            jax.ShapeDtypeStruct((2, d), f32),
        ),
        compiler_params=params(),
        name="post_ffn",
    )(ffn, dh2, resid, cotangent, slot_col, mixed, w_attn_out, gain)


def last_kernel(dq_ref, dk_ref, dv_ref, h1_ref, x_ref, dres_ref, w_ref, gain_ref,
                gtok_ref, gw_ref, gvec_ref):
    d = x_ref.shape[1]
    parts = (dq_ref[...], dk_ref[...], dv_ref[...])
    h1 = h1_ref[...]
    u = sum(dot_nt(p, w_ref[:, j * d:(j + 1) * d]) for j, p in enumerate(parts))
    n, rstd = normalise(x_ref[...].astype(f32))
    gtok_ref[...] = dres_ref[...] + norm_back(u, gain_ref[...], n, rstd)
    gg = jnp.sum(u * n, axis=0, keepdims=True)
    gs = jnp.sum(u, axis=0, keepdims=True)
    first = pl.program_id(0) == 0

    @pl.when(first)
    def _():
        for j, p in enumerate(parts):
            gw_ref[:, j * d:(j + 1) * d] = dot_tn(h1, p)
        gvec_ref[0:1, :] = gg
        gvec_ref[1:2, :] = gs

    @pl.when(jnp.logical_not(first))
    def _():
        for j, p in enumerate(parts):
            gw_ref[:, j * d:(j + 1) * d] += dot_tn(h1, p)
        gvec_ref[0:1, :] += gg
        gvec_ref[1:2, :] += gs


def last_step(dq, dk, dv, h1, tokens, d_resid, w_qkv, gain):
    t, d = tokens.shape
    return pl.pallas_call(
        last_kernel,
        grid=(t // ROWS,),
        in_specs=[rows_of(d)] * 6 + [full(d, 3 * d), full(1, d)],
        out_specs=[rows_of(d), full(d, 3 * d), full(2, d)],
        out_shape=(
            jax.ShapeDtypeStruct((t, d), f32),
            jax.ShapeDtypeStruct((d, 3 * d), f32),
            jax.ShapeDtypeStruct((2, d), f32),
        ),
        compiler_params=params(),
        name="last_step",
    )(dq, dk, dv, h1, tokens, d_resid, w_qkv, gain)


def shards(tokens, cotangent, seg_start, dispatch_slot, ln1_gain, ln1_shift, w_qkv, w_attn_out,
           ln2_gain, ln2_shift, w_in, w_out):
    tok_count = tokens.shape[0]
    n_expert = lax.axis_size("expert")
    group_size = n_expert // 2
    capacity = 2 * tok_count // n_expert
    n_slots = n_expert * capacity
    chunk = 384
    g1, s1, g2, s2 = (v[None] for v in (ln1_gain, ln1_shift, ln2_gain, ln2_shift))
    slot_col = dispatch_slot[:, None]
    modality = dispatch_slot // (capacity * group_size)
    language = jnp.max((modality == 1).astype(jnp.int32), keepdims=True)
    meta = block_meta(seg_start, 256, 512)
    seg_col = jnp.broadcast_to(seg_start[:, None], (tok_count, PAIR))
    seg_row = seg_start[None]

    h1, qkv = ln_qkv(tokens, g1, s1, w_qkv)
    mixed, lse = attn_fwd(qkv, meta, seg_col, seg_row)
    resid, h2, cotm = proj_ln(tokens, mixed, cotangent, slot_col, w_attn_out, g2, s2, n_slots)
    ffn, dh2, g_in, g_out = ffn_both(language, h2, cotm, w_in, w_out, chunk)
    own = (jnp.arange(2, dtype=jnp.int32) == language)[:, None, None]
    zero = jnp.zeros((), bf16)
    summed = [
        lax.psum(
            lax.psum_scatter(
                jnp.where(own, g[None], zero), "expert", scatter_dimension=1, tiled=True
            ),
            "dp",
        ).astype(f32)
        for g in (g_in, g_out)
    ]
    result_out, d_resid, d_mixed, g_wo, gvec2 = post_ffn(
        ffn, dh2, resid, cotangent, slot_col, mixed, w_attn_out, g2, n_slots
    )
    dq, dk, dv = attn_bwd(qkv, d_mixed, mixed, lse, meta, seg_col, seg_row)
    grad_tokens, g_wqkv, gvec1 = last_step(dq, dk, dv, h1, tokens, d_resid, w_qkv, g1)
    counts = jnp.sum(
        (modality[:, None] == jnp.arange(2, dtype=jnp.int32)[None]).astype(f32), axis=0
    )
    g_wqkv, g_wo = (
        v.astype(f32) for v in lax.psum((g_wqkv.astype(bf16), g_wo.astype(bf16)), ("dp", "expert"))
    )
    gvec1, gvec2, counts = lax.psum((gvec1, gvec2, counts), ("dp", "expert"))
    factor = (jnp.sum(counts) / (2.0 * counts))[:, None, None]
    grad_w_in = jnp.transpose(summed[0], (0, 2, 1)) * factor
    grad_w_out = summed[1] * factor
    return (
        result_out, grad_tokens, gvec1[0], gvec1[1], g_wqkv, g_wo, gvec2[0], gvec2[1],
        grad_w_in, grad_w_out, counts.astype(jnp.int32),
    )


def solution(mesh):
    rows = P(("dp", "expert"), None)
    flat = P(("dp", "expert"))
    rep = P()
    return jax.shard_map(
        shards,
        mesh=mesh,
        in_specs=(rows, rows, flat, flat) + (rep,) * 8,
        out_specs=(rows, rows) + (rep,) * 6 + (P(None, None, "expert"), P(None, "expert", None), rep),
        check_vma=False,
    )
```

```python
import functools
import math

import jax
import jax.numpy as jnp
from jax import lax
from jax.experimental import pallas as pl
from jax.experimental.pallas import tpu as pltpu
from jax.sharding import Mesh, PartitionSpec as P

HEADS = 12
DH = 64
LEN = 1024
NEG = -1e30
EPS = 1e-05
PAIR = 128
LOG2E = math.log2(math.e)
bf16 = jnp.bfloat16
f32 = jnp.float32
VMEM_BYTES = 56 << 20


def work(us):
    return pl.CostEstimate(flops=int(us * 1e9), bytes_accessed=1 << 20, transcendentals=0)


def dot_nn(a, b):
    return lax.dot_general(a, b, (((1,), (0,)), ((), ())), preferred_element_type=f32)


def dot_nt(a, b):
    return lax.dot_general(a, b, (((1,), (1,)), ((), ())), preferred_element_type=f32)


def dot_tn(a, b):
    return lax.dot_general(a, b, (((0,), (0,)), ((), ())), preferred_element_type=f32)


def window(lo_ref, i, t, win, seg_col_ref):
    base=lo_ref[0,i]+t*win
    start=pl.multiple_of(jnp.minimum(base,LEN-win),16)
    seg_k=seg_col_ref[pl.ds(start,win),:]
    pos=start+lax.broadcasted_iota(jnp.int32,(win,PAIR),0)
    return start, jnp.where(pos>=base,seg_k,jnp.full_like(seg_k,-1))

def fwd_kernel(qb, win, lo_ref, q_ref, k_ref, v_ref, seg_col_ref, seg_row_ref, o_ref, lse_ref):
    c=LOG2E/math.sqrt(DH)
    def block(i,_):
        r0=pl.multiple_of(i*qb,qb)
        q=q_ref[pl.ds(r0,qb),:]
        low=lax.broadcasted_iota(jnp.int32,(qb,PAIR),1)<DH
        zero=jnp.zeros_like(q)
        qs=(jnp.where(low,q,zero),jnp.where(low,zero,q))
        seg_q=seg_row_ref[:,pl.ds(r0,qb)]
        def win_step(t,carry):
            start,seg_k=window(lo_ref,i,t,win,seg_col_ref)
            ok=jnp.concatenate([seg_k]*(qb//PAIR),axis=1)==seg_q
            kw=k_ref[pl.ds(start,win),:]
            out=[]
            for h in range(2):
                m,l,acc=carry[h]
                s=jnp.where(ok,dot_nt(kw,qs[h])*c,NEG)
                mn=jnp.maximum(m,jnp.max(s,axis=0,keepdims=True))
                al=jnp.exp2(m-mn)
                p=jnp.exp2(s-mn)
                l=l*al+jnp.sum(p,axis=0,keepdims=True)
                vtw=v_ref[pl.ds(start,win),:].T[h*DH:(h+1)*DH]
                acc=acc*al+dot_nn(vtw,p.astype(bf16))
                out.append((mn,l,acc))
            return tuple(out)
        init=(jnp.full((1,qb),NEG,f32),jnp.zeros((1,qb),f32),jnp.zeros((DH,qb),f32))
        res=lax.fori_loop(0,lo_ref[1,i],win_step,(init,init))
        ot=jnp.concatenate([a/l for m,l,a in res],axis=0)
        o_ref[pl.ds(r0,qb),:]=ot.T.astype(bf16)
        lse_ref[0,:,pl.ds(r0,qb)]=jnp.concatenate([m+jnp.log2(l) for m,l,a in res],axis=0)
        return 0
    single=lo_ref[2,0]==1
    @pl.when(single)
    def _():
        low=lax.broadcasted_iota(jnp.int32,(qb,PAIR),1)<DH
        def scores(i,h):
            q=q_ref[i*qb:(i+1)*qb,:]
            zero=jnp.zeros_like(q)
            qh=jnp.where(low,q,zero) if h==0 else jnp.where(low,zero,q)
            start=pl.multiple_of(lo_ref[0,i],16)
            ok=jnp.concatenate([seg_col_ref[pl.ds(start,win),:]]*(qb//PAIR),axis=1)==seg_row_ref[:,i*qb:(i+1)*qb]
            return jnp.where(ok,dot_nt(k_ref[pl.ds(start,win),:],qh)*c,NEG)
        units=[(i,h) for i in range(LEN//qb) for h in range(2)]
        ahead=3
        queue=[scores(*u) for u in units[:ahead]]
        done={}
        for n,(i,h) in enumerate(units):
            s=queue.pop(0)
            m=jnp.max(s,axis=0,keepdims=True)
            if n+ahead<len(units): queue.append(scores(*units[n+ahead]))
            p=jnp.exp2(s-m)
            l=jnp.sum(p,axis=0,keepdims=True)
            if h==0:
                vt=v_ref[pl.ds(pl.multiple_of(lo_ref[0,i],16),win),:].T
            acc=dot_nn(vt[h*DH:(h+1)*DH],p.astype(bf16))
            done[h]=(acc/l,m+jnp.log2(l))
            if h==1:
                o_ref[i*qb:(i+1)*qb,:]=jnp.concatenate([done[0][0],done[1][0]],axis=0).T.astype(bf16)
                lse_ref[0,:,i*qb:(i+1)*qb]=jnp.concatenate([done[0][1],done[1][1]],axis=0)
    @pl.when(jnp.logical_not(single))
    def _():
        lax.fori_loop(0,LEN//qb,block,0)

def attn_fwd(qkv, meta, seg_col, seg_row, qb=256, win=512):
    nh=HEADS//2
    return pl.pallas_call(
        functools.partial(fwd_kernel,qb,win),
        out_shape=(jax.ShapeDtypeStruct((LEN,HEADS*DH),bf16),jax.ShapeDtypeStruct((nh,2,LEN),f32)),
        grid_spec=pltpu.PrefetchScalarGridSpec(num_scalar_prefetch=1,grid=(nh,),
            in_specs=[pl.BlockSpec((LEN,PAIR),lambda h,*_:(0,h)),
                      pl.BlockSpec((LEN,PAIR),lambda h,*_:(0,nh+h)),
                      pl.BlockSpec((LEN,PAIR),lambda h,*_:(0,2*nh+h)),
                      pl.BlockSpec((LEN,PAIR),lambda h,*_:(0,0)),
                      pl.BlockSpec((1,LEN),lambda h,*_:(0,0))],
            out_specs=[pl.BlockSpec((LEN,PAIR),lambda h,*_:(0,h)),
                       pl.BlockSpec((1,2,LEN),lambda h,*_:(h,0,0))],
            ),
        compiler_params=pltpu.CompilerParams(vmem_limit_bytes=VMEM_BYTES),
        cost_estimate=work(14.0),
        name="attn_fwd",
    )(meta,qkv,qkv,qkv,seg_col,seg_row)

def bwd_kernel(qb, win, lo_ref, q_ref, k_ref, v_ref, dm_ref, o_ref, lse_ref, seg_col_ref, seg_row_ref, dq_ref, dk_ref, dv_ref, dka, dva):
    dka[...]=jnp.zeros_like(dka); dva[...]=jnp.zeros_like(dva)
    c=LOG2E/math.sqrt(DH); scale=1.0/math.sqrt(DH)
    def block(i,_):
        r0=pl.multiple_of(i*qb,qb)
        q=q_ref[pl.ds(r0,qb),:]; dm=dm_ref[pl.ds(r0,qb),:]
        low=lax.broadcasted_iota(jnp.int32,(qb,PAIR),1)<DH
        zero=jnp.zeros_like(q)
        qs=(jnp.where(low,q,zero),jnp.where(low,zero,q))
        dms=(jnp.where(low,dm,zero),jnp.where(low,zero,dm))
        seg_q=seg_row_ref[:,pl.ds(r0,qb)]
        prod=(dm.astype(f32)*o_ref[pl.ds(r0,qb),:].astype(f32)).T
        delta=[jnp.sum(prod[h*DH:(h+1)*DH],axis=0,keepdims=True) for h in range(2)]
        lse=[lse_ref[0,h:h+1,pl.ds(r0,qb)] for h in range(2)]
        def win_step(t,carry):
            start,seg_k=window(lo_ref,i,t,win,seg_col_ref)
            ok=jnp.concatenate([seg_k]*(qb//PAIR),axis=1)==seg_q
            kw=k_ref[pl.ds(start,win),:]; vw=v_ref[pl.ds(start,win),:]
            out=[]
            dk=dka[pl.ds(start,win),:]; dv=dva[pl.ds(start,win),:]
            for h in range(2):
                s=dot_nt(kw,qs[h])
                p=jnp.where(ok,jnp.exp2(s*c-lse[h]),0.0)
                dp=dot_nt(vw,dms[h])
                ds=(p*(dp-delta[h])).astype(bf16)
                dv=dv+dot_nn(p.astype(bf16),dms[h])
                dk=dk+dot_nn(ds,qs[h])
                out.append(carry[h]+dot_nn(kw.T[h*DH:(h+1)*DH],ds))
            dka[pl.ds(start,win),:]=dk; dva[pl.ds(start,win),:]=dv
            return tuple(out)
        init=jnp.zeros((DH,qb),f32)
        res=lax.fori_loop(0,lo_ref[1,i],win_step,(init,init))
        dq_ref[pl.ds(r0,qb),:]=(jnp.concatenate(res,axis=0)*scale).T.astype(bf16)
        return 0
    single=lo_ref[2,0]==1
    @pl.when(single)
    def _():
        low=lax.broadcasted_iota(jnp.int32,(qb,PAIR),1)<DH
        def half(x,h):
            zero=jnp.zeros_like(x)
            return jnp.where(low,x,zero) if h==0 else jnp.where(low,zero,x)
        def products(i,h):
            start=pl.multiple_of(lo_ref[0,i],16)
            qh=half(q_ref[i*qb:(i+1)*qb,:],h); dmh=half(dm_ref[i*qb:(i+1)*qb,:],h)
            return dot_nt(k_ref[pl.ds(start,win),:],qh),dot_nt(v_ref[pl.ds(start,win),:],dmh),qh,dmh
        units=[(i,h) for i in range(LEN//qb) for h in range(2)]
        ahead=2
        queue=[products(*u) for u in units[:ahead]]
        dqs={}
        for n,(i,h) in enumerate(units):
            s,dp,qh,dmh=queue.pop(0)
            if n+ahead<len(units): queue.append(products(*units[n+ahead]))
            start=pl.multiple_of(lo_ref[0,i],16)
            rows=slice(i*qb,(i+1)*qb)
            if h==0:
                kt=k_ref[pl.ds(start,win),:].T
                prod=(dm_ref[rows,:].astype(f32)*o_ref[rows,:].astype(f32)).T
                ok=jnp.concatenate([seg_col_ref[pl.ds(start,win),:]]*(qb//PAIR),axis=1)==seg_row_ref[:,rows]
            delta=jnp.sum(prod[h*DH:(h+1)*DH],axis=0,keepdims=True)
            p=jnp.where(ok,jnp.exp2(s*c-lse_ref[0,h:h+1,rows]),0.0)
            ds=(p*(dp-delta)).astype(bf16)
            dva[pl.ds(start,win),:]+=dot_nn(p.astype(bf16),dmh)
            dka[pl.ds(start,win),:]+=dot_nn(ds,qh)
            dqs[h]=dot_nn(kt[h*DH:(h+1)*DH],ds)
            if h==1:
                dq_ref[rows,:]=(jnp.concatenate([dqs[0],dqs[1]],axis=0)*scale).T.astype(bf16)
    @pl.when(jnp.logical_not(single))
    def _():
        lax.fori_loop(0,LEN//qb,block,0)
    dk_ref[...]=(dka[...]*scale).astype(bf16)
    dv_ref[...]=dva[...].astype(bf16)

def attn_bwd(qkv, dmixed, mixed, lse, meta, seg_col, seg_row, qb=256, win=512, h0=0, nh=6):
    np_=HEADS//2
    col=lambda off: pl.BlockSpec((LEN,PAIR),lambda h,*_:(0,off+h0+h))
    out=pl.BlockSpec((LEN,PAIR),lambda h,*_:(0,h))
    sh=jax.ShapeDtypeStruct((LEN,nh*PAIR),bf16)
    return pl.pallas_call(
        functools.partial(bwd_kernel,qb,win),
        out_shape=(sh,sh,sh),
        grid_spec=pltpu.PrefetchScalarGridSpec(num_scalar_prefetch=1,grid=(nh,),
            in_specs=[col(0),col(np_),col(2*np_),col(0),col(0),
                      pl.BlockSpec((1,2,LEN),lambda h,*_:(h0+h,0,0)),
                      pl.BlockSpec((LEN,PAIR),lambda h,*_:(0,0)),
                      pl.BlockSpec((1,LEN),lambda h,*_:(0,0))],
            out_specs=[out,out,out],
            scratch_shapes=[pltpu.VMEM((LEN,PAIR),f32),pltpu.VMEM((LEN,PAIR),f32)]),
        compiler_params=pltpu.CompilerParams(vmem_limit_bytes=VMEM_BYTES),
        cost_estimate=work(3.7 * nh),
        name="attn_bwd",
    )(meta,qkv,qkv,qkv,dmixed,mixed,lse,seg_col,seg_row)

ROWS = 256


def full(*shape):
    return pl.BlockSpec(shape, lambda *_: (0,) * len(shape))


def rows_of(width):
    return pl.BlockSpec((ROWS, width), lambda i, *_: (i, 0))


def normalise(x):
    centred = x - jnp.mean(x, axis=-1, keepdims=True)
    rstd = lax.rsqrt(jnp.mean(centred * centred, axis=-1, keepdims=True) + EPS)
    return centred * rstd, rstd


def norm_back(u, gain, n, rstd):
    ug = u * gain
    return rstd * (
        ug - jnp.mean(ug, axis=-1, keepdims=True) - n * jnp.mean(ug * n, axis=-1, keepdims=True)
    )


def params():
    return pltpu.CompilerParams(vmem_limit_bytes=VMEM_BYTES)


def qkv_kernel(x_ref, gain_ref, shift_ref, w_ref, h1_ref, qkv_ref):
    n, _ = normalise(x_ref[...].astype(f32))
    h1 = (n * gain_ref[...][None] + shift_ref[...][None]).astype(bf16)
    h1_ref[...] = h1
    qkv_ref[...] = dot_nn(h1, w_ref[...]).astype(bf16)


def ln_qkv(tokens, gain, shift, w_qkv):
    t, d = tokens.shape
    return pl.pallas_call(
        qkv_kernel,
        grid=(t // ROWS,),
        in_specs=[rows_of(d), full(d), full(d), full(d, 3 * d)],
        out_specs=[rows_of(d), rows_of(3 * d)],
        out_shape=(
            jax.ShapeDtypeStruct((t, d), bf16),
            jax.ShapeDtypeStruct((t, 3 * d), bf16),
        ),
        compiler_params=params(),
        cost_estimate=work(8.0),
        name="ln_qkv",
    )(tokens, gain, shift, w_qkv)


def prelude_kernel(n_slots, seg_ref, slot_ref, meta_ref, info_ref, seg_col_ref, seg_row_ref, valid_ref):
    seg = seg_ref[...]
    slot = slot_ref[...]
    per, lanes = seg.shape
    blocks = meta_ref.shape[1]
    rows = per // blocks
    pos = lax.broadcasted_iota(jnp.int32, seg.shape, 0) * lanes + lax.broadcasted_iota(
        jnp.int32, seg.shape, 1
    )
    most = 0
    for i in range(blocks):
        part = seg[i * rows:(i + 1) * rows]
        hit = jnp.logical_and(seg >= jnp.min(part), seg <= jnp.max(part))
        first = jnp.min(jnp.where(hit, pos, LEN))
        last = jnp.max(jnp.where(hit, pos + 1, 0))
        lo = jnp.minimum(first // 16 * 16, LEN - WIN)
        count = (last - lo + WIN - 1) // WIN
        meta_ref[0, i] = lo
        meta_ref[1, i] = count
        most = jnp.maximum(most, count)
    for i in range(blocks):
        meta_ref[2, i] = (most == 1).astype(jnp.int32)
    second = jnp.logical_and(slot >= n_slots // 2, slot < n_slots).astype(jnp.int32)
    first = (slot < n_slots // 2).astype(jnp.int32)
    info_ref[0] = jnp.max(second)
    info_ref[1] = jnp.sum(first)
    info_ref[2] = jnp.sum(second)
    seg = seg.astype(f32)
    valid = (slot < n_slots).astype(f32)
    for i in range(per):
        at = slice(i * lanes, (i + 1) * lanes)
        seg_row_ref[:, at] = seg[i:i + 1]
        seg_col_ref[at, :] = jnp.broadcast_to(seg[i:i + 1], (lanes, lanes)).T
        valid_ref[at, :] = jnp.broadcast_to(valid[i:i + 1], (lanes, lanes)).T


def prelude(seg_start, dispatch_slot, n_slots):
    t = seg_start.shape[0]
    smem = pl.BlockSpec(memory_space=pltpu.SMEM)
    vmem = pl.BlockSpec(memory_space=pltpu.VMEM)
    return pl.pallas_call(
        functools.partial(prelude_kernel, n_slots),
        in_specs=[vmem, vmem],
        out_specs=[smem, smem, vmem, vmem, vmem],
        out_shape=(
            jax.ShapeDtypeStruct((3, LEN // QBLOCK), jnp.int32),
            jax.ShapeDtypeStruct((3,), jnp.int32),
            jax.ShapeDtypeStruct((t, PAIR), f32),
            jax.ShapeDtypeStruct((1, t), f32),
            jax.ShapeDtypeStruct((t, PAIR), f32),
        ),
        cost_estimate=work(2.0),
        name="prelude",
    )(seg_start.reshape(t // PAIR, PAIR), dispatch_slot.reshape(t // PAIR, PAIR))


def proj_kernel(x_ref, mixed_ref, cot_ref, valid_ref, w_ref, gain_ref, shift_ref,
                resid_ref, h2_ref, cotm_ref):
    resid = x_ref[...].astype(f32) + dot_nn(mixed_ref[...], w_ref[...])
    resid_ref[...] = resid
    n, _ = normalise(resid)
    routed = jnp.concatenate([valid_ref[...]] * (resid.shape[1] // PAIR), axis=1) > 0.5
    h2 = n * gain_ref[...][None] + shift_ref[...][None]
    h2_ref[...] = jnp.where(routed, h2, 0.0).astype(bf16)
    cotm_ref[...] = jnp.where(routed, cot_ref[...].astype(f32), 0.0).astype(bf16)


def proj_ln(tokens, mixed, cotangent, valid, w_attn_out, gain, shift):
    t, d = tokens.shape
    return pl.pallas_call(
        proj_kernel,
        grid=(t // ROWS,),
        in_specs=[rows_of(d), rows_of(d), rows_of(d), rows_of(PAIR), full(d, d), full(d), full(d)],
        out_specs=[rows_of(d), rows_of(d), rows_of(d)],
        out_shape=(
            jax.ShapeDtypeStruct((t, d), f32),
            jax.ShapeDtypeStruct((t, d), bf16),
            jax.ShapeDtypeStruct((t, d), bf16),
        ),
        compiler_params=params(),
        cost_estimate=work(7.0),
        name="proj_ln",
    )(tokens, mixed, cotangent, valid, w_attn_out, gain, shift)


def gelu_parts(v):
    half = 0.5 * (1.0 + lax.erf(v * math.sqrt(0.5)))
    bell = jnp.exp(-0.5 * v * v) * (1.0 / math.sqrt(2.0 * math.pi))
    return v * half, half + v * bell


TOKENS_STEP = 256


def expert_kernel(kinds, which_ref, *refs):
    n = 2 * len(kinds)
    h2_ref, cot_ref = refs[:2]
    win_refs, wout_refs = refs[2:2 + n], refs[2 + n:2 + 2 * n]
    ffn_ref, dh2_ref = refs[2 + 2 * n:4 + 2 * n]
    out_refs = refs[4 + 2 * n:]
    win = jnp.concatenate([r[0] for r in win_refs], axis=1)
    wout = jnp.concatenate([r[0] for r in wout_refs], axis=0)
    t = h2_ref.shape[0]

    @pl.when(pl.program_id(0) == 0)
    def _():
        ffn_ref[...] = jnp.zeros_like(ffn_ref)
        dh2_ref[...] = jnp.zeros_like(dh2_ref)

    hiddens, d_pres = [], []
    for at in range(0, t, TOKENS_STEP):
        rows = slice(at, at + TOKENS_STEP)
        hidden, slope = gelu_parts(dot_nn(h2_ref[rows, :], win))
        d_hidden = dot_nt(cot_ref[rows, :], wout)
        hiddens.append(hidden.astype(bf16))
        d_pres.append((d_hidden * slope).astype(bf16))
    for i, at in enumerate(range(0, t, TOKENS_STEP)):
        rows = slice(at, at + TOKENS_STEP)
        ffn_ref[rows, :] += dot_nn(hiddens[i], wout)
        dh2_ref[rows, :] += dot_nt(d_pres[i], win)
    g_in = dot_tn(jnp.concatenate(d_pres, axis=0), h2_ref[...]).astype(bf16)
    g_out = dot_tn(jnp.concatenate(hiddens, axis=0), cot_ref[...]).astype(bf16)
    unit = win_refs[0].shape[2]
    e = which_ref[0]
    for k, kind in enumerate(kinds):
        out = out_refs[k]
        for core in range(2):
            at = (2 * k + core) * unit
            for j, g in enumerate((g_in, g_out)):
                part = g[at:at + unit]
                if kind == "z":
                    out[core, e, j] = part
                    out[core, 1 - e, j] = jnp.zeros_like(part)
                else:
                    n_dp = out.shape[0] // 2
                    step = unit // n_dp
                    for to in range(n_dp):
                        out[2 * to + core, 0, j] = part[to * step:(to + 1) * step]


def expert_part(which, h2, cot, w_in, w_out, first, kinds, unit, n_z, n_dp):
    t, d = h2.shape
    parts = w_in.shape[2] // (unit * n_z * 2)

    def column(p, core):
        return pl.BlockSpec((1, d, unit), lambda z, w: (w[0], 0, parts * (2 * z + core) + p))

    def row(p, core):
        return pl.BlockSpec((1, unit, d), lambda z, w: (w[0], parts * (2 * z + core) + p, 0))

    order = [(first + k, core) for k in range(len(kinds)) for core in range(2)]
    shapes, specs = [], []
    for kind in kinds:
        if kind == "z":
            shapes.append((2 * n_z, 2, 2, unit, d))
            specs.append(pl.BlockSpec((2, 2, 2, unit, d), lambda z, w: (z, 0, 0, 0, 0)))
        else:
            shapes.append((2 * n_dp, n_z, 2, unit // n_dp, d))
            specs.append(
                pl.BlockSpec((2 * n_dp, 1, 2, unit // n_dp, d), lambda z, w: (0, z, 0, 0, 0))
            )
    n = len(order)
    return pl.pallas_call(
        functools.partial(expert_kernel, kinds),
        grid_spec=pltpu.PrefetchScalarGridSpec(
            num_scalar_prefetch=1,
            grid=(n_z,),
            in_specs=[full(t, d), full(t, d)]
            + [column(*o) for o in order]
            + [row(*o) for o in order],
            out_specs=[full(t, d), full(t, d)] + specs,
        ),
        out_shape=[jax.ShapeDtypeStruct((t, d), f32)] * 2
        + [jax.ShapeDtypeStruct(s, bf16) for s in shapes],
        compiler_params=params(),
        cost_estimate=work(16.0 * len(kinds)),
        name="expert_part",
    )(which, h2, cot, *[w_in] * n, *[w_out] * n)


def post_kernel(n, *refs):
    sums, rest = refs[:2 * n], refs[2 * n:]
    resid_ref, cot_ref, w_ref, gain_ref, out_ref, dres_ref, dbr_ref, dmix_ref, gvec_ref = rest
    resid = resid_ref[...]
    ffn = sum(r[...] for r in sums[:n]).astype(bf16).astype(f32)
    out_ref[...] = (resid + ffn).astype(bf16)
    u = sum(r[...] for r in sums[n:]).astype(bf16).astype(f32)
    nrm, rstd = normalise(resid)
    d_resid = cot_ref[...].astype(f32) + norm_back(u, gain_ref[...][None], nrm, rstd)
    dres_ref[...] = d_resid
    d_branch = d_resid.astype(bf16)
    dbr_ref[...] = d_branch
    dmix_ref[...] = dot_nt(d_branch, w_ref[...]).astype(bf16)
    gg = jnp.sum(u * nrm, axis=0, keepdims=True)
    gs = jnp.sum(u, axis=0, keepdims=True)
    step = pl.program_id(0)

    @pl.when(step == 0)
    def _():
        gvec_ref[0:1, :] = gg
        gvec_ref[1:2, :] = gs

    @pl.when(step > 0)
    def _():
        gvec_ref[0:1, :] += gg
        gvec_ref[1:2, :] += gs


def post_ffn(ffns, dh2s, resid, cotangent, w_attn_out, gain):
    t, d = resid.shape
    n = len(ffns)
    return pl.pallas_call(
        functools.partial(post_kernel, n),
        grid=(t // ROWS,),
        in_specs=[rows_of(d)] * (2 * n + 2) + [full(d, d), full(d)],
        out_specs=[rows_of(d)] * 4 + [full(2, d)],
        out_shape=(
            jax.ShapeDtypeStruct((t, d), bf16),
            jax.ShapeDtypeStruct((t, d), f32),
            jax.ShapeDtypeStruct((t, d), bf16),
            jax.ShapeDtypeStruct((t, d), bf16),
            jax.ShapeDtypeStruct((2, d), f32),
        ),
        compiler_params=params(),
        cost_estimate=work(9.0),
        name="post_ffn",
    )(*ffns, *dh2s, resid, cotangent, w_attn_out, gain)


def weight_kernel(shape, c_ref, *refs):
    ins, (other_ref, mine_ref) = refs[:-2], refs[-2:]

    def products(out_ref):
        at, k = 0, 0
        for count in shape:
            left = ins[k][...]
            for r in ins[k + 1:k + 1 + count]:
                width = r.shape[1]
                out_ref[:, at:at + width] = dot_tn(left, r[...]).astype(bf16)
                at += width
            k += count + 1

    @pl.when(pl.program_id(0) == 0)
    def _():
        products(other_ref)

    @pl.when(pl.program_id(0) == 1)
    def _():
        products(mine_ref)


def weight_grads(core, products):
    t, d = products[0][0].shape
    half = d // 2
    args, specs, width = [], [], 0
    for left, rights in products:
        args.append(left)
        specs.append(pl.BlockSpec((t, half), lambda i, c: (0, 1 - (c[0] ^ i))))
        for r in rights:
            args.append(r)
            specs.append(full(t, r.shape[1]))
            width += r.shape[1]
    shape = jax.ShapeDtypeStruct((half, width), bf16)
    return pl.pallas_call(
        functools.partial(weight_kernel, tuple(len(rights) for _, rights in products)),
        grid_spec=pltpu.PrefetchScalarGridSpec(
            num_scalar_prefetch=1,
            grid=(2,),
            in_specs=specs,
            out_specs=[full(half, width)] * 2,
        ),
        out_shape=(shape, shape),
        compiler_params=params(),
        cost_estimate=work(4.5 * width / d),
        name="weight_grads",
    )(core, *args)


def input_kernel(groups, *refs):
    ins, (x_ref, dres_ref, w_ref, gain_ref, gtok_ref, gvec_ref) = refs[:3 * groups], refs[3 * groups:]
    d = x_ref.shape[1]
    u = None
    for j in range(3):
        side = jnp.concatenate([r[...] for r in ins[j::3]], axis=1)
        term = dot_nt(side, w_ref[:, j * d:(j + 1) * d])
        u = term if u is None else u + term
    n, rstd = normalise(x_ref[...].astype(f32))
    gtok_ref[...] = dres_ref[...] + norm_back(u, gain_ref[...][None], n, rstd)
    gg = jnp.sum(u * n, axis=0, keepdims=True)
    gs = jnp.sum(u, axis=0, keepdims=True)
    first = pl.program_id(0) == 0

    @pl.when(first)
    def _():
        gvec_ref[0:1, :] = gg
        gvec_ref[1:2, :] = gs

    @pl.when(jnp.logical_not(first))
    def _():
        gvec_ref[0:1, :] += gg
        gvec_ref[1:2, :] += gs


def input_grad(parts, tokens, d_resid, w_qkv, gain):
    t, d = tokens.shape
    groups = len(parts) // 3
    return pl.pallas_call(
        functools.partial(input_kernel, groups),
        grid=(t // ROWS,),
        in_specs=[rows_of(p.shape[1]) for p in parts]
        + [rows_of(d), rows_of(d), full(d, 3 * d), full(d)],
        out_specs=[rows_of(d), full(2, d)],
        out_shape=(
            jax.ShapeDtypeStruct((t, d), f32),
            jax.ShapeDtypeStruct((2, d), f32),
        ),
        compiler_params=params(),
        cost_estimate=work(10.0),
        name="input_grad",
    )(*parts, tokens, d_resid, w_qkv, gain)


def sum_kernel(voice_ref, got_ref, out_ref):
    for e in range(2):
        total = None
        for k in range(got_ref.shape[0]):
            share = jnp.where(voice_ref[k] == e, 1.0, 0.0)
            term = got_ref[k].astype(f32) * share
            total = term if total is None else total + term
        out_ref[:, e] = total.astype(bf16)


def sum_sides(voice, got):
    n, n_z, two, step, d = got.shape
    return pl.pallas_call(
        sum_kernel,
        grid_spec=pltpu.PrefetchScalarGridSpec(
            num_scalar_prefetch=1,
            grid=(n_z,),
            in_specs=[pl.BlockSpec((n, 1, two, step, d), lambda z, *_: (0, z, 0, 0, 0))],
            out_specs=pl.BlockSpec((1, 2, two, step, d), lambda z, *_: (z, 0, 0, 0, 0)),
        ),
        out_shape=jax.ShapeDtypeStruct((n_z, 2, two, step, d), bf16),
        compiler_params=params(),
        cost_estimate=work(3.0),
        name="sum_sides",
    )(voice, got)


def finish_kernel(factor_ref, a_ref, b_ref, c_ref, gin_ref, gout_ref):
    for e in range(2):
        factor = factor_ref[e]
        unit = a_ref.shape[2]
        for k, ref in enumerate((a_ref, b_ref, c_ref)):
            for j, out_ref in enumerate((gin_ref, gout_ref)):
                if k == 0:
                    v = ref[e, j].astype(f32)
                else:
                    v = jnp.concatenate(
                        [ref[to, e, j].astype(f32) for to in range(ref.shape[0])], axis=0
                    )
                v = v * factor
                at = slice(k * unit, (k + 1) * unit)
                if j == 0:
                    out_ref[e, :, at] = v.T
                else:
                    out_ref[e, at, :] = v


def finish_experts(factor, blocks):
    unit, d = blocks[0].shape[2:]
    vmem = pl.BlockSpec(memory_space=pltpu.VMEM)
    return pl.pallas_call(
        finish_kernel,
        in_specs=[pl.BlockSpec(memory_space=pltpu.SMEM), vmem, vmem, vmem],
        out_specs=[vmem, vmem],
        out_shape=(
            jax.ShapeDtypeStruct((2, d, 3 * unit), f32),
            jax.ShapeDtypeStruct((2, 3 * unit, d), f32),
        ),
        compiler_params=params(),
        cost_estimate=work(4.0),
        name="finish_experts",
    )(factor, *blocks)


def join_kernel(widths, core_ref, *refs):
    n = len(widths)
    gw_ref, gwo_ref = refs[2 * n:]
    d = gwo_ref.shape[1]
    pick = pl.program_id(0) == core_ref[0]
    before = 0
    for k, width in enumerate(widths):
        whole, away = refs[2 * k], refs[2 * k + 1]

        def put(out_ref, at, src, size):
            @pl.when(pick)
            def _():
                out_ref[:, at:at + size] = whole[:, src:src + size].astype(f32)

            @pl.when(jnp.logical_not(pick))
            def _():
                out_ref[:, at:at + size] = away[:, src:src + size].astype(f32)

        for third in range(3):
            put(gw_ref, third * d + before, third * width, width)
        if k == 0:
            put(gwo_ref, 0, 3 * width, d)
        before += width


def join_weights(core, sums, d):
    half = d // 2
    extra = [d] + [0] * (len(sums) - 1)
    widths = [(s[0].shape[1] - x) // 3 for s, x in zip(sums, extra)]
    flat = [v for s in sums for v in s]
    return pl.pallas_call(
        functools.partial(join_kernel, widths),
        grid_spec=pltpu.PrefetchScalarGridSpec(
            num_scalar_prefetch=1,
            grid=(2,),
            in_specs=[full(*v.shape) for v in flat],
            out_specs=[
                pl.BlockSpec((half, 3 * d), lambda i, *_: (i, 0)),
                pl.BlockSpec((half, d), lambda i, *_: (i, 0)),
            ],
        ),
        out_shape=(
            jax.ShapeDtypeStruct((d, 3 * d), f32),
            jax.ShapeDtypeStruct((d, d), f32),
        ),
        compiler_params=params(),
        cost_estimate=work(5.0),
        name="join_weights",
    )(core, *flat)


SWAP = [(0, 1), (1, 0)]
NEAR = [(0, 1), (1, 0), (2, 3), (3, 2)]
FAR = [(0, 3), (3, 0), (1, 2), (2, 1)]


def add_f32(a, b):
    return a.astype(f32) + b.astype(f32)


def sum_over_z(v):
    v = add_f32(v, lax.ppermute(v, "z", NEAR)).astype(v.dtype)
    return add_f32(v, lax.ppermute(v, "z", FAR)).astype(v.dtype)


def exchange(v, axes="dp"):
    return lax.all_to_all(v, axes, split_axis=0, concat_axis=0, tiled=True)


def spread(piece, n_dp):
    return exchange(jnp.broadcast_to(piece[None], (n_dp,) + piece.shape))


def tie(v, *after):
    return lax.optimization_barrier((v,) + after)[0] if after else v


def merge(mine, away):
    return add_f32(mine, away).astype(bf16)


def scatter(merged, n_dp):
    half, width = merged.shape
    return exchange(merged.reshape(n_dp, half // n_dp, width))


def total(pieces):
    return jnp.sum(pieces.astype(f32), axis=0).astype(bf16)


def small_sum(v, steps):
    for axis, pairs in steps:
        v = v + lax.ppermute(v, axis, pairs)
    return v


UNIT = 128
QBLOCK = 256
WIN = 512
GROUPS = (3, 3)
IN_PLANE = (("core", SWAP), ("dp", NEAR), ("dp", FAR))
ALONG_Z = (("z", NEAR), ("z", FAR))


def tuned(tokens, cotangent, seg_start, dispatch_slot, ln1_gain, ln1_shift, w_qkv, w_attn_out,
          ln2_gain, ln2_shift, w_in, w_out):
    tok_count, d = tokens.shape
    n_dp, n_z = lax.axis_size("dp"), lax.axis_size("z")
    n_slots = 2 * n_z * (2 * tok_count // (2 * n_z))
    core = lax.axis_index("core")
    core_1 = core.reshape(1).astype(jnp.int32)
    meta, info, seg_col, seg_row, valid = prelude(seg_start, dispatch_slot, n_slots)
    lane = lax.broadcasted_iota(jnp.int32, (1, d), 1)
    me = lax.axis_index("dp") * 2 + core
    voice = small_sum(jnp.where(lane == me, info[0].astype(f32), 0.0), IN_PLANE)
    voice = voice[0, : 2 * n_dp].astype(jnp.int32)

    h1, qkv = ln_qkv(tokens, ln1_gain, ln1_shift, w_qkv)
    mixed, lse = attn_fwd(qkv, meta, seg_col, seg_row, QBLOCK, WIN)
    resid, h2, cotm = proj_ln(tokens, mixed, cotangent, valid, w_attn_out, ln2_gain, ln2_shift)

    def expert(first, kinds, *after):
        return expert_part(info, tie(h2, *after), cotm, w_in, w_out, first, kinds, UNIT, n_z, n_dp)

    def bwd(at, nh, *after):
        return attn_bwd(qkv, tie(d_mixed, *after), mixed, lse, meta, seg_col, seg_row, QBLOCK, WIN, at, nh)

    plane = ("dp", "core")
    ffn_a, dh2_a, pad_a = expert(0, ("z",), voice)
    own_a = lax.psum_scatter(pad_a, ("z", "core"), scatter_dimension=0, tiled=True)
    ffn_b, dh2_b, pad_b = expert(1, ("plane",), ffn_a)
    got_b = exchange(pad_b, plane)
    ffn_c, dh2_c, pad_c = expert(2, ("plane",), ffn_b)
    got_c = exchange(pad_c, plane)
    result_out, d_resid, d_branch, d_mixed, gvec2 = post_ffn(
        (ffn_a, ffn_b, ffn_c), (dh2_a, dh2_b, dh2_c), resid, cotangent, w_attn_out, ln2_gain
    )
    one, two = GROUPS
    grads_1 = bwd(0, one)
    both_b = sum_sides(voice, tie(got_b, grads_1[0]))
    both_b = tie(both_b, own_a)
    half_b = lax.psum_scatter(both_b, "z", scatter_dimension=0, tiled=True)
    other_1, mine_1 = weight_grads(core_1, [(tie(h1, both_b), grads_1), (mixed, [d_branch])])
    away_1 = lax.ppermute(other_1, "core", SWAP)
    grads_2 = bwd(one, two, mine_1)
    merged_1 = merge(mine_1, tie(away_1, grads_2[0]))
    both_c = sum_sides(voice, tie(got_c, merged_1))
    both_c = tie(both_c, half_b)
    half_c = lax.psum_scatter(both_c, "z", scatter_dimension=0, tiled=True)
    pieces_1 = scatter(merged_1, n_dp)
    other_2, mine_2 = weight_grads(core_1, [(tie(h1, merged_1, both_c), grads_2)])
    away_2 = lax.ppermute(other_2, "core", SWAP)
    parts = grads_1 + grads_2
    grad_tokens, gvec1 = input_grad(parts, tie(tokens, mine_2), d_resid, w_qkv, ln1_gain)
    merged_2 = merge(mine_2, tie(away_2, gvec1))
    pieces_2 = scatter(merged_2, n_dp)
    near_1, near_2 = total(tie(pieces_1, merged_2)), total(pieces_2)
    sums = []
    for v in (near_1, near_2):
        whole = spread(sum_over_z(v), n_dp).reshape(d // 2, -1)
        sums.append((whole, lax.ppermute(whole, "core", SWAP)))
    block_b, block_c = spread(half_b[0], n_dp), spread(half_c[0], n_dp)
    block_a = lax.psum(tie(own_a, half_c), "dp")[0]
    own_counts = jnp.where(lane == 0, info[1], jnp.where(lane == 1, info[2], 0)).astype(f32)
    vectors = small_sum(jnp.concatenate([gvec1, gvec2, own_counts], axis=0), IN_PLANE + ALONG_Z)
    all_counts = vectors[4, :2]
    grad_wqkv, grad_wo = join_weights(core_1, sums, d)
    factor = jnp.sum(all_counts) / (2.0 * all_counts)
    grad_w_in, grad_w_out = finish_experts(factor, (block_a, block_b, block_c))
    return (
        result_out, grad_tokens, vectors[0], vectors[1], grad_wqkv, grad_wo, vectors[2], vectors[3],
        grad_w_in, grad_w_out, all_counts.astype(jnp.int32),
    )


def general(tokens, cotangent, seg_start, dispatch_slot, ln1_gain, ln1_shift, w_qkv, w_attn_out,
            ln2_gain, ln2_shift, w_in, w_out):
    tok_count, d = tokens.shape
    n_expert = lax.axis_size("expert")
    n_slots = n_expert * (2 * tok_count // n_expert)
    everywhere = ("dp", "expert")
    first_half = jnp.zeros((1,), jnp.int32)
    meta, info, seg_col, seg_row, valid = prelude(seg_start, dispatch_slot, n_slots)
    h1, qkv = ln_qkv(tokens, ln1_gain, ln1_shift, w_qkv)
    mixed, lse = attn_fwd(qkv, meta, seg_col, seg_row, QBLOCK, WIN)
    resid, h2, cotm = proj_ln(tokens, mixed, cotangent, valid, w_attn_out, ln2_gain, ln2_shift)
    blocks = w_in.shape[2] // (UNIT * 2)
    ffn, dh2, grads = expert_part(info, h2, cotm, w_in, w_out, 0, ("z",), UNIT, blocks, 1)
    grads = jnp.transpose(grads, (1, 2, 0, 3, 4)).reshape(2, 2, 2 * blocks * UNIT, d)
    grads = lax.psum_scatter(grads, "expert", scatter_dimension=2, tiled=True)
    grads = lax.psum(grads, "dp").astype(f32)
    result_out, d_resid, d_branch, d_mixed, gvec2 = post_ffn(
        (ffn,), (dh2,), resid, cotangent, w_attn_out, ln2_gain
    )
    parts = attn_bwd(qkv, d_mixed, mixed, lse, meta, seg_col, seg_row, QBLOCK, WIN)
    bottom, top = weight_grads(first_half, [(h1, parts), (mixed, [d_branch])])
    grad_tokens, gvec1 = input_grad(parts, tokens, d_resid, w_qkv, ln1_gain)
    weights = lax.psum(jnp.concatenate([top, bottom], axis=0), everywhere)
    grad_wqkv, grad_wo = weights[:, : 3 * d], weights[:, 3 * d:]
    counts, gvec1, gvec2 = lax.psum((info[1:].astype(f32), gvec1, gvec2), everywhere)
    factor = (jnp.sum(counts) / (2.0 * counts))[:, None, None]
    return (
        result_out, grad_tokens, gvec1[0], gvec1[1], grad_wqkv.astype(f32), grad_wo.astype(f32),
        gvec2[0], gvec2[1], jnp.transpose(grads[:, 0], (0, 2, 1)) * factor, grads[:, 1] * factor,
        counts.astype(jnp.int32),
    )


def solution(mesh):
    n_dp, n_expert = mesh.shape["dp"], mesh.shape["expert"]
    if (n_dp, n_expert) == (4, 8):
        mesh = Mesh(mesh.devices.reshape(n_dp, n_expert // 2, 2), ("dp", "z", "core"))
        body, expert = tuned, ("z", "core")
    else:
        body, expert = general, ("expert",)
    everywhere = ("dp",) + expert
    rows = P(everywhere, None)
    flat = P(everywhere)
    rep = P()
    return jax.shard_map(
        body,
        mesh=mesh,
        in_specs=(rows, rows, flat, flat) + (rep,) * 8,
        out_specs=(rows, rows) + (rep,) * 6 + (P(None, None, expert), P(None, expert, None), rep),
        check_vma=False,
    )
```

```python
import functools
import math

import jax
import jax.numpy as jnp
from jax import lax
from jax.experimental import pallas as pl
from jax.experimental.pallas import tpu as pltpu
from jax.sharding import Mesh, PartitionSpec as P

HEADS = 12
DH = 64
LEN = 1024
NEG = -1e30
EPS = 1e-05
PAIR = 128
LOG2E = math.log2(math.e)
bf16 = jnp.bfloat16
f32 = jnp.float32
VMEM_BYTES = 22 << 20
COST = {"early": 1e11, "late": 1.3e9, "none": 0.0, "tail": 1e11}
PHASE = ["early"]


def near(v):
    return pltpu.with_memory_space_constraint(v, pltpu.VMEM)


def far(v):
    return pltpu.with_memory_space_constraint(v, pltpu.HBM)


def work(us):
    return pl.CostEstimate(flops=int(us * COST[PHASE[0]]), bytes_accessed=1 << 20, transcendentals=0)


def dot_nn(a, b):
    return lax.dot_general(a, b, (((1,), (0,)), ((), ())), preferred_element_type=f32)


def dot_nt(a, b):
    return lax.dot_general(a, b, (((1,), (1,)), ((), ())), preferred_element_type=f32)


def dot_tn(a, b):
    return lax.dot_general(a, b, (((0,), (0,)), ((), ())), preferred_element_type=f32)


def window(lo_ref, i, t, win, seg_col_ref):
    base=lo_ref[0,i]+t*win
    start=pl.multiple_of(jnp.minimum(base,LEN-win),16)
    seg_k=seg_col_ref[pl.ds(start,win),:]
    pos=start+lax.broadcasted_iota(jnp.int32,(win,PAIR),0)
    return start, jnp.where(pos>=base,seg_k,jnp.full_like(seg_k,-1))

def fwd_kernel(qb, win, lo_ref, q_ref, k_ref, v_ref, seg_col_ref, seg_row_ref, o_ref, ot_ref, lse_ref):
    c=LOG2E/math.sqrt(DH)
    def block(i,_):
        r0=pl.multiple_of(i*qb,qb)
        q=q_ref[pl.ds(r0,qb),:]
        low=lax.broadcasted_iota(jnp.int32,(qb,PAIR),1)<DH
        zero=jnp.zeros_like(q)
        qs=(jnp.where(low,q,zero),jnp.where(low,zero,q))
        seg_q=seg_row_ref[:,pl.ds(r0,qb)]
        def win_step(t,carry):
            start,seg_k=window(lo_ref,i,t,win,seg_col_ref)
            ok=jnp.concatenate([seg_k]*(qb//PAIR),axis=1)==seg_q
            kw=k_ref[pl.ds(start,win),:]
            out=[]
            for h in range(2):
                m,l,acc=carry[h]
                s=jnp.where(ok,dot_nt(kw,qs[h])*c,NEG)
                mn=jnp.maximum(m,jnp.max(s,axis=0,keepdims=True))
                al=jnp.exp2(m-mn)
                p=jnp.exp2(s-mn)
                l=l*al+jnp.sum(p,axis=0,keepdims=True)
                vtw=v_ref[pl.ds(start,win),:].T[h*DH:(h+1)*DH]
                acc=acc*al+dot_nn(vtw,p.astype(bf16))
                out.append((mn,l,acc))
            return tuple(out)
        init=(jnp.full((1,qb),NEG,f32),jnp.zeros((1,qb),f32),jnp.zeros((DH,qb),f32))
        res=lax.fori_loop(0,lo_ref[1,i],win_step,(init,init))
        ot=jnp.concatenate([a/l for m,l,a in res],axis=0).astype(bf16)
        ot_ref[:,pl.ds(r0,qb)]=ot
        o_ref[pl.ds(r0,qb),:]=ot.T
        lse_ref[0,:,pl.ds(r0,qb)]=jnp.concatenate([m+jnp.log2(l) for m,l,a in res],axis=0)
        return 0
    single=lo_ref[2,0]==1
    @pl.when(single)
    def _():
        low=lax.broadcasted_iota(jnp.int32,(qb,PAIR),1)<DH
        def scores(i,h):
            q=q_ref[i*qb:(i+1)*qb,:]
            zero=jnp.zeros_like(q)
            qh=jnp.where(low,q,zero) if h==0 else jnp.where(low,zero,q)
            start=pl.multiple_of(lo_ref[0,i],16)
            ok=jnp.concatenate([seg_col_ref[pl.ds(start,win),:]]*(qb//PAIR),axis=1)==seg_row_ref[:,i*qb:(i+1)*qb]
            return jnp.where(ok,dot_nt(k_ref[pl.ds(start,win),:],qh)*c,NEG)
        units=[(i,h) for i in range(LEN//qb) for h in range(2)]
        ahead=3
        queue=[scores(*u) for u in units[:ahead]]
        done={}
        for n,(i,h) in enumerate(units):
            s=queue.pop(0)
            m=jnp.max(s,axis=0,keepdims=True)
            if n+ahead<len(units): queue.append(scores(*units[n+ahead]))
            p=jnp.exp2(s-m)
            l=jnp.sum(p,axis=0,keepdims=True)
            if h==0:
                vt=v_ref[pl.ds(pl.multiple_of(lo_ref[0,i],16),win),:].T
            acc=dot_nn(vt[h*DH:(h+1)*DH],p.astype(bf16))
            done[h]=(acc/l,m+jnp.log2(l))
            if h==1:
                ot=jnp.concatenate([done[0][0],done[1][0]],axis=0).astype(bf16)
                ot_ref[:,i*qb:(i+1)*qb]=ot
                o_ref[i*qb:(i+1)*qb,:]=ot.T
                lse_ref[0,:,i*qb:(i+1)*qb]=jnp.concatenate([done[0][1],done[1][1]],axis=0)
    @pl.when(jnp.logical_not(single))
    def _():
        lax.fori_loop(0,LEN//qb,block,0)

def attn_fwd(qkv, meta, seg_col, seg_row, qb=256, win=512):
    nh=HEADS//2
    return pl.pallas_call(
        functools.partial(fwd_kernel,qb,win),
        out_shape=(pltpu.VMEM((LEN,HEADS*DH),bf16),pltpu.HBM((HEADS*DH,LEN),bf16),
                   jax.ShapeDtypeStruct((nh,2,LEN),f32)),
        grid_spec=pltpu.PrefetchScalarGridSpec(num_scalar_prefetch=1,grid=(nh,),
            in_specs=[pl.BlockSpec((LEN,PAIR),lambda h,*_:(0,h)),
                      pl.BlockSpec((LEN,PAIR),lambda h,*_:(0,nh+h)),
                      pl.BlockSpec((LEN,PAIR),lambda h,*_:(0,2*nh+h)),
                      pl.BlockSpec((LEN,PAIR),lambda h,*_:(0,0)),
                      pl.BlockSpec((1,LEN),lambda h,*_:(0,0))],
            out_specs=[pl.BlockSpec((LEN,PAIR),lambda h,*_:(0,h)),
                       pl.BlockSpec((PAIR,LEN),lambda h,*_:(h,0)),
                       pl.BlockSpec((1,2,LEN),lambda h,*_:(h,0,0))],
            ),
        compiler_params=pltpu.CompilerParams(vmem_limit_bytes=VMEM_BYTES),
        cost_estimate=work(14.0),
        name="attn_fwd",
    )(meta,*[far(qkv)]*3,seg_col,seg_row)

def bwd_kernel(qb, win, lo_ref, q_ref, k_ref, v_ref, dm_ref, ot_ref, lse_ref, seg_col_ref, seg_row_ref, out_ref, dka, dva):
    dka[...]=jnp.zeros_like(dka); dva[...]=jnp.zeros_like(dva)
    c=LOG2E/math.sqrt(DH); scale=1.0/math.sqrt(DH)
    def block(i,_):
        r0=pl.multiple_of(i*qb,qb)
        q=q_ref[pl.ds(r0,qb),:]; dm=dm_ref[pl.ds(r0,qb),:]
        low=lax.broadcasted_iota(jnp.int32,(qb,PAIR),1)<DH
        zero=jnp.zeros_like(q)
        qs=(jnp.where(low,q,zero),jnp.where(low,zero,q))
        dms=(jnp.where(low,dm,zero),jnp.where(low,zero,dm))
        seg_q=seg_row_ref[:,pl.ds(r0,qb)]
        prod=dm.T.astype(f32)*ot_ref[:,pl.ds(r0,qb)].astype(f32)
        delta=[jnp.sum(prod[h*DH:(h+1)*DH],axis=0,keepdims=True) for h in range(2)]
        lse=[lse_ref[0,h:h+1,pl.ds(r0,qb)] for h in range(2)]
        def win_step(t,carry):
            start,seg_k=window(lo_ref,i,t,win,seg_col_ref)
            ok=jnp.concatenate([seg_k]*(qb//PAIR),axis=1)==seg_q
            kw=k_ref[pl.ds(start,win),:]; vw=v_ref[pl.ds(start,win),:]
            out=[]
            dk=dka[pl.ds(start,win),:]; dv=dva[pl.ds(start,win),:]
            for h in range(2):
                s=dot_nt(kw,qs[h])
                p=jnp.where(ok,jnp.exp2(s*c-lse[h]),0.0)
                dp=dot_nt(vw,dms[h])
                ds=(p*(dp-delta[h])).astype(bf16)
                dv=dv+dot_nn(p.astype(bf16),dms[h])
                dk=dk+dot_nn(ds,qs[h])
                out.append(carry[h]+dot_nn(kw.T[h*DH:(h+1)*DH],ds))
            dka[pl.ds(start,win),:]=dk; dva[pl.ds(start,win),:]=dv
            return tuple(out)
        init=jnp.zeros((DH,qb),f32)
        res=lax.fori_loop(0,lo_ref[1,i],win_step,(init,init))
        out_ref[0,pl.ds(r0,qb),:]=(jnp.concatenate(res,axis=0)*scale).T.astype(bf16)
        return 0
    single=lo_ref[2,0]==1
    @pl.when(single)
    def _():
        low=lax.broadcasted_iota(jnp.int32,(qb,PAIR),1)<DH
        def half(x,h):
            zero=jnp.zeros_like(x)
            return jnp.where(low,x,zero) if h==0 else jnp.where(low,zero,x)
        def products(i,h):
            start=pl.multiple_of(lo_ref[0,i],16)
            qh=half(q_ref[i*qb:(i+1)*qb,:],h); dmh=half(dm_ref[i*qb:(i+1)*qb,:],h)
            return dot_nt(k_ref[pl.ds(start,win),:],qh),dot_nt(v_ref[pl.ds(start,win),:],dmh),qh,dmh
        units=[(i,h) for i in range(LEN//qb) for h in range(2)]
        ahead=2
        queue=[products(*u) for u in units[:ahead]]
        dqs={}
        for n,(i,h) in enumerate(units):
            s,dp,qh,dmh=queue.pop(0)
            if n+ahead<len(units): queue.append(products(*units[n+ahead]))
            start=pl.multiple_of(lo_ref[0,i],16)
            rows=slice(i*qb,(i+1)*qb)
            if h==0:
                kt=k_ref[pl.ds(start,win),:].T
                prod=dm_ref[rows,:].T.astype(f32)*ot_ref[:,rows].astype(f32)
                ok=jnp.concatenate([seg_col_ref[pl.ds(start,win),:]]*(qb//PAIR),axis=1)==seg_row_ref[:,rows]
            delta=jnp.sum(prod[h*DH:(h+1)*DH],axis=0,keepdims=True)
            p=jnp.where(ok,jnp.exp2(s*c-lse_ref[0,h:h+1,rows]),0.0)
            ds=(p*(dp-delta)).astype(bf16)
            dva[pl.ds(start,win),:]+=dot_nn(p.astype(bf16),dmh)
            dka[pl.ds(start,win),:]+=dot_nn(ds,qh)
            dqs[h]=dot_nn(kt[h*DH:(h+1)*DH],ds)
            if h==1:
                out_ref[0,rows,:]=(jnp.concatenate([dqs[0],dqs[1]],axis=0)*scale).T.astype(bf16)
    @pl.when(jnp.logical_not(single))
    def _():
        lax.fori_loop(0,LEN//qb,block,0)
    out_ref[1]=(dka[...]*scale).astype(bf16)
    out_ref[2]=dva[...].astype(bf16)

def attn_bwd(qkv, dmixed, mixed_t, lse, meta, seg_col, seg_row, qb=256, win=512, h0=0, nh=6):
    np_=HEADS//2
    col=lambda off: pl.BlockSpec((LEN,PAIR),lambda h,*_:(0,off+h0+h))
    return pl.pallas_call(
        functools.partial(bwd_kernel,qb,win),
        out_shape=pltpu.VMEM((3,LEN,nh*PAIR),bf16),
        grid_spec=pltpu.PrefetchScalarGridSpec(num_scalar_prefetch=1,grid=(nh,),
            in_specs=[col(0),col(np_),col(2*np_),col(0),pl.BlockSpec((PAIR,LEN),lambda h,*_:(h0+h,0)),
                      pl.BlockSpec((1,2,LEN),lambda h,*_:(h0+h,0,0)),
                      pl.BlockSpec((LEN,PAIR),lambda h,*_:(0,0)),
                      pl.BlockSpec((1,LEN),lambda h,*_:(0,0))],
            out_specs=pl.BlockSpec((3,LEN,PAIR),lambda h,*_:(0,0,h)),
            scratch_shapes=[pltpu.VMEM((LEN,PAIR),f32),pltpu.VMEM((LEN,PAIR),f32)]),
        compiler_params=pltpu.CompilerParams(vmem_limit_bytes=VMEM_BYTES),
        cost_estimate=work(3.7 * nh),
        name="attn_bwd",
    )(meta,*[far(qkv)]*3,far(dmixed),far(mixed_t),lse,seg_col,seg_row)

ROWS = 256


def full(*shape):
    return pl.BlockSpec(shape, lambda *_: (0,) * len(shape))


def once(*shape):
    return pl.BlockSpec(shape, lambda *_: (0,) * len(shape), pipeline_mode=pl.Buffered(1))


def resident():
    return pl.BlockSpec(memory_space=pltpu.VMEM)


def rows_of(width):
    return pl.BlockSpec((ROWS, width), lambda i, *_: (i, 0))


def normalise(x):
    centred = x - jnp.mean(x, axis=-1, keepdims=True)
    rstd = lax.rsqrt(jnp.mean(centred * centred, axis=-1, keepdims=True) + EPS)
    return centred * rstd, rstd


def norm_back(u, gain, n, rstd):
    ug = u * gain
    return rstd * (
        ug - jnp.mean(ug, axis=-1, keepdims=True) - n * jnp.mean(ug * n, axis=-1, keepdims=True)
    )


def params():
    return pltpu.CompilerParams(vmem_limit_bytes=VMEM_BYTES)


def qkv_kernel(x_ref, gain_ref, shift_ref, w_ref, h1_ref, qkv_ref):
    n, _ = normalise(x_ref[...].astype(f32))
    h1 = (n * gain_ref[...][None] + shift_ref[...][None]).astype(bf16)
    h1_ref[...] = h1.T
    qkv_ref[...] = dot_nn(h1, w_ref[...]).astype(bf16)


def ln_qkv(tokens, gain, shift, w_qkv):
    t, d = tokens.shape
    return pl.pallas_call(
        qkv_kernel,
        grid=(t // ROWS,),
        in_specs=[rows_of(d), full(d), full(d), once(d, 3 * d)],
        out_specs=[pl.BlockSpec((d, ROWS), lambda i: (0, i)), rows_of(3 * d)],
        out_shape=(
            pltpu.HBM((d, t), bf16),
            pltpu.HBM((t, 3 * d), bf16),
        ),
        compiler_params=params(),
        cost_estimate=work(8.0),
        name="ln_qkv",
    )(far(tokens), gain, shift, far(w_qkv))


def prelude_kernel(n_slots, seg_ref, slot_ref, meta_ref, info_ref, seg_col_ref, seg_row_ref, valid_ref):
    seg = seg_ref[...]
    slot = slot_ref[...]
    per, lanes = seg.shape
    blocks = meta_ref.shape[1]
    rows = per // blocks
    pos = lax.broadcasted_iota(jnp.int32, seg.shape, 0) * lanes + lax.broadcasted_iota(
        jnp.int32, seg.shape, 1
    )
    most = 0
    for i in range(blocks):
        part = seg[i * rows:(i + 1) * rows]
        hit = jnp.logical_and(seg >= jnp.min(part), seg <= jnp.max(part))
        first = jnp.min(jnp.where(hit, pos, LEN))
        last = jnp.max(jnp.where(hit, pos + 1, 0))
        lo = jnp.minimum(first // 16 * 16, LEN - WIN)
        count = (last - lo + WIN - 1) // WIN
        meta_ref[0, i] = lo
        meta_ref[1, i] = count
        most = jnp.maximum(most, count)
    for i in range(blocks):
        meta_ref[2, i] = (most == 1).astype(jnp.int32)
    second = jnp.logical_and(slot >= n_slots // 2, slot < n_slots).astype(jnp.int32)
    first = (slot < n_slots // 2).astype(jnp.int32)
    info_ref[0] = jnp.max(second)
    info_ref[1] = jnp.sum(first)
    info_ref[2] = jnp.sum(second)
    seg = seg.astype(f32)
    valid = (slot < n_slots).astype(f32)
    for i in range(per):
        at = slice(i * lanes, (i + 1) * lanes)
        seg_row_ref[:, at] = seg[i:i + 1]
        seg_col_ref[at, :] = jnp.broadcast_to(seg[i:i + 1], (lanes, lanes)).T
        valid_ref[at, :] = jnp.broadcast_to(valid[i:i + 1], (lanes, lanes)).T


def prelude(seg_start, dispatch_slot, n_slots):
    t = seg_start.shape[0]
    smem = pl.BlockSpec(memory_space=pltpu.SMEM)
    vmem = pl.BlockSpec(memory_space=pltpu.VMEM)
    return pl.pallas_call(
        functools.partial(prelude_kernel, n_slots),
        in_specs=[vmem, vmem],
        out_specs=[smem, smem, vmem, vmem, vmem],
        out_shape=(
            jax.ShapeDtypeStruct((3, LEN // QBLOCK), jnp.int32),
            jax.ShapeDtypeStruct((3,), jnp.int32),
            jax.ShapeDtypeStruct((t, PAIR), f32),
            jax.ShapeDtypeStruct((1, t), f32),
            jax.ShapeDtypeStruct((t, PAIR), f32),
        ),
        cost_estimate=work(2.0),
        name="prelude",
    )(seg_start.reshape(t // PAIR, PAIR), dispatch_slot.reshape(t // PAIR, PAIR))


def proj_kernel(x_ref, mixed_ref, cot_ref, valid_ref, w_ref, gain_ref, shift_ref,
                resid_ref, h2_ref, cotm_ref):
    resid = x_ref[...].astype(f32) + dot_nn(mixed_ref[...], w_ref[...])
    resid_ref[...] = resid
    n, _ = normalise(resid)
    routed = jnp.concatenate([valid_ref[...]] * (resid.shape[1] // PAIR), axis=1) > 0.5
    h2 = n * gain_ref[...][None] + shift_ref[...][None]
    h2_ref[...] = jnp.where(routed, h2, 0.0).astype(bf16)
    cotm_ref[...] = jnp.where(routed, cot_ref[...].astype(f32), 0.0).astype(bf16)


def proj_ln(tokens, mixed, cotangent, valid, w_attn_out, gain, shift):
    t, d = tokens.shape
    return pl.pallas_call(
        proj_kernel,
        grid=(t // ROWS,),
        in_specs=[rows_of(d), rows_of(d), rows_of(d), rows_of(PAIR), full(d, d), full(d), full(d)],
        out_specs=[rows_of(d), rows_of(d), rows_of(d)],
        out_shape=(
            pltpu.HBM((t, d), f32),
            pltpu.VMEM((t, d), bf16),
            pltpu.VMEM((t, d), bf16),
        ),
        compiler_params=params(),
        cost_estimate=work(7.0),
        name="proj_ln",
    )(far(tokens), near(mixed), far(cotangent), valid, far(w_attn_out), gain, shift)


def gelu_parts(v):
    half = 0.5 * (1.0 + lax.erf(v * math.sqrt(0.5)))
    bell = jnp.exp(-0.5 * v * v) * (1.0 / math.sqrt(2.0 * math.pi))
    return v * half, half + v * bell


TOKENS_STEP = 256


def expert_kernel(axis, which_ref, place_ref, h2_ref, cot_ref, wina_ref, winb_ref, wouta_ref, woutb_ref,
                  hid_ref, dpre_ref, *out_refs):
    win = jnp.concatenate([wina_ref[0], winb_ref[0]], axis=1)
    wout = jnp.concatenate([wouta_ref[0], woutb_ref[0]], axis=0)
    hiddens, d_pres = [], []
    for at in range(0, h2_ref.shape[0], TOKENS_STEP):
        rows = slice(at, at + TOKENS_STEP)
        hidden, slope = gelu_parts(dot_nn(h2_ref[rows, :], win))
        hidden = hidden.astype(bf16)
        d_pre = (dot_nt(cot_ref[rows, :], wout) * slope).astype(bf16)
        hid_ref[rows, :] = hidden
        dpre_ref[rows, :] = d_pre
        hiddens.append(hidden)
        d_pres.append(d_pre)
    g_in = dot_tn(jnp.concatenate(d_pres, axis=0), h2_ref[...]).astype(bf16)
    g_out = dot_tn(jnp.concatenate(hiddens, axis=0), cot_ref[...]).astype(bf16)
    unit = wina_ref.shape[2]
    if axis is None:
        e = which_ref[0]
        for core in range(2):
            for j, g in enumerate((g_in, g_out)):
                part = g[core * unit:(core + 1) * unit]
                n_dp = out_refs[0].shape[1]
                step = unit // n_dp
                for to in range(n_dp):
                    piece = part[to * step:(to + 1) * step]
                    out_refs[0][core, to, e, j] = piece
                    out_refs[0][core, to, 1 - e, j] = jnp.zeros_like(piece)
    else:
        hold = out_refs[4]
        hold[0] = g_in
        hold[1] = g_out
        half = unit // 2
        for k in range(4):
            core, side = place_ref[0] ^ (k & 1), place_ref[axis] ^ (k >> 1)
            at = pl.multiple_of(core * unit + side * half, half)
            for j in range(2):
                out_refs[k][0, j] = hold[j, pl.ds(at, half), :]


def expert_part(which, place, h2, cot, w_in, w_out, p, axis, unit, n_z, n_dp=1):
    t, d = h2.shape
    parts = w_in.shape[2] // (unit * n_z * 2)

    def column(core):
        return pl.BlockSpec((1, d, unit), lambda z, w, _: (w[0], 0, parts * (2 * z + core) + p))

    def row(core):
        return pl.BlockSpec((1, unit, d), lambda z, w, _: (w[0], parts * (2 * z + core) + p, 0))

    if axis is None:
        step = unit // n_dp
        shapes = [pltpu.HBM((2 * n_z, n_dp, 2, 2, step, d), bf16)]
        specs = [pl.BlockSpec((2, n_dp, 2, 2, step, d), lambda z, *_: (z, 0, 0, 0, 0, 0))]
        scratch = []
    else:
        shapes = [pltpu.HBM((n_z, 2, unit // 2, d), bf16)] * 4
        specs = [pl.BlockSpec((1, 2, unit // 2, d), lambda z, *_: (z, 0, 0, 0))] * 4
        scratch = [pltpu.VMEM((2, 2 * unit, d), bf16)]
    act = (t, 2 * n_z * unit)
    act_spec = pl.BlockSpec((t, 2 * unit), lambda z, *_: (0, z))
    return pl.pallas_call(
        functools.partial(expert_kernel, axis),
        grid_spec=pltpu.PrefetchScalarGridSpec(
            num_scalar_prefetch=2,
            grid=(n_z,),
            in_specs=[resident(), resident(), column(0), column(1), row(0), row(1)],
            out_specs=[act_spec, act_spec] + specs,
            scratch_shapes=scratch,
        ),
        out_shape=[pltpu.HBM(act, bf16), pltpu.HBM(act, bf16)] + shapes,
        compiler_params=params(),
        cost_estimate=work(33.0 / parts),
        name="expert_part",
    )(which, place, near(h2), near(cot), *[far(w_in)] * 2, *[far(w_out)] * 2)


def in_order(refs, unit):
    blocks = refs[0].shape[1] // unit
    return jnp.concatenate(
        [r[:, b * unit:(b + 1) * unit] for b in range(blocks) for r in refs], axis=1
    )


def post_kernel(n, unit, which_ref, *refs):
    dpre_refs, rest = refs[:n], refs[n:]
    win_ref, resid_ref, cot_ref, w_ref, gain_ref, dres_ref, dbr_ref, dmix_ref, gvec_ref = rest
    u = dot_nt(in_order(dpre_refs, unit), win_ref[0]).astype(bf16).astype(f32)
    nrm, rstd = normalise(resid_ref[...])
    d_resid = cot_ref[...].astype(f32) + norm_back(u, gain_ref[...][None], nrm, rstd)
    dres_ref[...] = d_resid
    d_branch = d_resid.astype(bf16)
    dbr_ref[...] = d_branch
    dmix_ref[...] = dot_nt(d_branch, w_ref[...]).astype(bf16)
    gg = jnp.sum(u * nrm, axis=0, keepdims=True)
    gs = jnp.sum(u, axis=0, keepdims=True)
    step = pl.program_id(0)

    @pl.when(step == 0)
    def _():
        gvec_ref[0:1, :] = gg
        gvec_ref[1:2, :] = gs

    @pl.when(step > 0)
    def _():
        gvec_ref[0:1, :] += gg
        gvec_ref[1:2, :] += gs


def post_ffn(which, d_pres, w_in, resid, cotangent, w_attn_out, gain, unit):
    t, d = resid.shape
    n = len(d_pres)
    ff = w_in.shape[2]
    return pl.pallas_call(
        functools.partial(post_kernel, n, unit),
        grid_spec=pltpu.PrefetchScalarGridSpec(
            num_scalar_prefetch=1,
            grid=(t // ROWS,),
            in_specs=[rows_of(ff // n)] * n
            + [pl.BlockSpec((1, d, ff), lambda i, w: (w[0], 0, 0), pipeline_mode=pl.Buffered(1))]
            + [rows_of(d)] * 2
            + [full(d, d), full(d)],
            out_specs=[rows_of(d)] * 3 + [full(2, d)],
        ),
        out_shape=(
            pltpu.HBM((t, d), f32),
            pltpu.HBM((t, d), bf16),
            pltpu.HBM((t, d), bf16),
            jax.ShapeDtypeStruct((2, d), f32),
        ),
        compiler_params=params(),
        cost_estimate=work(10.0),
        name="post_ffn",
    )(which, *[far(v) for v in d_pres], far(w_in), far(resid), far(cotangent), far(w_attn_out), gain)


def result_kernel(n, unit, which_ref, *refs):
    wout_ref, resid_ref, out_ref = refs[n:]
    ffn = dot_nn(in_order(refs[:n], unit), wout_ref[0]).astype(bf16).astype(f32)
    out_ref[...] = (resid_ref[...] + ffn).astype(bf16)


def result_of(which, hiddens, w_out, resid, unit):
    t, d = resid.shape
    n = len(hiddens)
    ff = w_out.shape[1]
    return pl.pallas_call(
        functools.partial(result_kernel, n, unit),
        grid_spec=pltpu.PrefetchScalarGridSpec(
            num_scalar_prefetch=1,
            grid=(t // ROWS,),
            in_specs=[rows_of(ff // n)] * n
            + [pl.BlockSpec((1, ff, d), lambda i, w: (w[0], 0, 0), pipeline_mode=pl.Buffered(1)), rows_of(d)],
            out_specs=rows_of(d),
        ),
        out_shape=pltpu.HBM((t, d), bf16),
        compiler_params=params(),
        cost_estimate=work(8.0),
        name="result_of",
    )(which, *[far(v) for v in hiddens], far(w_out), far(resid))


def weight_kernel(c_ref, *refs):
    extra = len(refs) == 6
    h1_ref, d_ref = refs[:2]
    other_ref, mine_ref = refs[-2:]
    half = other_ref.shape[0]
    mine_at = pl.multiple_of(c_ref[0] * half, half)
    other_at = pl.multiple_of(half - c_ref[0] * half, half)

    def products(left_ref, right):
        other_ref[...] = dot_nn(left_ref[pl.ds(other_at, half), :], right).astype(bf16)
        mine_ref[...] = dot_nn(left_ref[pl.ds(mine_at, half), :], right).astype(bf16)

    if not extra:
        products(h1_ref, d_ref[0])
        return

    @pl.when(pl.program_id(0) < 3)
    def _():
        products(h1_ref, d_ref[0])

    @pl.when(pl.program_id(0) >= 3)
    def _():
        products(refs[2], refs[3][...])


def weight_grads(core, h1_t, d_qkv, more=()):
    d, t = h1_t.shape
    half, width = d // 2, d_qkv.shape[2]
    blocks = 3
    specs = [full(d, t), pl.BlockSpec((1, t, width), lambda i, c: (jnp.minimum(i, 2), 0, 0))]
    if more:
        specs += [full(d, t), pl.BlockSpec((t, width), lambda i, c: (0, jnp.maximum(i - 3, 0)))]
        blocks += more[1].shape[1] // width
    shape = pltpu.HBM((half, blocks * width), bf16)
    return pl.pallas_call(
        weight_kernel,
        grid_spec=pltpu.PrefetchScalarGridSpec(
            num_scalar_prefetch=1,
            grid=(blocks,),
            in_specs=specs,
            out_specs=[pl.BlockSpec((half, width), lambda i, c: (0, i))] * 2,
        ),
        out_shape=(shape, shape),
        compiler_params=params(),
        cost_estimate=work(1.2 * blocks * width / half),
        name="weight_grads",
    )(core, far(h1_t), near(d_qkv), *[far(v) for v in more])


def input_kernel(groups, *refs):
    ins, (x_ref, dres_ref, w_ref, gain_ref, gtok_ref, gvec_ref) = refs[:groups], refs[groups:]
    side = jnp.concatenate([r[j] for j in range(3) for r in ins], axis=1)
    u = dot_nt(side, w_ref[...])
    n, rstd = normalise(x_ref[...].astype(f32))
    gtok_ref[...] = dres_ref[...] + norm_back(u, gain_ref[...][None], n, rstd)
    gg = jnp.sum(u * n, axis=0, keepdims=True)
    gs = jnp.sum(u, axis=0, keepdims=True)
    first = pl.program_id(0) == 0

    @pl.when(first)
    def _():
        gvec_ref[0:1, :] = gg
        gvec_ref[1:2, :] = gs

    @pl.when(jnp.logical_not(first))
    def _():
        gvec_ref[0:1, :] += gg
        gvec_ref[1:2, :] += gs


def input_grad(parts, tokens, d_resid, w_qkv, gain):
    t, d = tokens.shape
    return pl.pallas_call(
        functools.partial(input_kernel, len(parts)),
        grid=(t // ROWS,),
        in_specs=[pl.BlockSpec((3, ROWS, p.shape[2]), lambda i: (0, i, 0)) for p in parts]
        + [rows_of(d), rows_of(d), once(d, 3 * d), full(d)],
        out_specs=[rows_of(d), full(2, d)],
        out_shape=(
            pltpu.HBM((t, d), f32),
            jax.ShapeDtypeStruct((2, d), f32),
        ),
        compiler_params=params(),
        cost_estimate=work(10.0),
        name="input_grad",
    )(*[far(p) for p in parts], far(tokens), far(d_resid), far(w_qkv), gain)


def sum_kernel(axis, place_ref, voice_ref, a_ref, b_ref, c_ref, d_ref, keep_ref, send_ref):
    me = place_ref[3]
    bit = place_ref[3 - axis]
    step = keep_ref.shape[3]
    for j in range(2):
        for out_ref, mine in ((keep_ref, bit), (send_ref, 1 - bit)):
            at = pl.multiple_of(mine * step, step)
            sides = [None, None]
            for k, ref in enumerate((a_ref, b_ref, c_ref, d_ref)):
                term = ref[0, j, pl.ds(at, step), :].astype(f32)
                second = voice_ref[me ^ ((k & 1) | ((k >> 1) << axis))] == 1
                for e in range(2):
                    part = jnp.where(second, term if e else 0.0, 0.0 if e else term)
                    sides[e] = part if sides[e] is None else sides[e] + part
            for e in range(2):
                out_ref[0, e, j] = sides[e].astype(bf16)


def sum_sides(axis, place, voice, got):
    n_z, two, rows, d = got[0].shape
    spec = pl.BlockSpec((1, two, rows, d), lambda z, *_: (z, 0, 0, 0))
    out = pl.BlockSpec((1, 2, two, rows // 2, d), lambda z, *_: (z, 0, 0, 0, 0))
    shape = jax.ShapeDtypeStruct((n_z, 2, two, rows // 2, d), bf16)
    return pl.pallas_call(
        functools.partial(sum_kernel, axis),
        grid_spec=pltpu.PrefetchScalarGridSpec(
            num_scalar_prefetch=2,
            grid=(n_z,),
            in_specs=[spec] * 4,
            out_specs=[out, out],
        ),
        out_shape=(shape, shape),
        compiler_params=params(),
        cost_estimate=work(3.0),
        name="sum_sides",
    )(place, voice, *[near(v) for v in got])


def finish_kernel(axes, place_ref, tally_ref, *refs):
    blocks, (gin_ref, gout_ref, counts_ref, hold_ref) = refs[:-4], refs[-4:]
    spots = [(ref, k) for ref in blocks for k in range(ref.shape[1])]
    d = gin_ref.shape[1]
    lane = lax.broadcasted_iota(jnp.int32, (1, d), 1)
    counts = [jnp.sum(jnp.where(lane == 128 + e, tally_ref[...], 0.0)) for e in range(2)]
    for e in range(2):
        counts_ref[e] = counts[e].astype(jnp.int32)
    unit = hold_ref.shape[0]
    step = unit // 4
    for p, ((ref, part), axis) in enumerate(zip(spots, axes)):
        for e in range(2):
            factor = jnp.full((1, d), counts[0] + counts[1], f32) / (2.0 * counts[e])
            for j in range(2):
                for k in range(4):
                    to = 2 * (k & 1) + (k >> 1) if axis == X else k
                    rows = slice(to * step, (to + 1) * step)
                    hold_ref[rows, :] = ref[k, part, e, j].astype(f32) * factor
                where = slice(p * unit, (p + 1) * unit)
                if j == 0:
                    gin_ref[e, :, where] = hold_ref[...].T
                else:
                    gout_ref[e, where, :] = hold_ref[...]


def finish_experts(axes, place, tally, blocks):
    step, d = blocks[0].shape[-2:]
    n = len(axes)
    smem = pl.BlockSpec(memory_space=pltpu.SMEM)
    return pl.pallas_call(
        functools.partial(finish_kernel, axes),
        in_specs=[smem] + [resident()] * (1 + len(blocks)),
        out_specs=[resident(), resident(), smem],
        out_shape=(
            jax.ShapeDtypeStruct((2, d, n * 4 * step), f32),
            jax.ShapeDtypeStruct((2, n * 4 * step, d), f32),
            jax.ShapeDtypeStruct((2,), jnp.int32),
        ),
        scratch_shapes=[pltpu.VMEM((4 * step, d), f32)],
        compiler_params=params(),
        cost_estimate=work(4.0),
        name="finish_experts",
    )(place, tally, *[near(v) for v in blocks])


def join_kernel(widths, place_ref, *refs):
    n = len(widths)
    gw_ref, gwo_ref, vec_ref = refs[2 * n:]
    d = gwo_ref.shape[2]
    rows = gwo_ref.shape[1]
    rel = pl.program_id(0) ^ (place_ref[3] >> 1)
    at = place_ref[3] >> 1
    vec = refs[2 * n - 2][at, rows:, :d].astype(f32) + refs[2 * n - 1][at, rows:, :d].astype(f32)
    vec_ref[...] = vec[:8]
    before = 0
    for k, width in enumerate(widths):
        for half, ref in ((place_ref[0], refs[2 * k]), (1 - place_ref[0], refs[2 * k + 1])):
            for third in range(3):
                at, src = third * d + before, third * width
                gw_ref[half, :, at:at + width] = ref[rel, :rows, src:src + width].astype(f32)
            if k == 0:
                gwo_ref[half] = ref[rel, :rows, 3 * width:].astype(f32)
        before += width


def join_weights(place, sums, d):
    step = d // 8
    extra = [d] + [0] * (len(sums) - 1)
    widths = [(s[0].shape[2] - x) // 3 for s, x in zip(sums, extra)]
    flat = [v for pair in sums for v in pair]
    gw, gwo, vec = pl.pallas_call(
        functools.partial(join_kernel, widths),
        grid_spec=pltpu.PrefetchScalarGridSpec(
            num_scalar_prefetch=1,
            grid=(4,),
            in_specs=[resident()] * len(flat),
            out_specs=[
                pl.BlockSpec((2, step, 3 * d), lambda i, *_: (0, i, 0)),
                pl.BlockSpec((2, step, d), lambda i, *_: (0, i, 0)),
                full(8, d),
            ],
        ),
        out_shape=(
            jax.ShapeDtypeStruct((2, d // 2, 3 * d), f32),
            jax.ShapeDtypeStruct((2, d // 2, d), f32),
            jax.ShapeDtypeStruct((8, d), f32),
        ),
        compiler_params=params(),
        cost_estimate=work(5.0),
        name="join_weights",
    )(place, *[near(v) for v in flat])
    return gw.reshape(d, 3 * d), gwo.reshape(d, d), vec


X, Y = 1, 2
NEAR = [(0, 1), (1, 0), (2, 3), (3, 2)]
FAR = [(0, 3), (3, 0), (1, 2), (2, 1)]


def swap_core(v):
    return lax.ppermute(v, "core", [(0, 1), (1, 0)])


def swap(v, axis):
    return lax.ppermute(v, "dp", [(i, i ^ axis) for i in range(4)])


def swap_both(v, axis):
    return lax.ppermute(v, ("dp", "core"), [(i, i ^ (1 | (axis << 1))) for i in range(8)])


def along_z(v, pairs):
    return lax.ppermute(v, "z", pairs)


def tie(v, *after):
    return lax.optimization_barrier((v,) + after)[0] if after else v


def small_kernel(fn, *refs):
    out_ref = refs[-1]
    out_ref[...] = fn(*[r[...] for r in refs[:-1]]).astype(out_ref.dtype)


def small(fn, *args, space=pltpu.VMEM, name="small"):
    shape = jax.eval_shape(fn, *args)
    return pl.pallas_call(
        functools.partial(small_kernel, fn),
        in_specs=[resident()] * len(args),
        out_specs=resident(),
        out_shape=pltpu.VMEM(shape.shape, args[0].dtype),
        compiler_params=params(),
        cost_estimate=work(1.0),
        name=name,
    )(*[near(v) for v in args])


def add_f32(a, b):
    return a.astype(f32) + b.astype(f32)


def add(a, b):
    return small(add_f32, a, b, name="add")


def merge_kernel(mine_ref, away_ref, first_ref, second_ref, out_ref):
    n, rows, width = out_ref.shape
    rows -= 16
    d = first_ref.shape[1]
    for k in range(n):
        at = slice(k * rows, (k + 1) * rows)
        out_ref[k, :rows] = (mine_ref[at, :].astype(f32) + away_ref[at, :].astype(f32)).astype(bf16)
        out_ref[k, rows:] = jnp.zeros((16, width), bf16)
    small = jnp.concatenate([first_ref[...], second_ref[...], jnp.zeros((12, d), f32)], axis=0)
    out_ref[0, rows:, :d] = small.astype(bf16)


def merge_small(mine, away, first, second):
    half, width = mine.shape
    return pl.pallas_call(
        merge_kernel,
        in_specs=[resident()] * 4,
        out_specs=resident(),
        out_shape=pltpu.VMEM((4, half // 4 + 16, width), bf16),
        compiler_params=params(),
        cost_estimate=work(1.0),
        name="merge_small",
    )(near(mine), near(away), first, second)


def split_kernel(axis, place_ref, *refs):
    keep_ref, send_ref = refs[-2:]
    bit = place_ref[axis]
    for out_ref, at in ((keep_ref, bit), (send_ref, 1 - bit)):
        v = refs[0][at]
        for r in refs[1:-2]:
            v = v.astype(f32) + r[at].astype(f32)
        out_ref[...] = v.astype(bf16)


def split(place, axis, *v):
    shape = pltpu.VMEM(v[0].shape[1:], bf16)
    return pl.pallas_call(
        functools.partial(split_kernel, axis),
        in_specs=[pl.BlockSpec(memory_space=pltpu.SMEM)] + [resident()] * len(v),
        out_specs=[resident()] * 2,
        out_shape=(shape, shape),
        compiler_params=params(),
        cost_estimate=work(1.0),
        name="split",
    )(place, *[near(x) for x in v])


def total(v):
    return small(lambda x: sum(x[k].astype(f32) for k in range(x.shape[0])), v, name="total")


def stack(*v):
    return small(lambda *x: jnp.stack(x), *v, name="stack")


class Line:
    def __init__(self):
        self.last = ()

    def __call__(self, step, first, *rest):
        out = step(tie(first, *self.last), *rest)
        self.last = (jax.tree.leaves(out)[0],)
        return out


UNIT = 128
QBLOCK = 256
WIN = 512
GROUPS = (3, 3)


def tuned(tokens, cotangent, seg_start, dispatch_slot, ln1_gain, ln1_shift, w_qkv, w_attn_out,
          ln2_gain, ln2_shift, w_in, w_out):
    tok_count, d = tokens.shape
    n_z = lax.axis_size("z")
    n_slots = 2 * n_z * (2 * tok_count // (2 * n_z))
    core, dp = lax.axis_index("core"), lax.axis_index("dp")
    bits = {X: dp & 1, Y: dp >> 1}
    place = jnp.stack([core, bits[X], bits[Y], dp * 2 + core]).astype(jnp.int32)
    line = Line()
    PHASE[0] = "early"

    def around(v):
        return [v, swap(v, X), swap(v, Y), swap(v, X | Y)]

    def exchange(v):
        return lax.all_to_all(v, "dp", split_axis=0, concat_axis=0, tiled=True)

    def merge(a, b):
        return small(add_f32, a, b, name="merge").reshape(4, -1, a.shape[1])

    meta, info, seg_col, seg_row, valid = prelude(seg_start, dispatch_slot, n_slots)
    lane = lax.broadcasted_iota(jnp.int32, (1, d), 1)
    voice = jnp.where(lane == place[3], info[0], 0)
    voice = jnp.where(lane == 128, info[1], jnp.where(lane == 129, info[2], voice)).astype(f32)
    away = swap_core(voice)
    h1_t, qkv = line(ln_qkv, tokens, ln1_gain, ln1_shift, w_qkv)
    voice = line(add, voice, away)
    away = swap(voice, X)
    mixed, mixed_t, lse = line(
        lambda v: attn_fwd(v, meta, seg_col, seg_row, QBLOCK, WIN), qkv
    )
    voice = line(add, voice, away)
    away = swap(voice, Y)
    resid, h2, cotm = line(
        lambda v: proj_ln(tokens, v, cotangent, valid, w_attn_out, ln2_gain, ln2_shift), mixed
    )
    tally = line(add, voice, away)
    voice = tally[0, :8].astype(jnp.int32)
    away_t = along_z(tally, NEAR)

    def expert(p, axis):
        return line(
            lambda v: expert_part(info, place, v, cotm, w_in, w_out, p, axis, UNIT, n_z, 4), h2
        )

    def plane(pieces, axis):
        return [pieces[0], swap_core(pieces[1]), swap(pieces[2], axis), swap_both(pieces[3], axis)]

    hid_b, dpre_b, *out_b = expert(1, X)
    got_b = plane(out_b, X)
    tally = line(add, tally, away_t)
    away_t = along_z(tally, FAR)
    hid_a, dpre_a, out_a = expert(0, None)
    tally = line(add, tally, away_t)
    own_a = lax.psum_scatter(out_a, ("z", "core"), scatter_dimension=0, tiled=True)
    hid_c, dpre_c, *out_c = expert(2, Y)
    got_c = plane(out_c, Y)
    d_resid, d_branch, d_mixed, gvec2 = line(
        lambda v: post_ffn(
            info, (dpre_a, v, dpre_c), w_in, resid, cotangent, w_attn_out, ln2_gain, UNIT
        ),
        dpre_b,
    )

    def sides(got, axis):
        return line(lambda v: sum_sides(axis, place, voice, (got[0], got[1], got[2], v)), got[3])

    def bwd(at, nh):
        return line(
            lambda v: attn_bwd(qkv, v, mixed_t, lse, meta, seg_col, seg_row, QBLOCK, WIN, at, nh),
            d_mixed,
        )

    def scatter_z(v):
        return lax.psum_scatter(v, "z", scatter_dimension=0, tiled=True)[0]

    one, two = GROUPS
    keep_b, send_b = sides(got_b, X)
    away_b = swap(send_b, Y)
    d_qkv_1 = bwd(0, one)
    other_1, mine_1 = line(lambda v: weight_grads(place, v, d_qkv_1, (mixed_t, d_branch)), h1_t)
    away_1 = swap_core(other_1)
    keep_c, send_c = sides(got_c, Y)
    away_c = swap(send_c, X)
    both_b = line(add, keep_b, away_b)
    half_b = scatter_z(both_b)
    keep_a, send_a = line(lambda v: split(place, Y, v.reshape((2, 2) + v.shape[1:])), own_a[0])
    away_a = swap(send_a, Y)
    all_1 = exchange(line(merge, mine_1, away_1))
    d_qkv_2 = bwd(one, two)
    PHASE[0] = "late"
    PHASE[0] = "early"
    other_2, mine_2 = line(lambda v: weight_grads(place, v, d_qkv_2), h1_t)
    away_2 = swap_core(other_2)
    PHASE[0] = "late"
    both_c = line(add, keep_c, away_c)
    half_c = scatter_z(both_c)
    keep_a, send_a = line(lambda a, b: split(place, X, a, b), keep_a, away_a)
    away_a = swap(send_a, X)
    piece_1 = line(total, all_1)
    away_1 = along_z(piece_1, NEAR)

    def copies(*v):
        return small(lambda *x: jnp.stack([jnp.stack(x)] * 4), *v, name="copies")

    half_a = line(add, keep_a, away_a)
    all_ab = exchange(line(copies, half_a, half_b))
    grad_tokens, gvec1 = line(
        lambda v: input_grad((d_qkv_1, d_qkv_2), v, d_resid, w_qkv, ln1_gain), tokens
    )
    all_2 = exchange(line(lambda a, b: merge_small(a, b, gvec1, gvec2), tie(mine_2, all_ab), away_2))
    piece_1 = line(add, piece_1, away_1)
    away_1 = along_z(piece_1, FAR)
    result_out = line(lambda v: result_of(info, (hid_a, hid_b, hid_c), w_out, v, UNIT), resid)
    piece_2 = line(total, all_2)
    away_2 = along_z(piece_2, NEAR)
    all_c = exchange(line(copies, half_c))
    PHASE[0] = "tail"
    piece_2 = line(add, piece_2, away_2)
    away_2 = along_z(piece_2, FAR)
    piece_1 = line(add, piece_1, away_1)
    around_1 = around(piece_1)
    piece_2 = line(add, piece_2, away_2)
    around_2 = around(piece_2)
    grad_w_in, grad_w_out, all_counts = line(
        lambda v: finish_experts((Y, X, Y), place, tie(tally, piece_2), (all_ab, v)), all_c
    )
    whole_1 = line(stack, *around_1)
    other_1 = swap_core(whole_1)
    whole_2 = line(stack, *around_2)
    other_2 = swap_core(whole_2)
    grad_wqkv, grad_wo, vectors = join_weights(
        place, ((tie(whole_1, *line.last), other_1), (whole_2, other_2)), d
    )
    PHASE[0] = "early"
    return (
        result_out, grad_tokens, vectors[0], vectors[1], grad_wqkv, grad_wo, vectors[2], vectors[3],
        grad_w_in, grad_w_out, all_counts,
    )


def general(tokens, cotangent, seg_start, dispatch_slot, ln1_gain, ln1_shift, w_qkv, w_attn_out,
            ln2_gain, ln2_shift, w_in, w_out):
    tok_count, d = tokens.shape
    n_expert = lax.axis_size("expert")
    n_slots = n_expert * (2 * tok_count // n_expert)
    everywhere = ("dp", "expert")
    first_half = jnp.zeros((1,), jnp.int32)
    meta, info, seg_col, seg_row, valid = prelude(seg_start, dispatch_slot, n_slots)
    h1_t, qkv = ln_qkv(tokens, ln1_gain, ln1_shift, w_qkv)
    mixed, mixed_t, lse = attn_fwd(qkv, meta, seg_col, seg_row, QBLOCK, WIN)
    resid, h2, cotm = proj_ln(tokens, mixed, cotangent, valid, w_attn_out, ln2_gain, ln2_shift)
    blocks = w_in.shape[2] // (UNIT * 2)
    hidden, d_pre, grads = expert_part(
        info, first_half, h2, cotm, w_in, w_out, 0, None, UNIT, blocks
    )
    grads = jnp.transpose(grads[:, 0], (1, 2, 0, 3, 4)).reshape(2, 2, 2 * blocks * UNIT, d)
    grads = lax.psum_scatter(grads, "expert", scatter_dimension=2, tiled=True)
    grads = lax.psum(grads, "dp").astype(f32)
    d_resid, d_branch, d_mixed, gvec2 = post_ffn(
        info, (d_pre,), w_in, resid, cotangent, w_attn_out, ln2_gain, UNIT
    )
    result_out = result_of(info, (hidden,), w_out, resid, UNIT)
    d_qkv = attn_bwd(qkv, d_mixed, mixed_t, lse, meta, seg_col, seg_row, QBLOCK, WIN)
    bottom, top = weight_grads(first_half, h1_t, d_qkv, (mixed_t, d_branch))
    grad_tokens, gvec1 = input_grad((d_qkv,), tokens, d_resid, w_qkv, ln1_gain)
    weights = lax.psum(jnp.concatenate([top, bottom], axis=0), everywhere).astype(f32)
    grad_wqkv, grad_wo = weights[:, : 3 * d], weights[:, 3 * d:]
    counts, gvec1, gvec2 = lax.psum((info[1:].astype(f32), gvec1, gvec2), everywhere)
    factor = (jnp.sum(counts) / (2.0 * counts))[:, None, None]
    return (
        result_out, grad_tokens, gvec1[0], gvec1[1], grad_wqkv, grad_wo,
        gvec2[0], gvec2[1], jnp.transpose(grads[:, 0], (0, 2, 1)) * factor, grads[:, 1] * factor,
        counts.astype(jnp.int32),
    )


def solution(mesh):
    n_dp, n_expert = mesh.shape["dp"], mesh.shape["expert"]
    if (n_dp, n_expert) == (4, 8):
        mesh = Mesh(mesh.devices.reshape(n_dp, n_expert // 2, 2), ("dp", "z", "core"))
        body, expert = tuned, ("z", "core")
    else:
        body, expert = general, ("expert",)
    everywhere = ("dp",) + expert
    rows = P(everywhere, None)
    flat = P(everywhere)
    rep = P()
    return jax.shard_map(
        body,
        mesh=mesh,
        in_specs=(rows, rows, flat, flat) + (rep,) * 8,
        out_specs=(rows, rows) + (rep,) * 6 + (P(None, None, expert), P(None, expert, None), rep),
        check_vma=False,
    )
```

```python
import functools
import math

import jax
import jax.numpy as jnp
from jax import lax
from jax.experimental import pallas as pl
from jax.experimental.pallas import tpu as pltpu
from jax.sharding import Mesh, PartitionSpec as P

HEADS = 12
DH = 64
LEN = 1024
NEG = -1e30
EPS = 1e-05
PAIR = 128
LOG2E = math.log2(math.e)
bf16 = jnp.bfloat16
f32 = jnp.float32
VMEM_BYTES = 22 << 20
COST = {"early": 1e11, "late": 1.2e9, "none": 0.0, "tail": 1e11}
PHASE = ["early"]


def near(v):
    return pltpu.with_memory_space_constraint(v, pltpu.VMEM)


def far(v):
    return pltpu.with_memory_space_constraint(v, pltpu.HBM)


def work(us):
    return pl.CostEstimate(flops=int(us * COST[PHASE[0]]), bytes_accessed=1 << 20, transcendentals=0)


def dot_nn(a, b):
    return lax.dot_general(a, b, (((1,), (0,)), ((), ())), preferred_element_type=f32)


def dot_nt(a, b):
    return lax.dot_general(a, b, (((1,), (1,)), ((), ())), preferred_element_type=f32)


def dot_tn(a, b):
    return lax.dot_general(a, b, (((0,), (0,)), ((), ())), preferred_element_type=f32)


def window(lo_ref, i, t, win, seg_col_ref):
    base=lo_ref[0,i]+t*win
    start=pl.multiple_of(jnp.minimum(base,LEN-win),16)
    seg_k=seg_col_ref[pl.ds(start,win),:]
    pos=start+lax.broadcasted_iota(jnp.int32,(win,PAIR),0)
    return start, jnp.where(pos>=base,seg_k,jnp.full_like(seg_k,-1))

def fwd_kernel(qb, win, lo_ref, q_ref, k_ref, v_ref, seg_col_ref, seg_row_ref, o_ref, ot_ref, lse_ref):
    c=LOG2E/math.sqrt(DH)
    def block(i,_):
        r0=pl.multiple_of(i*qb,qb)
        q=q_ref[pl.ds(r0,qb),:]
        low=lax.broadcasted_iota(jnp.int32,(qb,PAIR),1)<DH
        zero=jnp.zeros_like(q)
        qs=(jnp.where(low,q,zero),jnp.where(low,zero,q))
        seg_q=seg_row_ref[:,pl.ds(r0,qb)]
        def win_step(t,carry):
            start,seg_k=window(lo_ref,i,t,win,seg_col_ref)
            ok=jnp.concatenate([seg_k]*(qb//PAIR),axis=1)==seg_q
            kw=k_ref[pl.ds(start,win),:]
            out=[]
            for h in range(2):
                m,l,acc=carry[h]
                s=jnp.where(ok,dot_nt(kw,qs[h])*c,NEG)
                mn=jnp.maximum(m,jnp.max(s,axis=0,keepdims=True))
                al=jnp.exp2(m-mn)
                p=jnp.exp2(s-mn)
                l=l*al+jnp.sum(p,axis=0,keepdims=True)
                vtw=v_ref[pl.ds(start,win),:].T[h*DH:(h+1)*DH]
                acc=acc*al+dot_nn(vtw,p.astype(bf16))
                out.append((mn,l,acc))
            return tuple(out)
        init=(jnp.full((1,qb),NEG,f32),jnp.zeros((1,qb),f32),jnp.zeros((DH,qb),f32))
        res=lax.fori_loop(0,lo_ref[1,i],win_step,(init,init))
        ot=jnp.concatenate([a/l for m,l,a in res],axis=0).astype(bf16)
        ot_ref[:,pl.ds(r0,qb)]=ot
        o_ref[pl.ds(r0,qb),:]=ot.T
        lse_ref[0,:,pl.ds(r0,qb)]=jnp.concatenate([m+jnp.log2(l) for m,l,a in res],axis=0)
        return 0
    single=lo_ref[2,0]==1
    @pl.when(single)
    def _():
        low=lax.broadcasted_iota(jnp.int32,(qb,PAIR),1)<DH
        def scores(i,h):
            q=q_ref[i*qb:(i+1)*qb,:]
            zero=jnp.zeros_like(q)
            qh=jnp.where(low,q,zero) if h==0 else jnp.where(low,zero,q)
            start=pl.multiple_of(lo_ref[0,i],16)
            ok=jnp.concatenate([seg_col_ref[pl.ds(start,win),:]]*(qb//PAIR),axis=1)==seg_row_ref[:,i*qb:(i+1)*qb]
            return jnp.where(ok,dot_nt(k_ref[pl.ds(start,win),:],qh)*c,NEG)
        units=[(i,h) for i in range(LEN//qb) for h in range(2)]
        ahead=3
        queue=[scores(*u) for u in units[:ahead]]
        done={}
        for n,(i,h) in enumerate(units):
            s=queue.pop(0)
            m=jnp.max(s,axis=0,keepdims=True)
            if n+ahead<len(units): queue.append(scores(*units[n+ahead]))
            p=jnp.exp2(s-m)
            l=jnp.sum(p,axis=0,keepdims=True)
            if h==0:
                vt=v_ref[pl.ds(pl.multiple_of(lo_ref[0,i],16),win),:].T
            acc=dot_nn(vt[h*DH:(h+1)*DH],p.astype(bf16))
            done[h]=(acc/l,m+jnp.log2(l))
            if h==1:
                ot=jnp.concatenate([done[0][0],done[1][0]],axis=0).astype(bf16)
                ot_ref[:,i*qb:(i+1)*qb]=ot
                o_ref[i*qb:(i+1)*qb,:]=ot.T
                lse_ref[0,:,i*qb:(i+1)*qb]=jnp.concatenate([done[0][1],done[1][1]],axis=0)
    @pl.when(jnp.logical_not(single))
    def _():
        lax.fori_loop(0,LEN//qb,block,0)

def attn_fwd(qkv, meta, seg_col, seg_row, qb=256, win=512):
    nh=HEADS//2
    return pl.pallas_call(
        functools.partial(fwd_kernel,qb,win),
        out_shape=(pltpu.VMEM((LEN,HEADS*DH),bf16),pltpu.HBM((HEADS*DH,LEN),bf16),
                   jax.ShapeDtypeStruct((nh,2,LEN),f32)),
        grid_spec=pltpu.PrefetchScalarGridSpec(num_scalar_prefetch=1,grid=(nh,),
            in_specs=[pl.BlockSpec((LEN,PAIR),lambda h,*_:(0,h)),
                      pl.BlockSpec((LEN,PAIR),lambda h,*_:(0,nh+h)),
                      pl.BlockSpec((LEN,PAIR),lambda h,*_:(0,2*nh+h)),
                      pl.BlockSpec((LEN,PAIR),lambda h,*_:(0,0)),
                      pl.BlockSpec((1,LEN),lambda h,*_:(0,0))],
            out_specs=[pl.BlockSpec((LEN,PAIR),lambda h,*_:(0,h)),
                       pl.BlockSpec((PAIR,LEN),lambda h,*_:(h,0)),
                       pl.BlockSpec((1,2,LEN),lambda h,*_:(h,0,0))],
            ),
        compiler_params=pltpu.CompilerParams(vmem_limit_bytes=VMEM_BYTES),
        cost_estimate=work(14.0),
        name="attn_fwd",
    )(meta,*[far(qkv)]*3,seg_col,seg_row)

def bwd_kernel(qb, win, lo_ref, q_ref, k_ref, v_ref, dm_ref, ot_ref, lse_ref, seg_col_ref, seg_row_ref, out_ref, dka, dva):
    dka[...]=jnp.zeros_like(dka); dva[...]=jnp.zeros_like(dva)
    c=LOG2E/math.sqrt(DH); scale=1.0/math.sqrt(DH)
    def block(i,_):
        r0=pl.multiple_of(i*qb,qb)
        q=q_ref[pl.ds(r0,qb),:]; dm=dm_ref[pl.ds(r0,qb),:]
        low=lax.broadcasted_iota(jnp.int32,(qb,PAIR),1)<DH
        zero=jnp.zeros_like(q)
        qs=(jnp.where(low,q,zero),jnp.where(low,zero,q))
        dms=(jnp.where(low,dm,zero),jnp.where(low,zero,dm))
        seg_q=seg_row_ref[:,pl.ds(r0,qb)]
        prod=dm.T.astype(f32)*ot_ref[:,pl.ds(r0,qb)].astype(f32)
        delta=[jnp.sum(prod[h*DH:(h+1)*DH],axis=0,keepdims=True) for h in range(2)]
        lse=[lse_ref[0,h:h+1,pl.ds(r0,qb)] for h in range(2)]
        def win_step(t,carry):
            start,seg_k=window(lo_ref,i,t,win,seg_col_ref)
            ok=jnp.concatenate([seg_k]*(qb//PAIR),axis=1)==seg_q
            kw=k_ref[pl.ds(start,win),:]; vw=v_ref[pl.ds(start,win),:]
            out=[]
            dk=dka[pl.ds(start,win),:]; dv=dva[pl.ds(start,win),:]
            for h in range(2):
                s=dot_nt(kw,qs[h])
                p=jnp.where(ok,jnp.exp2(s*c-lse[h]),0.0)
                dp=dot_nt(vw,dms[h])
                ds=(p*(dp-delta[h])).astype(bf16)
                dv=dv+dot_nn(p.astype(bf16),dms[h])
                dk=dk+dot_nn(ds,qs[h])
                out.append(carry[h]+dot_nn(kw.T[h*DH:(h+1)*DH],ds))
            dka[pl.ds(start,win),:]=dk; dva[pl.ds(start,win),:]=dv
            return tuple(out)
        init=jnp.zeros((DH,qb),f32)
        res=lax.fori_loop(0,lo_ref[1,i],win_step,(init,init))
        out_ref[0,pl.ds(r0,qb),:]=(jnp.concatenate(res,axis=0)*scale).T.astype(bf16)
        return 0
    single=lo_ref[2,0]==1
    @pl.when(single)
    def _():
        low=lax.broadcasted_iota(jnp.int32,(qb,PAIR),1)<DH
        def half(x,h):
            zero=jnp.zeros_like(x)
            return jnp.where(low,x,zero) if h==0 else jnp.where(low,zero,x)
        def products(i,h):
            start=pl.multiple_of(lo_ref[0,i],16)
            qh=half(q_ref[i*qb:(i+1)*qb,:],h); dmh=half(dm_ref[i*qb:(i+1)*qb,:],h)
            return dot_nt(k_ref[pl.ds(start,win),:],qh),dot_nt(v_ref[pl.ds(start,win),:],dmh),qh,dmh
        units=[(i,h) for i in range(LEN//qb) for h in range(2)]
        ahead=2
        queue=[products(*u) for u in units[:ahead]]
        dqs={}
        for n,(i,h) in enumerate(units):
            s,dp,qh,dmh=queue.pop(0)
            if n+ahead<len(units): queue.append(products(*units[n+ahead]))
            start=pl.multiple_of(lo_ref[0,i],16)
            rows=slice(i*qb,(i+1)*qb)
            if h==0:
                kt=k_ref[pl.ds(start,win),:].T
                prod=dm_ref[rows,:].T.astype(f32)*ot_ref[:,rows].astype(f32)
                ok=jnp.concatenate([seg_col_ref[pl.ds(start,win),:]]*(qb//PAIR),axis=1)==seg_row_ref[:,rows]
            delta=jnp.sum(prod[h*DH:(h+1)*DH],axis=0,keepdims=True)
            p=jnp.where(ok,jnp.exp2(s*c-lse_ref[0,h:h+1,rows]),0.0)
            ds=(p*(dp-delta)).astype(bf16)
            dva[pl.ds(start,win),:]+=dot_nn(p.astype(bf16),dmh)
            dka[pl.ds(start,win),:]+=dot_nn(ds,qh)
            dqs[h]=dot_nn(kt[h*DH:(h+1)*DH],ds)
            if h==1:
                out_ref[0,rows,:]=(jnp.concatenate([dqs[0],dqs[1]],axis=0)*scale).T.astype(bf16)
    @pl.when(jnp.logical_not(single))
    def _():
        lax.fori_loop(0,LEN//qb,block,0)
    out_ref[1]=(dka[...]*scale).astype(bf16)
    out_ref[2]=dva[...].astype(bf16)

def attn_bwd(qkv, dmixed, mixed_t, lse, meta, seg_col, seg_row, qb=256, win=512, h0=0, nh=6):
    np_=HEADS//2
    col=lambda off: pl.BlockSpec((LEN,PAIR),lambda h,*_:(0,off+h0+h))
    return pl.pallas_call(
        functools.partial(bwd_kernel,qb,win),
        out_shape=pltpu.VMEM((3,LEN,nh*PAIR),bf16),
        grid_spec=pltpu.PrefetchScalarGridSpec(num_scalar_prefetch=1,grid=(nh,),
            in_specs=[col(0),col(np_),col(2*np_),col(0),pl.BlockSpec((PAIR,LEN),lambda h,*_:(h0+h,0)),
                      pl.BlockSpec((1,2,LEN),lambda h,*_:(h0+h,0,0)),
                      pl.BlockSpec((LEN,PAIR),lambda h,*_:(0,0)),
                      pl.BlockSpec((1,LEN),lambda h,*_:(0,0))],
            out_specs=pl.BlockSpec((3,LEN,PAIR),lambda h,*_:(0,0,h)),
            scratch_shapes=[pltpu.VMEM((LEN,PAIR),f32),pltpu.VMEM((LEN,PAIR),f32)]),
        compiler_params=pltpu.CompilerParams(vmem_limit_bytes=VMEM_BYTES),
        cost_estimate=work(3.7 * nh),
        name="attn_bwd",
    )(meta,*[far(qkv)]*3,far(dmixed),far(mixed_t),lse,seg_col,seg_row)

ROWS = 256


def full(*shape):
    return pl.BlockSpec(shape, lambda *_: (0,) * len(shape))


def once(*shape):
    return pl.BlockSpec(shape, lambda *_: (0,) * len(shape), pipeline_mode=pl.Buffered(1))


def resident():
    return pl.BlockSpec(memory_space=pltpu.VMEM)


def rows_of(width):
    return pl.BlockSpec((ROWS, width), lambda i, *_: (i, 0))


def normalise(x):
    centred = x - jnp.mean(x, axis=-1, keepdims=True)
    rstd = lax.rsqrt(jnp.mean(centred * centred, axis=-1, keepdims=True) + EPS)
    return centred * rstd, rstd


def norm_back(u, gain, n, rstd):
    ug = u * gain
    return rstd * (
        ug - jnp.mean(ug, axis=-1, keepdims=True) - n * jnp.mean(ug * n, axis=-1, keepdims=True)
    )


def params():
    return pltpu.CompilerParams(vmem_limit_bytes=VMEM_BYTES)


def qkv_kernel(x_ref, gain_ref, shift_ref, w_ref, h1_ref, qkv_ref):
    n, _ = normalise(x_ref[...].astype(f32))
    h1 = (n * gain_ref[...][None] + shift_ref[...][None]).astype(bf16)
    h1_ref[...] = h1.T
    qkv_ref[...] = dot_nn(h1, w_ref[...]).astype(bf16)


def ln_qkv(tokens, gain, shift, w_qkv):
    t, d = tokens.shape
    return pl.pallas_call(
        qkv_kernel,
        grid=(t // ROWS,),
        in_specs=[rows_of(d), full(d), full(d), once(d, 3 * d)],
        out_specs=[pl.BlockSpec((d, ROWS), lambda i: (0, i)), rows_of(3 * d)],
        out_shape=(
            pltpu.HBM((d, t), bf16),
            pltpu.HBM((t, 3 * d), bf16),
        ),
        compiler_params=params(),
        cost_estimate=work(8.0),
        name="ln_qkv",
    )(far(tokens), gain, shift, far(w_qkv))


def prelude_kernel(n_slots, place_ref, seg_ref, slot_ref, meta_ref, info_ref, seg_col_ref, seg_row_ref,
                   valid_ref, voice_ref):
    seg = seg_ref[...]
    slot = slot_ref[...]
    per, lanes = seg.shape
    blocks = meta_ref.shape[1]
    rows = per // blocks
    pos = lax.broadcasted_iota(jnp.int32, seg.shape, 0) * lanes + lax.broadcasted_iota(
        jnp.int32, seg.shape, 1
    )
    most = 0
    for i in range(blocks):
        part = seg[i * rows:(i + 1) * rows]
        hit = jnp.logical_and(seg >= jnp.min(part), seg <= jnp.max(part))
        first = jnp.min(jnp.where(hit, pos, LEN))
        last = jnp.max(jnp.where(hit, pos + 1, 0))
        lo = jnp.minimum(first // 16 * 16, LEN - WIN)
        count = (last - lo + WIN - 1) // WIN
        meta_ref[0, i] = lo
        meta_ref[1, i] = count
        most = jnp.maximum(most, count)
    for i in range(blocks):
        meta_ref[2, i] = (most == 1).astype(jnp.int32)
    second = jnp.logical_and(slot >= n_slots // 2, slot < n_slots).astype(jnp.int32)
    first = (slot < n_slots // 2).astype(jnp.int32)
    info_ref[0] = jnp.max(second)
    info_ref[1] = jnp.sum(first)
    info_ref[2] = jnp.sum(second)
    lane = lax.broadcasted_iota(jnp.int32, voice_ref.shape, 1)
    voice = jnp.where(lane == place_ref[3], jnp.max(second).astype(f32), 0.0)
    voice = jnp.where(lane == 128, jnp.sum(first).astype(f32), voice)
    voice_ref[...] = jnp.where(lane == 129, jnp.sum(second).astype(f32), voice)
    seg = seg.astype(f32)
    valid = (slot < n_slots).astype(f32)
    for i in range(per):
        at = slice(i * lanes, (i + 1) * lanes)
        seg_row_ref[:, at] = seg[i:i + 1]
        seg_col_ref[at, :] = jnp.broadcast_to(seg[i:i + 1], (lanes, lanes)).T
        valid_ref[at, :] = jnp.broadcast_to(valid[i:i + 1], (lanes, lanes)).T


def prelude(place, seg_start, dispatch_slot, n_slots):
    t = seg_start.shape[0]
    smem = pl.BlockSpec(memory_space=pltpu.SMEM)
    vmem = pl.BlockSpec(memory_space=pltpu.VMEM)
    return pl.pallas_call(
        functools.partial(prelude_kernel, n_slots),
        in_specs=[smem, vmem, vmem],
        out_specs=[smem, smem, vmem, vmem, vmem, vmem],
        out_shape=(
            jax.ShapeDtypeStruct((3, LEN // QBLOCK), jnp.int32),
            jax.ShapeDtypeStruct((3,), jnp.int32),
            jax.ShapeDtypeStruct((t, PAIR), f32),
            jax.ShapeDtypeStruct((1, t), f32),
            jax.ShapeDtypeStruct((t, PAIR), f32),
            jax.ShapeDtypeStruct((1, 2 * PAIR), f32),
        ),
        cost_estimate=work(2.0),
        name="prelude",
    )(place, seg_start.reshape(t // PAIR, PAIR), dispatch_slot.reshape(t // PAIR, PAIR))


def proj_kernel(x_ref, mixed_ref, cot_ref, valid_ref, w_ref, gain_ref, shift_ref,
                resid_ref, h2_ref, cotm_ref):
    resid = x_ref[...].astype(f32) + dot_nn(mixed_ref[...], w_ref[...])
    resid_ref[...] = resid
    n, _ = normalise(resid)
    routed = jnp.concatenate([valid_ref[...]] * (resid.shape[1] // PAIR), axis=1) > 0.5
    h2 = n * gain_ref[...][None] + shift_ref[...][None]
    h2_ref[...] = jnp.where(routed, h2, 0.0).astype(bf16)
    cotm_ref[...] = jnp.where(routed, cot_ref[...].astype(f32), 0.0).astype(bf16)


def proj_ln(tokens, mixed, cotangent, valid, w_attn_out, gain, shift):
    t, d = tokens.shape
    return pl.pallas_call(
        proj_kernel,
        grid=(t // ROWS,),
        in_specs=[rows_of(d), rows_of(d), rows_of(d), rows_of(PAIR), full(d, d), full(d), full(d)],
        out_specs=[rows_of(d), rows_of(d), rows_of(d)],
        out_shape=(
            pltpu.HBM((t, d), f32),
            pltpu.VMEM((t, d), bf16),
            pltpu.VMEM((t, d), bf16),
        ),
        compiler_params=params(),
        cost_estimate=work(7.0),
        name="proj_ln",
    )(far(tokens), near(mixed), far(cotangent), valid, far(w_attn_out), gain, shift)


def gelu_parts(v):
    half = 0.5 * (1.0 + lax.erf(v * math.sqrt(0.5)))
    bell = jnp.exp(-0.5 * v * v) * (1.0 / math.sqrt(2.0 * math.pi))
    return v * half, half + v * bell


TOKENS_STEP = 256


def expert_kernel(axis, which_ref, place_ref, h2_ref, cot_ref, wina_ref, winb_ref, wouta_ref, woutb_ref,
                  hid_ref, dpre_ref, *out_refs):
    win = jnp.concatenate([wina_ref[0], winb_ref[0]], axis=1)
    wout = jnp.concatenate([wouta_ref[0], woutb_ref[0]], axis=0)
    hiddens, d_pres = [], []
    for at in range(0, h2_ref.shape[0], TOKENS_STEP):
        rows = slice(at, at + TOKENS_STEP)
        hidden, slope = gelu_parts(dot_nn(h2_ref[rows, :], win))
        hidden = hidden.astype(bf16)
        d_pre = (dot_nt(cot_ref[rows, :], wout) * slope).astype(bf16)
        hid_ref[rows, :] = hidden
        dpre_ref[rows, :] = d_pre
        hiddens.append(hidden)
        d_pres.append(d_pre)
    g_in = dot_tn(jnp.concatenate(d_pres, axis=0), h2_ref[...]).astype(bf16)
    g_out = dot_tn(jnp.concatenate(hiddens, axis=0), cot_ref[...]).astype(bf16)
    unit = wina_ref.shape[2]
    if axis is None:
        e = which_ref[0]
        for core in range(2):
            for j, g in enumerate((g_in, g_out)):
                part = g[core * unit:(core + 1) * unit]
                n_dp = out_refs[0].shape[1]
                step = unit // n_dp
                for to in range(n_dp):
                    piece = part[to * step:(to + 1) * step]
                    out_refs[0][core, to, e, j] = piece
                    out_refs[0][core, to, 1 - e, j] = jnp.zeros_like(piece)
    else:
        hold = out_refs[4]
        hold[0] = g_in
        hold[1] = g_out
        half = unit // 2
        for k in range(4):
            core, side = place_ref[0] ^ (k & 1), place_ref[axis] ^ (k >> 1)
            at = pl.multiple_of(core * unit + side * half, half)
            for j in range(2):
                out_refs[k][0, j] = hold[j, pl.ds(at, half), :]


def expert_part(which, place, h2, cot, w_in, w_out, p, axis, unit, n_z, n_dp=1):
    t, d = h2.shape
    parts = w_in.shape[2] // (unit * n_z * 2)

    def column(core):
        return pl.BlockSpec((1, d, unit), lambda z, w, _: (w[0], 0, parts * (2 * z + core) + p))

    def row(core):
        return pl.BlockSpec((1, unit, d), lambda z, w, _: (w[0], parts * (2 * z + core) + p, 0))

    if axis is None:
        step = unit // n_dp
        shapes = [pltpu.HBM((2 * n_z, n_dp, 2, 2, step, d), bf16)]
        specs = [pl.BlockSpec((2, n_dp, 2, 2, step, d), lambda z, *_: (z, 0, 0, 0, 0, 0))]
        scratch = []
    else:
        shapes = [pltpu.HBM((n_z, 2, unit // 2, d), bf16)] * 4
        specs = [pl.BlockSpec((1, 2, unit // 2, d), lambda z, *_: (z, 0, 0, 0))] * 4
        scratch = [pltpu.VMEM((2, 2 * unit, d), bf16)]
    act = (t, 2 * n_z * unit)
    act_spec = pl.BlockSpec((t, 2 * unit), lambda z, *_: (0, z))
    return pl.pallas_call(
        functools.partial(expert_kernel, axis),
        grid_spec=pltpu.PrefetchScalarGridSpec(
            num_scalar_prefetch=2,
            grid=(n_z,),
            in_specs=[resident(), resident(), column(0), column(1), row(0), row(1)],
            out_specs=[act_spec, act_spec] + specs,
            scratch_shapes=scratch,
        ),
        out_shape=[pltpu.HBM(act, bf16), pltpu.HBM(act, bf16)] + shapes,
        compiler_params=params(),
        cost_estimate=work(33.0 / parts),
        name="expert_part",
    )(which, place, near(h2), near(cot), *[far(w_in)] * 2, *[far(w_out)] * 2)


def in_order(refs, unit):
    blocks = refs[0].shape[1] // unit
    return jnp.concatenate(
        [r[:, b * unit:(b + 1) * unit] for b in range(blocks) for r in refs], axis=1
    )


def post_kernel(n, unit, which_ref, *refs):
    dpre_refs, rest = refs[:n], refs[n:]
    win_ref, resid_ref, cot_ref, w_ref, gain_ref, dres_ref, dbr_ref, dmix_ref, gvec_ref = rest
    u = dot_nt(in_order(dpre_refs, unit), win_ref[0]).astype(bf16).astype(f32)
    nrm, rstd = normalise(resid_ref[...])
    d_resid = cot_ref[...].astype(f32) + norm_back(u, gain_ref[...][None], nrm, rstd)
    dres_ref[...] = d_resid
    d_branch = d_resid.astype(bf16)
    dbr_ref[...] = d_branch
    dmix_ref[...] = dot_nt(d_branch, w_ref[...]).astype(bf16)
    gg = jnp.sum(u * nrm, axis=0, keepdims=True)
    gs = jnp.sum(u, axis=0, keepdims=True)
    step = pl.program_id(0)

    @pl.when(step == 0)
    def _():
        gvec_ref[0:1, :] = gg
        gvec_ref[1:2, :] = gs

    @pl.when(step > 0)
    def _():
        gvec_ref[0:1, :] += gg
        gvec_ref[1:2, :] += gs


def post_ffn(which, d_pres, w_in, resid, cotangent, w_attn_out, gain, unit):
    t, d = resid.shape
    n = len(d_pres)
    ff = w_in.shape[2]
    return pl.pallas_call(
        functools.partial(post_kernel, n, unit),
        grid_spec=pltpu.PrefetchScalarGridSpec(
            num_scalar_prefetch=1,
            grid=(t // ROWS,),
            in_specs=[rows_of(ff // n)] * n
            + [pl.BlockSpec((1, d, ff), lambda i, w: (w[0], 0, 0), pipeline_mode=pl.Buffered(1))]
            + [rows_of(d)] * 2
            + [full(d, d), full(d)],
            out_specs=[rows_of(d)] * 3 + [full(2, d)],
        ),
        out_shape=(
            pltpu.HBM((t, d), f32),
            pltpu.HBM((t, d), bf16),
            pltpu.HBM((t, d), bf16),
            jax.ShapeDtypeStruct((2, d), f32),
        ),
        compiler_params=params(),
        cost_estimate=work(10.0),
        name="post_ffn",
    )(which, *[far(v) for v in d_pres], far(w_in), far(resid), far(cotangent), far(w_attn_out), gain)


def result_kernel(n, unit, which_ref, *refs):
    wout_ref, resid_ref, out_ref = refs[n:]
    ffn = dot_nn(in_order(refs[:n], unit), wout_ref[0]).astype(bf16).astype(f32)
    out_ref[...] = (resid_ref[...] + ffn).astype(bf16)


def result_of(which, hiddens, w_out, resid, unit):
    t, d = resid.shape
    n = len(hiddens)
    ff = w_out.shape[1]
    return pl.pallas_call(
        functools.partial(result_kernel, n, unit),
        grid_spec=pltpu.PrefetchScalarGridSpec(
            num_scalar_prefetch=1,
            grid=(t // ROWS,),
            in_specs=[rows_of(ff // n)] * n
            + [pl.BlockSpec((1, ff, d), lambda i, w: (w[0], 0, 0), pipeline_mode=pl.Buffered(1)), rows_of(d)],
            out_specs=rows_of(d),
        ),
        out_shape=pltpu.HBM((t, d), bf16),
        compiler_params=params(),
        cost_estimate=work(8.0),
        name="result_of",
    )(which, *[far(v) for v in hiddens], far(w_out), far(resid))


def weight_kernel(c_ref, *refs):
    extra = len(refs) == 6
    h1_ref, d_ref = refs[:2]
    other_ref, mine_ref = refs[-2:]
    half = other_ref.shape[0]
    mine_at = pl.multiple_of(c_ref[0] * half, half)
    other_at = pl.multiple_of(half - c_ref[0] * half, half)

    def products(left_ref, right):
        other_ref[...] = dot_nn(left_ref[pl.ds(other_at, half), :], right).astype(bf16)
        mine_ref[...] = dot_nn(left_ref[pl.ds(mine_at, half), :], right).astype(bf16)

    if not extra:
        products(h1_ref, d_ref[0])
        return

    @pl.when(pl.program_id(0) < 3)
    def _():
        products(h1_ref, d_ref[0])

    @pl.when(pl.program_id(0) >= 3)
    def _():
        products(refs[2], refs[3][...])


def weight_grads(core, h1_t, d_qkv, more=()):
    d, t = h1_t.shape
    half, width = d // 2, d_qkv.shape[2]
    blocks = 3
    specs = [full(d, t), pl.BlockSpec((1, t, width), lambda i, c: (jnp.minimum(i, 2), 0, 0))]
    if more:
        specs += [full(d, t), pl.BlockSpec((t, width), lambda i, c: (0, jnp.maximum(i - 3, 0)))]
        blocks += more[1].shape[1] // width
    shape = pltpu.HBM((half, blocks * width), bf16)
    return pl.pallas_call(
        weight_kernel,
        grid_spec=pltpu.PrefetchScalarGridSpec(
            num_scalar_prefetch=1,
            grid=(blocks,),
            in_specs=specs,
            out_specs=[pl.BlockSpec((half, width), lambda i, c: (0, i))] * 2,
        ),
        out_shape=(shape, shape),
        compiler_params=params(),
        cost_estimate=work(1.2 * blocks * width / half),
        name="weight_grads",
    )(core, far(h1_t), near(d_qkv), *[far(v) for v in more])


def input_kernel(groups, *refs):
    ins, (x_ref, dres_ref, w_ref, gain_ref, gtok_ref, gvec_ref) = refs[:groups], refs[groups:]
    side = jnp.concatenate([r[j] for j in range(3) for r in ins], axis=1)
    u = dot_nt(side, w_ref[...])
    n, rstd = normalise(x_ref[...].astype(f32))
    gtok_ref[...] = dres_ref[...] + norm_back(u, gain_ref[...][None], n, rstd)
    gg = jnp.sum(u * n, axis=0, keepdims=True)
    gs = jnp.sum(u, axis=0, keepdims=True)
    first = pl.program_id(0) == 0

    @pl.when(first)
    def _():
        gvec_ref[0:1, :] = gg
        gvec_ref[1:2, :] = gs

    @pl.when(jnp.logical_not(first))
    def _():
        gvec_ref[0:1, :] += gg
        gvec_ref[1:2, :] += gs


def input_grad(parts, tokens, d_resid, w_qkv, gain):
    t, d = tokens.shape
    return pl.pallas_call(
        functools.partial(input_kernel, len(parts)),
        grid=(t // ROWS,),
        in_specs=[pl.BlockSpec((3, ROWS, p.shape[2]), lambda i: (0, i, 0)) for p in parts]
        + [rows_of(d), rows_of(d), once(d, 3 * d), full(d)],
        out_specs=[rows_of(d), full(2, d)],
        out_shape=(
            pltpu.HBM((t, d), f32),
            jax.ShapeDtypeStruct((2, d), f32),
        ),
        compiler_params=params(),
        cost_estimate=work(10.0),
        name="input_grad",
    )(*[far(p) for p in parts], far(tokens), far(d_resid), far(w_qkv), gain)


def sum_kernel(axis, place_ref, voice_ref, a_ref, b_ref, c_ref, d_ref, keep_ref, send_ref):
    me = place_ref[3]
    bit = place_ref[3 - axis]
    step = keep_ref.shape[3]
    for j in range(2):
        for out_ref, mine in ((keep_ref, bit), (send_ref, 1 - bit)):
            at = pl.multiple_of(mine * step, step)
            sides = [None, None]
            for k, ref in enumerate((a_ref, b_ref, c_ref, d_ref)):
                term = ref[0, j, pl.ds(at, step), :].astype(f32)
                second = voice_ref[me ^ ((k & 1) | ((k >> 1) << axis))] == 1
                for e in range(2):
                    part = jnp.where(second, term if e else 0.0, 0.0 if e else term)
                    sides[e] = part if sides[e] is None else sides[e] + part
            for e in range(2):
                out_ref[0, e, j] = sides[e].astype(bf16)


def sum_sides(axis, place, voice, got):
    n_z, two, rows, d = got[0].shape
    spec = pl.BlockSpec((1, two, rows, d), lambda z, *_: (z, 0, 0, 0))
    out = pl.BlockSpec((1, 2, two, rows // 2, d), lambda z, *_: (z, 0, 0, 0, 0))
    shape = jax.ShapeDtypeStruct((n_z, 2, two, rows // 2, d), bf16)
    return pl.pallas_call(
        functools.partial(sum_kernel, axis),
        grid_spec=pltpu.PrefetchScalarGridSpec(
            num_scalar_prefetch=2,
            grid=(n_z,),
            in_specs=[spec] * 4,
            out_specs=[out, out],
        ),
        out_shape=(shape, shape),
        compiler_params=params(),
        cost_estimate=work(3.0),
        name="sum_sides",
    )(place, voice, *[near(v) for v in got])


def finish_kernel(axes, place_ref, tally_ref, *refs):
    blocks, (gin_ref, gout_ref, counts_ref, hold_ref) = refs[:-4], refs[-4:]
    spots = [(ref, k) for ref in blocks for k in range(ref.shape[1])]
    d = gin_ref.shape[1]
    lane = lax.broadcasted_iota(jnp.int32, tally_ref.shape, 1)
    counts = [jnp.sum(jnp.where(lane == 128 + e, tally_ref[...], 0.0)) for e in range(2)]
    for e in range(2):
        counts_ref[e] = counts[e].astype(jnp.int32)
    unit = hold_ref.shape[0]
    step = unit // 4
    for p, ((ref, part), axis) in enumerate(zip(spots, axes)):
        for e in range(2):
            factor = jnp.full((1, d), counts[0] + counts[1], f32) / (2.0 * counts[e])
            for j in range(2):
                for k in range(4):
                    to = 2 * (k & 1) + (k >> 1) if axis == X else k
                    rows = slice(to * step, (to + 1) * step)
                    hold_ref[rows, :] = ref[k, part, e, j].astype(f32) * factor
                where = slice(p * unit, (p + 1) * unit)
                if j == 0:
                    gin_ref[e, :, where] = hold_ref[...].T
                else:
                    gout_ref[e, where, :] = hold_ref[...]


def finish_experts(axes, place, tally, blocks):
    step, d = blocks[0].shape[-2:]
    n = len(axes)
    smem = pl.BlockSpec(memory_space=pltpu.SMEM)
    return pl.pallas_call(
        functools.partial(finish_kernel, axes),
        in_specs=[smem] + [resident()] * (1 + len(blocks)),
        out_specs=[resident(), resident(), smem],
        out_shape=(
            jax.ShapeDtypeStruct((2, d, n * 4 * step), f32),
            jax.ShapeDtypeStruct((2, n * 4 * step, d), f32),
            jax.ShapeDtypeStruct((2,), jnp.int32),
        ),
        scratch_shapes=[pltpu.VMEM((4 * step, d), f32)],
        compiler_params=params(),
        cost_estimate=work(4.0),
        name="finish_experts",
    )(place, tally, *[near(v) for v in blocks])


def join_kernel(widths, place_ref, *refs):
    n = len(widths)
    gw_ref, gwo_ref, vec_ref = refs[2 * n:]
    d = gwo_ref.shape[2]
    rows = gwo_ref.shape[1]
    rel = pl.program_id(0) ^ (place_ref[3] >> 1)
    at = place_ref[3] >> 1
    vec = refs[2 * n - 2][at, rows:, :d].astype(f32) + refs[2 * n - 1][at, rows:, :d].astype(f32)
    vec_ref[...] = vec[:8]
    before = 0
    for k, width in enumerate(widths):
        for half, ref in ((place_ref[0], refs[2 * k]), (1 - place_ref[0], refs[2 * k + 1])):
            for third in range(3):
                at, src = third * d + before, third * width
                gw_ref[half, :, at:at + width] = ref[rel, :rows, src:src + width].astype(f32)
            if k == 0:
                gwo_ref[half] = ref[rel, :rows, 3 * width:].astype(f32)
        before += width


def join_weights(place, sums, d):
    step = d // 8
    extra = [d] + [0] * (len(sums) - 1)
    widths = [(s[0].shape[2] - x) // 3 for s, x in zip(sums, extra)]
    flat = [v for pair in sums for v in pair]
    gw, gwo, vec = pl.pallas_call(
        functools.partial(join_kernel, widths),
        grid_spec=pltpu.PrefetchScalarGridSpec(
            num_scalar_prefetch=1,
            grid=(4,),
            in_specs=[resident()] * len(flat),
            out_specs=[
                pl.BlockSpec((2, step, 3 * d), lambda i, *_: (0, i, 0)),
                pl.BlockSpec((2, step, d), lambda i, *_: (0, i, 0)),
                full(8, d),
            ],
        ),
        out_shape=(
            jax.ShapeDtypeStruct((2, d // 2, 3 * d), f32),
            jax.ShapeDtypeStruct((2, d // 2, d), f32),
            jax.ShapeDtypeStruct((8, d), f32),
        ),
        compiler_params=params(),
        cost_estimate=work(5.0),
        name="join_weights",
    )(place, *[near(v) for v in flat])
    return gw.reshape(d, 3 * d), gwo.reshape(d, d), vec


X, Y = 1, 2
NEAR = [(0, 1), (1, 0), (2, 3), (3, 2)]
FAR = [(0, 3), (3, 0), (1, 2), (2, 1)]


def swap_core(v):
    return lax.ppermute(v, "core", [(0, 1), (1, 0)])


def swap(v, axis):
    return lax.ppermute(v, "dp", [(i, i ^ axis) for i in range(4)])


def swap_both(v, axis):
    return lax.ppermute(v, ("dp", "core"), [(i, i ^ (1 | (axis << 1))) for i in range(8)])


def along_z(v, pairs):
    return lax.ppermute(v, "z", pairs)


def tie(v, *after):
    return lax.optimization_barrier((v,) + after)[0] if after else v


def small_kernel(fn, *refs):
    out_ref = refs[-1]
    out_ref[...] = fn(*[r[...] for r in refs[:-1]]).astype(out_ref.dtype)


def small(fn, *args, space=pltpu.VMEM, name="small"):
    shape = jax.eval_shape(fn, *args)
    return pl.pallas_call(
        functools.partial(small_kernel, fn),
        in_specs=[resident()] * len(args),
        out_specs=resident(),
        out_shape=pltpu.VMEM(shape.shape, args[0].dtype),
        compiler_params=params(),
        cost_estimate=work(1.0),
        name=name,
    )(*[near(v) for v in args])


def add_f32(a, b):
    return a.astype(f32) + b.astype(f32)


def add(a, b):
    return small(add_f32, a, b, name="add")


def merge_kernel(mine_ref, away_ref, first_ref, second_ref, out_ref):
    n, rows, width = out_ref.shape
    rows -= 16
    d = first_ref.shape[1]
    for k in range(n):
        at = slice(k * rows, (k + 1) * rows)
        out_ref[k, :rows] = (mine_ref[at, :].astype(f32) + away_ref[at, :].astype(f32)).astype(bf16)
        out_ref[k, rows:] = jnp.zeros((16, width), bf16)
    small = jnp.concatenate([first_ref[...], second_ref[...], jnp.zeros((12, d), f32)], axis=0)
    out_ref[0, rows:, :d] = small.astype(bf16)


def merge_small(mine, away, first, second):
    half, width = mine.shape
    return pl.pallas_call(
        merge_kernel,
        in_specs=[resident()] * 4,
        out_specs=resident(),
        out_shape=pltpu.VMEM((4, half // 4 + 16, width), bf16),
        compiler_params=params(),
        cost_estimate=work(1.0),
        name="merge_small",
    )(near(mine), near(away), first, second)


def split_kernel(axis, place_ref, *refs):
    keep_ref, send_ref = refs[-2:]
    bit = place_ref[axis]
    for out_ref, at in ((keep_ref, bit), (send_ref, 1 - bit)):
        v = refs[0][at]
        for r in refs[1:-2]:
            v = v.astype(f32) + r[at].astype(f32)
        out_ref[...] = v.astype(bf16)


def split(place, axis, *v):
    shape = pltpu.VMEM(v[0].shape[1:], bf16)
    return pl.pallas_call(
        functools.partial(split_kernel, axis),
        in_specs=[pl.BlockSpec(memory_space=pltpu.SMEM)] + [resident()] * len(v),
        out_specs=[resident()] * 2,
        out_shape=(shape, shape),
        compiler_params=params(),
        cost_estimate=work(1.0),
        name="split",
    )(place, *[near(x) for x in v])


def total(v):
    return small(lambda x: sum(x[k].astype(f32) for k in range(x.shape[0])), v, name="total")


def stack(*v):
    return small(lambda *x: jnp.stack(x), *v, name="stack")


class Line:
    def __init__(self):
        self.last = ()

    def __call__(self, step, first, *rest):
        out = step(tie(first, *self.last), *rest)
        self.last = (jax.tree.leaves(out)[0],)
        return out


UNIT = 128
QBLOCK = 256
WIN = 512
GROUPS = (3, 3)


def tuned(tokens, cotangent, seg_start, dispatch_slot, ln1_gain, ln1_shift, w_qkv, w_attn_out,
          ln2_gain, ln2_shift, w_in, w_out):
    tok_count, d = tokens.shape
    n_z = lax.axis_size("z")
    n_slots = 2 * n_z * (2 * tok_count // (2 * n_z))
    core, dp = lax.axis_index("core"), lax.axis_index("dp")
    bits = {X: dp & 1, Y: dp >> 1}
    place = jnp.stack([core, bits[X], bits[Y], dp * 2 + core]).astype(jnp.int32)
    line = Line()
    PHASE[0] = "early"

    def around(v):
        return [v, swap(v, X), swap(v, Y), swap(v, X | Y)]

    def exchange(v):
        return lax.all_to_all(v, "dp", split_axis=0, concat_axis=0, tiled=True)

    def merge(a, b):
        return small(add_f32, a, b, name="merge").reshape(4, -1, a.shape[1])

    meta, info, seg_col, seg_row, valid, voice = prelude(place, seg_start, dispatch_slot, n_slots)
    away = swap_core(voice)
    h1_t, qkv = line(ln_qkv, tokens, ln1_gain, ln1_shift, w_qkv)
    voice = line(add, voice, away)
    away = swap(voice, X)
    mixed, mixed_t, lse = line(
        lambda v: attn_fwd(v, meta, seg_col, seg_row, QBLOCK, WIN), qkv
    )
    voice = line(add, voice, away)
    away = swap(voice, Y)
    resid, h2, cotm = line(
        lambda v: proj_ln(tokens, v, cotangent, valid, w_attn_out, ln2_gain, ln2_shift), mixed
    )
    tally = line(add, voice, away)
    voice = tally[0, :8].astype(jnp.int32)

    def expert(p, axis):
        return line(
            lambda v: expert_part(info, place, v, cotm, w_in, w_out, p, axis, UNIT, n_z, 4), h2
        )

    def plane(pieces, axis):
        return [pieces[0], swap_core(pieces[1]), swap(pieces[2], axis), swap_both(pieces[3], axis)]

    hid_b, dpre_b, *out_b = expert(1, X)
    got_b = plane(out_b, X)
    hid_a, dpre_a, out_a = expert(0, None)
    own_a = lax.psum_scatter(out_a, ("z", "core"), scatter_dimension=0, tiled=True)
    hid_c, dpre_c, *out_c = expert(2, Y)
    got_c = plane(out_c, Y)
    d_resid, d_branch, d_mixed, gvec2 = line(
        lambda v: post_ffn(
            info, (dpre_a, v, dpre_c), w_in, resid, cotangent, w_attn_out, ln2_gain, UNIT
        ),
        dpre_b,
    )

    def sides(got, axis):
        return line(lambda v: sum_sides(axis, place, voice, (got[0], got[1], got[2], v)), got[3])

    def bwd(at, nh):
        return line(
            lambda v: attn_bwd(qkv, v, mixed_t, lse, meta, seg_col, seg_row, QBLOCK, WIN, at, nh),
            d_mixed,
        )

    def scatter_z(v):
        return lax.psum_scatter(v, "z", scatter_dimension=0, tiled=True)[0]

    one, two = GROUPS
    keep_b, send_b = sides(got_b, X)
    away_b = swap(send_b, Y)
    d_qkv_1 = bwd(0, one)
    other_1, mine_1 = line(lambda v: weight_grads(place, v, d_qkv_1, (mixed_t, d_branch)), h1_t)
    away_1 = swap_core(other_1)
    keep_c, send_c = sides(got_c, Y)
    away_c = swap(send_c, X)
    both_b = line(add, keep_b, away_b)
    half_b = scatter_z(both_b)
    keep_a, send_a = line(lambda v: split(place, Y, v.reshape((2, 2) + v.shape[1:])), own_a[0])
    away_a = swap(send_a, Y)
    all_1 = exchange(line(merge, mine_1, away_1))
    d_qkv_2 = bwd(one, two)
    PHASE[0] = "late"
    PHASE[0] = "early"
    other_2, mine_2 = line(lambda v: weight_grads(place, v, d_qkv_2), h1_t)
    away_2 = swap_core(other_2)
    PHASE[0] = "late"
    both_c = line(add, keep_c, away_c)
    half_c = scatter_z(both_c)
    keep_a, send_a = line(lambda a, b: split(place, X, a, b), keep_a, away_a)
    away_a = swap(send_a, X)
    piece_1 = line(total, all_1)
    away_1 = along_z(piece_1, NEAR)

    def copies(*v):
        return small(lambda *x: jnp.stack([jnp.stack(x)] * 4), *v, name="copies")

    away_t = along_z(tie(tally, mine_2), NEAR)
    grad_tokens, gvec1 = line(
        lambda v: input_grad((d_qkv_1, d_qkv_2), v, d_resid, w_qkv, ln1_gain), tokens
    )
    all_2 = exchange(line(lambda a, b: merge_small(a, b, gvec1, gvec2), mine_2, away_2))
    piece_1 = line(add, piece_1, away_1)
    away_1 = along_z(piece_1, FAR)
    tally = line(add, tally, away_t)
    away_t = along_z(tally, FAR)
    half_a = line(add, keep_a, away_a)
    result_out = line(lambda v: result_of(info, (hid_a, hid_b, hid_c), w_out, v, UNIT), resid)
    piece_2 = line(total, all_2)
    away_2 = along_z(piece_2, NEAR)
    PHASE[0] = "tail"
    all_e = exchange(line(copies, half_a, half_b, half_c))
    piece_2 = line(add, piece_2, away_2)
    away_2 = along_z(piece_2, FAR)
    piece_1 = line(add, piece_1, away_1)
    around_1 = around(piece_1)
    piece_2 = line(add, piece_2, away_2)
    around_2 = around(piece_2)
    whole_1 = line(stack, *around_1)
    other_1 = swap_core(whole_1)
    tally = line(add, tally, away_t)
    grad_w_in, grad_w_out, all_counts = line(
        lambda v: finish_experts((Y, X, Y), place, tie(tally, piece_2), (v,)), all_e
    )
    whole_2 = line(stack, *around_2)
    other_2 = swap_core(whole_2)
    grad_wqkv, grad_wo, vectors = join_weights(
        place, ((tie(whole_1, *line.last), other_1), (whole_2, other_2)), d
    )
    PHASE[0] = "early"
    return (
        result_out, grad_tokens, vectors[0], vectors[1], grad_wqkv, grad_wo, vectors[2], vectors[3],
        grad_w_in, grad_w_out, all_counts,
    )


def general(tokens, cotangent, seg_start, dispatch_slot, ln1_gain, ln1_shift, w_qkv, w_attn_out,
            ln2_gain, ln2_shift, w_in, w_out):
    tok_count, d = tokens.shape
    n_expert = lax.axis_size("expert")
    n_slots = n_expert * (2 * tok_count // n_expert)
    everywhere = ("dp", "expert")
    first_half = jnp.zeros((1,), jnp.int32)
    meta, info, seg_col, seg_row, valid, _ = prelude(
        jnp.zeros((4,), jnp.int32), seg_start, dispatch_slot, n_slots
    )
    h1_t, qkv = ln_qkv(tokens, ln1_gain, ln1_shift, w_qkv)
    mixed, mixed_t, lse = attn_fwd(qkv, meta, seg_col, seg_row, QBLOCK, WIN)
    resid, h2, cotm = proj_ln(tokens, mixed, cotangent, valid, w_attn_out, ln2_gain, ln2_shift)
    blocks = w_in.shape[2] // (UNIT * 2)
    hidden, d_pre, grads = expert_part(
        info, first_half, h2, cotm, w_in, w_out, 0, None, UNIT, blocks
    )
    grads = jnp.transpose(grads[:, 0], (1, 2, 0, 3, 4)).reshape(2, 2, 2 * blocks * UNIT, d)
    grads = lax.psum_scatter(grads, "expert", scatter_dimension=2, tiled=True)
    grads = lax.psum(grads, "dp").astype(f32)
    d_resid, d_branch, d_mixed, gvec2 = post_ffn(
        info, (d_pre,), w_in, resid, cotangent, w_attn_out, ln2_gain, UNIT
    )
    result_out = result_of(info, (hidden,), w_out, resid, UNIT)
    d_qkv = attn_bwd(qkv, d_mixed, mixed_t, lse, meta, seg_col, seg_row, QBLOCK, WIN)
    bottom, top = weight_grads(first_half, h1_t, d_qkv, (mixed_t, d_branch))
    grad_tokens, gvec1 = input_grad((d_qkv,), tokens, d_resid, w_qkv, ln1_gain)
    weights = lax.psum(jnp.concatenate([top, bottom], axis=0), everywhere).astype(f32)
    grad_wqkv, grad_wo = weights[:, : 3 * d], weights[:, 3 * d:]
    counts, gvec1, gvec2 = lax.psum((info[1:].astype(f32), gvec1, gvec2), everywhere)
    factor = (jnp.sum(counts) / (2.0 * counts))[:, None, None]
    return (
        result_out, grad_tokens, gvec1[0], gvec1[1], grad_wqkv, grad_wo,
        gvec2[0], gvec2[1], jnp.transpose(grads[:, 0], (0, 2, 1)) * factor, grads[:, 1] * factor,
        counts.astype(jnp.int32),
    )


def solution(mesh):
    n_dp, n_expert = mesh.shape["dp"], mesh.shape["expert"]
    if (n_dp, n_expert) == (4, 8):
        mesh = Mesh(mesh.devices.reshape(n_dp, n_expert // 2, 2), ("dp", "z", "core"))
        body, expert = tuned, ("z", "core")
    else:
        body, expert = general, ("expert",)
    everywhere = ("dp",) + expert
    rows = P(everywhere, None)
    flat = P(everywhere)
    rep = P()
    return jax.shard_map(
        body,
        mesh=mesh,
        in_specs=(rows, rows, flat, flat) + (rep,) * 8,
        out_specs=(rows, rows) + (rep,) * 6 + (P(None, None, expert), P(None, expert, None), rep),
        check_vma=False,
    )
```

```python
import functools
import math

import jax
import jax.numpy as jnp
from jax import lax
from jax.experimental import pallas as pl
from jax.experimental.pallas import tpu as pltpu
from jax.sharding import Mesh, PartitionSpec as P

HEADS = 12
DH = 64
LEN = 1024
NEG = -1e30
EPS = 1e-05
PAIR = 128
LOG2E = math.log2(math.e)
bf16 = jnp.bfloat16
f32 = jnp.float32
VMEM_BYTES = 22 << 20
COST = {"early": 1e11, "late": 1.2e9, "none": 0.0, "tail": 1e11}
PHASE = ["early"]


def near(v):
    return pltpu.with_memory_space_constraint(v, pltpu.VMEM)


def far(v):
    return pltpu.with_memory_space_constraint(v, pltpu.HBM)


def work(us):
    return pl.CostEstimate(flops=int(us * COST[PHASE[0]]), bytes_accessed=1 << 20, transcendentals=0)


def dot_nn(a, b):
    return lax.dot_general(a, b, (((1,), (0,)), ((), ())), preferred_element_type=f32)


def dot_nt(a, b):
    return lax.dot_general(a, b, (((1,), (1,)), ((), ())), preferred_element_type=f32)


def dot_tn(a, b):
    return lax.dot_general(a, b, (((0,), (0,)), ((), ())), preferred_element_type=f32)


def window(lo_ref, i, t, win, seg_col_ref):
    base=lo_ref[0,i]+t*win
    start=pl.multiple_of(jnp.minimum(base,LEN-win),16)
    seg_k=seg_col_ref[pl.ds(start,win),:]
    pos=start+lax.broadcasted_iota(jnp.int32,(win,PAIR),0)
    return start, jnp.where(pos>=base,seg_k,jnp.full_like(seg_k,-1))

def fwd_kernel(qb, win, lo_ref, q_ref, k_ref, v_ref, seg_col_ref, seg_row_ref, o_ref, ot_ref, lse_ref):
    c=LOG2E/math.sqrt(DH)
    def block(i,_):
        r0=pl.multiple_of(i*qb,qb)
        q=q_ref[pl.ds(r0,qb),:]
        low=lax.broadcasted_iota(jnp.int32,(qb,PAIR),1)<DH
        zero=jnp.zeros_like(q)
        qs=(jnp.where(low,q,zero),jnp.where(low,zero,q))
        seg_q=seg_row_ref[:,pl.ds(r0,qb)]
        def win_step(t,carry):
            start,seg_k=window(lo_ref,i,t,win,seg_col_ref)
            ok=jnp.concatenate([seg_k]*(qb//PAIR),axis=1)==seg_q
            kw=k_ref[pl.ds(start,win),:]
            out=[]
            for h in range(2):
                m,l,acc=carry[h]
                s=jnp.where(ok,dot_nt(kw,qs[h])*c,NEG)
                mn=jnp.maximum(m,jnp.max(s,axis=0,keepdims=True))
                al=jnp.exp2(m-mn)
                p=jnp.exp2(s-mn)
                l=l*al+jnp.sum(p,axis=0,keepdims=True)
                vtw=v_ref[pl.ds(start,win),:].T[h*DH:(h+1)*DH]
                acc=acc*al+dot_nn(vtw,p.astype(bf16))
                out.append((mn,l,acc))
            return tuple(out)
        init=(jnp.full((1,qb),NEG,f32),jnp.zeros((1,qb),f32),jnp.zeros((DH,qb),f32))
        res=lax.fori_loop(0,lo_ref[1,i],win_step,(init,init))
        ot=jnp.concatenate([a/l for m,l,a in res],axis=0).astype(bf16)
        ot_ref[:,pl.ds(r0,qb)]=ot
        o_ref[pl.ds(r0,qb),:]=ot.T
        lse_ref[0,:,pl.ds(r0,qb)]=jnp.concatenate([m+jnp.log2(l) for m,l,a in res],axis=0)
        return 0
    single=lo_ref[2,0]==1
    @pl.when(single)
    def _():
        low=lax.broadcasted_iota(jnp.int32,(qb,PAIR),1)<DH
        def scores(i,h):
            q=q_ref[i*qb:(i+1)*qb,:]
            zero=jnp.zeros_like(q)
            qh=jnp.where(low,q,zero) if h==0 else jnp.where(low,zero,q)
            start=pl.multiple_of(lo_ref[0,i],16)
            ok=jnp.concatenate([seg_col_ref[pl.ds(start,win),:]]*(qb//PAIR),axis=1)==seg_row_ref[:,i*qb:(i+1)*qb]
            return jnp.where(ok,dot_nt(k_ref[pl.ds(start,win),:],qh)*c,NEG)
        units=[(i,h) for i in range(LEN//qb) for h in range(2)]
        ahead=3
        queue=[scores(*u) for u in units[:ahead]]
        done={}
        for n,(i,h) in enumerate(units):
            s=queue.pop(0)
            m=jnp.max(s,axis=0,keepdims=True)
            if n+ahead<len(units): queue.append(scores(*units[n+ahead]))
            p=jnp.exp2(s-m)
            l=jnp.sum(p,axis=0,keepdims=True)
            if h==0:
                vt=v_ref[pl.ds(pl.multiple_of(lo_ref[0,i],16),win),:].T
            acc=dot_nn(vt[h*DH:(h+1)*DH],p.astype(bf16))
            done[h]=(acc/l,m+jnp.log2(l))
            if h==1:
                ot=jnp.concatenate([done[0][0],done[1][0]],axis=0).astype(bf16)
                ot_ref[:,i*qb:(i+1)*qb]=ot
                o_ref[i*qb:(i+1)*qb,:]=ot.T
                lse_ref[0,:,i*qb:(i+1)*qb]=jnp.concatenate([done[0][1],done[1][1]],axis=0)
    @pl.when(jnp.logical_not(single))
    def _():
        lax.fori_loop(0,LEN//qb,block,0)

def attn_fwd(qkv, meta, seg_col, seg_row, qb=256, win=512):
    nh=HEADS//2
    return pl.pallas_call(
        functools.partial(fwd_kernel,qb,win),
        out_shape=(pltpu.VMEM((LEN,HEADS*DH),bf16),pltpu.HBM((HEADS*DH,LEN),bf16),
                   jax.ShapeDtypeStruct((nh,2,LEN),f32)),
        grid_spec=pltpu.PrefetchScalarGridSpec(num_scalar_prefetch=1,grid=(nh,),
            in_specs=[pl.BlockSpec((LEN,PAIR),lambda h,*_:(0,h)),
                      pl.BlockSpec((LEN,PAIR),lambda h,*_:(0,nh+h)),
                      pl.BlockSpec((LEN,PAIR),lambda h,*_:(0,2*nh+h)),
                      pl.BlockSpec((LEN,PAIR),lambda h,*_:(0,0)),
                      pl.BlockSpec((1,LEN),lambda h,*_:(0,0))],
            out_specs=[pl.BlockSpec((LEN,PAIR),lambda h,*_:(0,h)),
                       pl.BlockSpec((PAIR,LEN),lambda h,*_:(h,0)),
                       pl.BlockSpec((1,2,LEN),lambda h,*_:(h,0,0))],
            ),
        compiler_params=pltpu.CompilerParams(vmem_limit_bytes=VMEM_BYTES),
        cost_estimate=work(14.0),
        name="attn_fwd",
    )(meta,*[far(qkv)]*3,seg_col,seg_row)

def bwd_kernel(qb, win, lo_ref, q_ref, k_ref, v_ref, dm_ref, ot_ref, lse_ref, seg_col_ref, seg_row_ref, out_ref, dka, dva):
    dka[...]=jnp.zeros_like(dka); dva[...]=jnp.zeros_like(dva)
    c=LOG2E/math.sqrt(DH); scale=1.0/math.sqrt(DH)
    def block(i,_):
        r0=pl.multiple_of(i*qb,qb)
        q=q_ref[pl.ds(r0,qb),:]; dm=dm_ref[pl.ds(r0,qb),:]
        low=lax.broadcasted_iota(jnp.int32,(qb,PAIR),1)<DH
        zero=jnp.zeros_like(q)
        qs=(jnp.where(low,q,zero),jnp.where(low,zero,q))
        dms=(jnp.where(low,dm,zero),jnp.where(low,zero,dm))
        seg_q=seg_row_ref[:,pl.ds(r0,qb)]
        prod=dm.T.astype(f32)*ot_ref[:,pl.ds(r0,qb)].astype(f32)
        delta=[jnp.sum(prod[h*DH:(h+1)*DH],axis=0,keepdims=True) for h in range(2)]
        lse=[lse_ref[0,h:h+1,pl.ds(r0,qb)] for h in range(2)]
        def win_step(t,carry):
            start,seg_k=window(lo_ref,i,t,win,seg_col_ref)
            ok=jnp.concatenate([seg_k]*(qb//PAIR),axis=1)==seg_q
            kw=k_ref[pl.ds(start,win),:]; vw=v_ref[pl.ds(start,win),:]
            out=[]
            dk=dka[pl.ds(start,win),:]; dv=dva[pl.ds(start,win),:]
            for h in range(2):
                s=dot_nt(kw,qs[h])
                p=jnp.where(ok,jnp.exp2(s*c-lse[h]),0.0)
                dp=dot_nt(vw,dms[h])
                ds=(p*(dp-delta[h])).astype(bf16)
                dv=dv+dot_nn(p.astype(bf16),dms[h])
                dk=dk+dot_nn(ds,qs[h])
                out.append(carry[h]+dot_nn(kw.T[h*DH:(h+1)*DH],ds))
            dka[pl.ds(start,win),:]=dk; dva[pl.ds(start,win),:]=dv
            return tuple(out)
        init=jnp.zeros((DH,qb),f32)
        res=lax.fori_loop(0,lo_ref[1,i],win_step,(init,init))
        out_ref[0,pl.ds(r0,qb),:]=(jnp.concatenate(res,axis=0)*scale).T.astype(bf16)
        return 0
    single=lo_ref[2,0]==1
    @pl.when(single)
    def _():
        low=lax.broadcasted_iota(jnp.int32,(qb,PAIR),1)<DH
        def half(x,h):
            zero=jnp.zeros_like(x)
            return jnp.where(low,x,zero) if h==0 else jnp.where(low,zero,x)
        def products(i,h):
            start=pl.multiple_of(lo_ref[0,i],16)
            qh=half(q_ref[i*qb:(i+1)*qb,:],h); dmh=half(dm_ref[i*qb:(i+1)*qb,:],h)
            return dot_nt(k_ref[pl.ds(start,win),:],qh),dot_nt(v_ref[pl.ds(start,win),:],dmh),qh,dmh
        units=[(i,h) for i in range(LEN//qb) for h in range(2)]
        ahead=2
        queue=[products(*u) for u in units[:ahead]]
        dqs={}
        for n,(i,h) in enumerate(units):
            s,dp,qh,dmh=queue.pop(0)
            if n+ahead<len(units): queue.append(products(*units[n+ahead]))
            start=pl.multiple_of(lo_ref[0,i],16)
            rows=slice(i*qb,(i+1)*qb)
            if h==0:
                kt=k_ref[pl.ds(start,win),:].T
                prod=dm_ref[rows,:].T.astype(f32)*ot_ref[:,rows].astype(f32)
                ok=jnp.concatenate([seg_col_ref[pl.ds(start,win),:]]*(qb//PAIR),axis=1)==seg_row_ref[:,rows]
            delta=jnp.sum(prod[h*DH:(h+1)*DH],axis=0,keepdims=True)
            p=jnp.where(ok,jnp.exp2(s*c-lse_ref[0,h:h+1,rows]),0.0)
            ds=(p*(dp-delta)).astype(bf16)
            dva[pl.ds(start,win),:]+=dot_nn(p.astype(bf16),dmh)
            dka[pl.ds(start,win),:]+=dot_nn(ds,qh)
            dqs[h]=dot_nn(kt[h*DH:(h+1)*DH],ds)
            if h==1:
                out_ref[0,rows,:]=(jnp.concatenate([dqs[0],dqs[1]],axis=0)*scale).T.astype(bf16)
    @pl.when(jnp.logical_not(single))
    def _():
        lax.fori_loop(0,LEN//qb,block,0)
    out_ref[1]=(dka[...]*scale).astype(bf16)
    out_ref[2]=dva[...].astype(bf16)

def attn_bwd(qkv, dmixed, mixed_t, lse, meta, seg_col, seg_row, qb=256, win=512, h0=0, nh=6):
    np_=HEADS//2
    col=lambda off: pl.BlockSpec((LEN,PAIR),lambda h,*_:(0,off+h0+h))
    return pl.pallas_call(
        functools.partial(bwd_kernel,qb,win),
        out_shape=pltpu.VMEM((3,LEN,nh*PAIR),bf16),
        grid_spec=pltpu.PrefetchScalarGridSpec(num_scalar_prefetch=1,grid=(nh,),
            in_specs=[col(0),col(np_),col(2*np_),col(0),pl.BlockSpec((PAIR,LEN),lambda h,*_:(h0+h,0)),
                      pl.BlockSpec((1,2,LEN),lambda h,*_:(h0+h,0,0)),
                      pl.BlockSpec((LEN,PAIR),lambda h,*_:(0,0)),
                      pl.BlockSpec((1,LEN),lambda h,*_:(0,0))],
            out_specs=pl.BlockSpec((3,LEN,PAIR),lambda h,*_:(0,0,h)),
            scratch_shapes=[pltpu.VMEM((LEN,PAIR),f32),pltpu.VMEM((LEN,PAIR),f32)]),
        compiler_params=pltpu.CompilerParams(vmem_limit_bytes=VMEM_BYTES),
        cost_estimate=work(3.7 * nh),
        name="attn_bwd",
    )(meta,*[far(qkv)]*3,far(dmixed),far(mixed_t),lse,seg_col,seg_row)

ROWS = 256


def full(*shape):
    return pl.BlockSpec(shape, lambda *_: (0,) * len(shape))


def once(*shape):
    return pl.BlockSpec(shape, lambda *_: (0,) * len(shape), pipeline_mode=pl.Buffered(1))


def resident():
    return pl.BlockSpec(memory_space=pltpu.VMEM)


def rows_of(width):
    return pl.BlockSpec((ROWS, width), lambda i, *_: (i, 0))


def normalise(x):
    centred = x - jnp.mean(x, axis=-1, keepdims=True)
    rstd = lax.rsqrt(jnp.mean(centred * centred, axis=-1, keepdims=True) + EPS)
    return centred * rstd, rstd


def norm_back(u, gain, n, rstd):
    ug = u * gain
    return rstd * (
        ug - jnp.mean(ug, axis=-1, keepdims=True) - n * jnp.mean(ug * n, axis=-1, keepdims=True)
    )


def params():
    return pltpu.CompilerParams(vmem_limit_bytes=VMEM_BYTES)


def qkv_kernel(x_ref, gain_ref, shift_ref, w_ref, h1_ref, qkv_ref):
    n, _ = normalise(x_ref[...].astype(f32))
    h1 = (n * gain_ref[...][None] + shift_ref[...][None]).astype(bf16)
    h1_ref[...] = h1.T
    qkv_ref[...] = dot_nn(h1, w_ref[...]).astype(bf16)


def ln_qkv(tokens, gain, shift, w_qkv):
    t, d = tokens.shape
    return pl.pallas_call(
        qkv_kernel,
        grid=(t // ROWS,),
        in_specs=[rows_of(d), full(d), full(d), once(d, 3 * d)],
        out_specs=[pl.BlockSpec((d, ROWS), lambda i: (0, i)), rows_of(3 * d)],
        out_shape=(
            pltpu.HBM((d, t), bf16),
            pltpu.HBM((t, 3 * d), bf16),
        ),
        compiler_params=params(),
        cost_estimate=work(8.0),
        name="ln_qkv",
    )(far(tokens), gain, shift, far(w_qkv))


def prelude_kernel(n_slots, place_ref, seg_ref, slot_ref, meta_ref, info_ref, seg_col_ref, seg_row_ref,
                   valid_ref, voice_ref):
    seg = seg_ref[...]
    slot = slot_ref[...]
    per, lanes = seg.shape
    blocks = meta_ref.shape[1]
    rows = per // blocks
    pos = lax.broadcasted_iota(jnp.int32, seg.shape, 0) * lanes + lax.broadcasted_iota(
        jnp.int32, seg.shape, 1
    )
    most = 0
    for i in range(blocks):
        part = seg[i * rows:(i + 1) * rows]
        hit = jnp.logical_and(seg >= jnp.min(part), seg <= jnp.max(part))
        first = jnp.min(jnp.where(hit, pos, LEN))
        last = jnp.max(jnp.where(hit, pos + 1, 0))
        lo = jnp.minimum(first // 16 * 16, LEN - WIN)
        count = (last - lo + WIN - 1) // WIN
        meta_ref[0, i] = lo
        meta_ref[1, i] = count
        most = jnp.maximum(most, count)
    for i in range(blocks):
        meta_ref[2, i] = (most == 1).astype(jnp.int32)
    second = jnp.logical_and(slot >= n_slots // 2, slot < n_slots).astype(jnp.int32)
    first = (slot < n_slots // 2).astype(jnp.int32)
    info_ref[0] = jnp.max(second)
    info_ref[1] = jnp.sum(first)
    info_ref[2] = jnp.sum(second)
    lane = lax.broadcasted_iota(jnp.int32, voice_ref.shape, 1)
    voice = jnp.where(lane == place_ref[3], jnp.max(second).astype(f32), 0.0)
    voice = jnp.where(lane == 128, jnp.sum(first).astype(f32), voice)
    voice_ref[...] = jnp.where(lane == 129, jnp.sum(second).astype(f32), voice)
    seg = seg.astype(f32)
    valid = (slot < n_slots).astype(f32)
    for i in range(per):
        at = slice(i * lanes, (i + 1) * lanes)
        seg_row_ref[:, at] = seg[i:i + 1]
        seg_col_ref[at, :] = jnp.broadcast_to(seg[i:i + 1], (lanes, lanes)).T
        valid_ref[at, :] = jnp.broadcast_to(valid[i:i + 1], (lanes, lanes)).T


def prelude(place, seg_start, dispatch_slot, n_slots):
    t = seg_start.shape[0]
    smem = pl.BlockSpec(memory_space=pltpu.SMEM)
    vmem = pl.BlockSpec(memory_space=pltpu.VMEM)
    return pl.pallas_call(
        functools.partial(prelude_kernel, n_slots),
        in_specs=[smem, vmem, vmem],
        out_specs=[smem, smem, vmem, vmem, vmem, vmem],
        out_shape=(
            jax.ShapeDtypeStruct((3, LEN // QBLOCK), jnp.int32),
            jax.ShapeDtypeStruct((3,), jnp.int32),
            jax.ShapeDtypeStruct((t, PAIR), f32),
            jax.ShapeDtypeStruct((1, t), f32),
            jax.ShapeDtypeStruct((t, PAIR), f32),
            jax.ShapeDtypeStruct((1, 2 * PAIR), f32),
        ),
        cost_estimate=work(2.0),
        name="prelude",
    )(place, seg_start.reshape(t // PAIR, PAIR), dispatch_slot.reshape(t // PAIR, PAIR))


def proj_kernel(x_ref, mixed_ref, cot_ref, valid_ref, w_ref, gain_ref, shift_ref,
                resid_ref, h2_ref, cotm_ref):
    resid = x_ref[...].astype(f32) + dot_nn(mixed_ref[...], w_ref[...])
    resid_ref[...] = resid
    n, _ = normalise(resid)
    routed = jnp.concatenate([valid_ref[...]] * (resid.shape[1] // PAIR), axis=1) > 0.5
    h2 = n * gain_ref[...][None] + shift_ref[...][None]
    h2_ref[...] = jnp.where(routed, h2, 0.0).astype(bf16)
    cotm_ref[...] = jnp.where(routed, cot_ref[...].astype(f32), 0.0).astype(bf16)


def proj_ln(tokens, mixed, cotangent, valid, w_attn_out, gain, shift):
    t, d = tokens.shape
    return pl.pallas_call(
        proj_kernel,
        grid=(t // ROWS,),
        in_specs=[rows_of(d), rows_of(d), rows_of(d), rows_of(PAIR), full(d, d), full(d), full(d)],
        out_specs=[rows_of(d), rows_of(d), rows_of(d)],
        out_shape=(
            pltpu.HBM((t, d), f32),
            pltpu.VMEM((t, d), bf16),
            pltpu.VMEM((t, d), bf16),
        ),
        compiler_params=params(),
        cost_estimate=work(7.0),
        name="proj_ln",
    )(far(tokens), near(mixed), far(cotangent), valid, far(w_attn_out), gain, shift)


def gelu_parts(v):
    half = 0.5 * (1.0 + lax.erf(v * math.sqrt(0.5)))
    bell = jnp.exp(-0.5 * v * v) * (1.0 / math.sqrt(2.0 * math.pi))
    return v * half, half + v * bell


TOKENS_STEP = 256


def expert_kernel(axis, which_ref, place_ref, h2_ref, cot_ref, wina_ref, winb_ref, wouta_ref, woutb_ref,
                  hid_ref, dpre_ref, *out_refs):
    win = jnp.concatenate([wina_ref[0], winb_ref[0]], axis=1)
    wout = jnp.concatenate([wouta_ref[0], woutb_ref[0]], axis=0)
    hiddens, d_pres = [], []
    for at in range(0, h2_ref.shape[0], TOKENS_STEP):
        rows = slice(at, at + TOKENS_STEP)
        hidden, slope = gelu_parts(dot_nn(h2_ref[rows, :], win))
        hidden = hidden.astype(bf16)
        d_pre = (dot_nt(cot_ref[rows, :], wout) * slope).astype(bf16)
        hid_ref[rows, :] = hidden
        dpre_ref[rows, :] = d_pre
        hiddens.append(hidden)
        d_pres.append(d_pre)
    g_in = dot_tn(jnp.concatenate(d_pres, axis=0), h2_ref[...]).astype(bf16)
    g_out = dot_tn(jnp.concatenate(hiddens, axis=0), cot_ref[...]).astype(bf16)
    unit = wina_ref.shape[2]
    if axis is None:
        e = which_ref[0]
        for core in range(2):
            for j, g in enumerate((g_in, g_out)):
                part = g[core * unit:(core + 1) * unit]
                n_dp = out_refs[0].shape[1]
                step = unit // n_dp
                for to in range(n_dp):
                    piece = part[to * step:(to + 1) * step]
                    out_refs[0][core, to, e, j] = piece
                    out_refs[0][core, to, 1 - e, j] = jnp.zeros_like(piece)
    else:
        hold = out_refs[4]
        hold[0] = g_in
        hold[1] = g_out
        half = unit // 2
        for k in range(4):
            core, side = place_ref[0] ^ (k & 1), place_ref[axis] ^ (k >> 1)
            at = pl.multiple_of(core * unit + side * half, half)
            for j in range(2):
                out_refs[k][0, j] = hold[j, pl.ds(at, half), :]


def expert_part(which, place, h2, cot, w_in, w_out, p, axis, unit, n_z, n_dp=1):
    t, d = h2.shape
    parts = w_in.shape[2] // (unit * n_z * 2)

    def column(core):
        return pl.BlockSpec((1, d, unit), lambda z, w, _: (w[0], 0, parts * (2 * z + core) + p))

    def row(core):
        return pl.BlockSpec((1, unit, d), lambda z, w, _: (w[0], parts * (2 * z + core) + p, 0))

    if axis is None:
        step = unit // n_dp
        shapes = [pltpu.HBM((2 * n_z, n_dp, 2, 2, step, d), bf16)]
        specs = [pl.BlockSpec((2, n_dp, 2, 2, step, d), lambda z, *_: (z, 0, 0, 0, 0, 0))]
        scratch = []
    else:
        shapes = [pltpu.HBM((n_z, 2, unit // 2, d), bf16)] * 4
        specs = [pl.BlockSpec((1, 2, unit // 2, d), lambda z, *_: (z, 0, 0, 0))] * 4
        scratch = [pltpu.VMEM((2, 2 * unit, d), bf16)]
    act = (t, 2 * n_z * unit)
    act_spec = pl.BlockSpec((t, 2 * unit), lambda z, *_: (0, z))
    return pl.pallas_call(
        functools.partial(expert_kernel, axis),
        grid_spec=pltpu.PrefetchScalarGridSpec(
            num_scalar_prefetch=2,
            grid=(n_z,),
            in_specs=[resident(), resident(), column(0), column(1), row(0), row(1)],
            out_specs=[act_spec, act_spec] + specs,
            scratch_shapes=scratch,
        ),
        out_shape=[pltpu.HBM(act, bf16), pltpu.HBM(act, bf16)] + shapes,
        compiler_params=params(),
        cost_estimate=work(33.0 / parts),
        name="expert_part",
    )(which, place, near(h2), near(cot), *[far(w_in)] * 2, *[far(w_out)] * 2)


def in_order(refs, unit):
    blocks = refs[0].shape[1] // unit
    return jnp.concatenate(
        [r[:, b * unit:(b + 1) * unit] for b in range(blocks) for r in refs], axis=1
    )


def post_kernel(n, unit, which_ref, *refs):
    dpre_refs, rest = refs[:n], refs[n:]
    win_ref, resid_ref, cot_ref, w_ref, gain_ref, dres_ref, dbr_ref, dmix_ref, gvec_ref = rest
    u = dot_nt(in_order(dpre_refs, unit), win_ref[0]).astype(bf16).astype(f32)
    nrm, rstd = normalise(resid_ref[...])
    d_resid = cot_ref[...].astype(f32) + norm_back(u, gain_ref[...][None], nrm, rstd)
    dres_ref[...] = d_resid
    d_branch = d_resid.astype(bf16)
    dbr_ref[...] = d_branch
    dmix_ref[...] = dot_nt(d_branch, w_ref[...]).astype(bf16)
    gg = jnp.sum(u * nrm, axis=0, keepdims=True)
    gs = jnp.sum(u, axis=0, keepdims=True)
    step = pl.program_id(0)

    @pl.when(step == 0)
    def _():
        gvec_ref[0:1, :] = gg
        gvec_ref[1:2, :] = gs

    @pl.when(step > 0)
    def _():
        gvec_ref[0:1, :] += gg
        gvec_ref[1:2, :] += gs


def post_ffn(which, d_pres, w_in, resid, cotangent, w_attn_out, gain, unit):
    t, d = resid.shape
    n = len(d_pres)
    ff = w_in.shape[2]
    return pl.pallas_call(
        functools.partial(post_kernel, n, unit),
        grid_spec=pltpu.PrefetchScalarGridSpec(
            num_scalar_prefetch=1,
            grid=(t // ROWS,),
            in_specs=[rows_of(ff // n)] * n
            + [pl.BlockSpec((1, d, ff), lambda i, w: (w[0], 0, 0), pipeline_mode=pl.Buffered(1))]
            + [rows_of(d)] * 2
            + [full(d, d), full(d)],
            out_specs=[rows_of(d)] * 3 + [full(2, d)],
        ),
        out_shape=(
            pltpu.HBM((t, d), f32),
            pltpu.HBM((t, d), bf16),
            pltpu.HBM((t, d), bf16),
            jax.ShapeDtypeStruct((2, d), f32),
        ),
        compiler_params=params(),
        cost_estimate=work(10.0),
        name="post_ffn",
    )(which, *[far(v) for v in d_pres], far(w_in), far(resid), far(cotangent), far(w_attn_out), gain)


def result_kernel(n, unit, which_ref, *refs):
    wout_ref, resid_ref, out_ref = refs[n:]
    ffn = dot_nn(in_order(refs[:n], unit), wout_ref[0]).astype(bf16).astype(f32)
    out_ref[...] = (resid_ref[...] + ffn).astype(bf16)


def result_of(which, hiddens, w_out, resid, unit):
    t, d = resid.shape
    n = len(hiddens)
    ff = w_out.shape[1]
    return pl.pallas_call(
        functools.partial(result_kernel, n, unit),
        grid_spec=pltpu.PrefetchScalarGridSpec(
            num_scalar_prefetch=1,
            grid=(t // ROWS,),
            in_specs=[rows_of(ff // n)] * n
            + [pl.BlockSpec((1, ff, d), lambda i, w: (w[0], 0, 0), pipeline_mode=pl.Buffered(1)), rows_of(d)],
            out_specs=rows_of(d),
        ),
        out_shape=pltpu.HBM((t, d), bf16),
        compiler_params=params(),
        cost_estimate=work(8.0),
        name="result_of",
    )(which, *[far(v) for v in hiddens], far(w_out), far(resid))


def weight_kernel(c_ref, *refs):
    extra = len(refs) == 6
    h1_ref, d_ref = refs[:2]
    other_ref, mine_ref = refs[-2:]
    half = other_ref.shape[0]
    mine_at = pl.multiple_of(c_ref[0] * half, half)
    other_at = pl.multiple_of(half - c_ref[0] * half, half)

    def products(left_ref, right):
        other_ref[...] = dot_nn(left_ref[pl.ds(other_at, half), :], right).astype(bf16)
        mine_ref[...] = dot_nn(left_ref[pl.ds(mine_at, half), :], right).astype(bf16)

    if not extra:
        products(h1_ref, d_ref[0])
        return

    @pl.when(pl.program_id(0) < 3)
    def _():
        products(h1_ref, d_ref[0])

    @pl.when(pl.program_id(0) >= 3)
    def _():
        products(refs[2], refs[3][...])


def weight_grads(core, h1_t, d_qkv, more=()):
    d, t = h1_t.shape
    half, width = d // 2, d_qkv.shape[2]
    blocks = 3
    specs = [full(d, t), pl.BlockSpec((1, t, width), lambda i, c: (jnp.minimum(i, 2), 0, 0))]
    if more:
        specs += [full(d, t), pl.BlockSpec((t, width), lambda i, c: (0, jnp.maximum(i - 3, 0)))]
        blocks += more[1].shape[1] // width
    shape = pltpu.HBM((half, blocks * width), bf16)
    return pl.pallas_call(
        weight_kernel,
        grid_spec=pltpu.PrefetchScalarGridSpec(
            num_scalar_prefetch=1,
            grid=(blocks,),
            in_specs=specs,
            out_specs=[pl.BlockSpec((half, width), lambda i, c: (0, i))] * 2,
        ),
        out_shape=(shape, shape),
        compiler_params=params(),
        cost_estimate=work(1.2 * blocks * width / half),
        name="weight_grads",
    )(core, far(h1_t), near(d_qkv), *[far(v) for v in more])


def input_kernel(groups, *refs):
    ins, (x_ref, dres_ref, w_ref, gain_ref, gtok_ref, gvec_ref) = refs[:groups], refs[groups:]
    side = jnp.concatenate([r[j] for j in range(3) for r in ins], axis=1)
    u = dot_nt(side, w_ref[...])
    n, rstd = normalise(x_ref[...].astype(f32))
    gtok_ref[...] = dres_ref[...] + norm_back(u, gain_ref[...][None], n, rstd)
    gg = jnp.sum(u * n, axis=0, keepdims=True)
    gs = jnp.sum(u, axis=0, keepdims=True)
    first = pl.program_id(0) == 0

    @pl.when(first)
    def _():
        gvec_ref[0:1, :] = gg
        gvec_ref[1:2, :] = gs

    @pl.when(jnp.logical_not(first))
    def _():
        gvec_ref[0:1, :] += gg
        gvec_ref[1:2, :] += gs


def input_grad(parts, tokens, d_resid, w_qkv, gain):
    t, d = tokens.shape
    return pl.pallas_call(
        functools.partial(input_kernel, len(parts)),
        grid=(t // ROWS,),
        in_specs=[pl.BlockSpec((3, ROWS, p.shape[2]), lambda i: (0, i, 0)) for p in parts]
        + [rows_of(d), rows_of(d), once(d, 3 * d), full(d)],
        out_specs=[rows_of(d), full(2, d)],
        out_shape=(
            pltpu.HBM((t, d), f32),
            jax.ShapeDtypeStruct((2, d), f32),
        ),
        compiler_params=params(),
        cost_estimate=work(10.0),
        name="input_grad",
    )(*[far(p) for p in parts], far(tokens), far(d_resid), far(w_qkv), gain)


def sum_kernel(axis, place_ref, voice_ref, a_ref, b_ref, c_ref, d_ref, keep_ref, send_ref):
    me = place_ref[3]
    bit = place_ref[3 - axis]
    step = keep_ref.shape[3]
    for j in range(2):
        for out_ref, mine in ((keep_ref, bit), (send_ref, 1 - bit)):
            at = pl.multiple_of(mine * step, step)
            sides = [None, None]
            for k, ref in enumerate((a_ref, b_ref, c_ref, d_ref)):
                term = ref[0, j, pl.ds(at, step), :].astype(f32)
                second = voice_ref[me ^ ((k & 1) | ((k >> 1) << axis))] == 1
                for e in range(2):
                    part = jnp.where(second, term if e else 0.0, 0.0 if e else term)
                    sides[e] = part if sides[e] is None else sides[e] + part
            for e in range(2):
                out_ref[0, e, j] = sides[e].astype(bf16)


def sum_sides(axis, place, voice, got):
    n_z, two, rows, d = got[0].shape
    spec = pl.BlockSpec((1, two, rows, d), lambda z, *_: (z, 0, 0, 0))
    out = pl.BlockSpec((1, 2, two, rows // 2, d), lambda z, *_: (z, 0, 0, 0, 0))
    shape = jax.ShapeDtypeStruct((n_z, 2, two, rows // 2, d), bf16)
    return pl.pallas_call(
        functools.partial(sum_kernel, axis),
        grid_spec=pltpu.PrefetchScalarGridSpec(
            num_scalar_prefetch=2,
            grid=(n_z,),
            in_specs=[spec] * 4,
            out_specs=[out, out],
        ),
        out_shape=(shape, shape),
        compiler_params=params(),
        cost_estimate=work(3.0),
        name="sum_sides",
    )(place, voice, *[near(v) for v in got])


def finish_kernel(axes, place_ref, tally_ref, *refs):
    near_ref, last_ref, gin_ref, gout_ref, counts_ref, hold_ref = refs
    d = gin_ref.shape[1]
    lane = lax.broadcasted_iota(jnp.int32, tally_ref.shape, 1)
    counts = [jnp.sum(jnp.where(lane == 128 + e, tally_ref[...], 0.0)) for e in range(2)]
    for e in range(2):
        counts_ref[e] = counts[e].astype(jnp.int32)
    unit = hold_ref.shape[0]
    step = unit // 4
    for p, axis in enumerate(axes):
        for e in range(2):
            factor = jnp.full((1, d), counts[0] + counts[1], f32) / (2.0 * counts[e])
            for j in range(2):
                for k in range(4):
                    x, y = k & 1, k >> 1
                    if p < 2:
                        x, y = place_ref[1] ^ x, place_ref[2] ^ y
                        piece = near_ref[k, p, e, j]
                    else:
                        piece = last_ref[k, 0, e, j]
                    to = 2 * x + y if axis == X else 2 * y + x
                    rows = pl.ds(pl.multiple_of(to * step, step), step)
                    hold_ref[rows, :] = piece.astype(f32) * factor
                where = slice(p * unit, (p + 1) * unit)
                if j == 0:
                    gin_ref[e, :, where] = hold_ref[...].T
                else:
                    gout_ref[e, where, :] = hold_ref[...]


def finish_experts(axes, place, tally, blocks):
    step, d = blocks[0].shape[-2:]
    n = len(axes)
    smem = pl.BlockSpec(memory_space=pltpu.SMEM)
    return pl.pallas_call(
        functools.partial(finish_kernel, axes),
        in_specs=[smem] + [resident()] * (1 + len(blocks)),
        out_specs=[resident(), resident(), smem],
        out_shape=(
            jax.ShapeDtypeStruct((2, d, n * 4 * step), f32),
            jax.ShapeDtypeStruct((2, n * 4 * step, d), f32),
            jax.ShapeDtypeStruct((2,), jnp.int32),
        ),
        scratch_shapes=[pltpu.VMEM((4 * step, d), f32)],
        compiler_params=params(),
        cost_estimate=work(4.0),
        name="finish_experts",
    )(place, tally, *[near(v) for v in blocks])


def join_kernel(widths, place_ref, *refs):
    n = len(widths)
    gw_ref, gwo_ref, vec_ref = refs[2 * n:]
    d = gwo_ref.shape[2]
    rows = gwo_ref.shape[1]
    rel = pl.program_id(0) ^ (place_ref[3] >> 1)
    at = place_ref[3] >> 1
    vec = refs[2 * n - 2][at, rows:, :d].astype(f32) + refs[2 * n - 1][at, rows:, :d].astype(f32)
    vec_ref[...] = vec[:8]
    before = 0
    for k, width in enumerate(widths):
        for half, ref in ((place_ref[0], refs[2 * k]), (1 - place_ref[0], refs[2 * k + 1])):
            for third in range(3):
                at, src = third * d + before, third * width
                gw_ref[half, :, at:at + width] = ref[rel, :rows, src:src + width].astype(f32)
            if k == 0:
                gwo_ref[half] = ref[rel, :rows, 3 * width:].astype(f32)
        before += width


def join_weights(place, sums, d):
    step = d // 8
    extra = [d] + [0] * (len(sums) - 1)
    widths = [(s[0].shape[2] - x) // 3 for s, x in zip(sums, extra)]
    flat = [v for pair in sums for v in pair]
    gw, gwo, vec = pl.pallas_call(
        functools.partial(join_kernel, widths),
        grid_spec=pltpu.PrefetchScalarGridSpec(
            num_scalar_prefetch=1,
            grid=(4,),
            in_specs=[resident()] * len(flat),
            out_specs=[
                pl.BlockSpec((2, step, 3 * d), lambda i, *_: (0, i, 0)),
                pl.BlockSpec((2, step, d), lambda i, *_: (0, i, 0)),
                full(8, d),
            ],
        ),
        out_shape=(
            jax.ShapeDtypeStruct((2, d // 2, 3 * d), f32),
            jax.ShapeDtypeStruct((2, d // 2, d), f32),
            jax.ShapeDtypeStruct((8, d), f32),
        ),
        compiler_params=params(),
        cost_estimate=work(5.0),
        name="join_weights",
    )(place, *[near(v) for v in flat])
    return gw.reshape(d, 3 * d), gwo.reshape(d, d), vec


X, Y = 1, 2
NEAR = [(0, 1), (1, 0), (2, 3), (3, 2)]
FAR = [(0, 3), (3, 0), (1, 2), (2, 1)]


def swap_core(v):
    return lax.ppermute(v, "core", [(0, 1), (1, 0)])


def swap(v, axis):
    return lax.ppermute(v, "dp", [(i, i ^ axis) for i in range(4)])


def swap_both(v, axis):
    return lax.ppermute(v, ("dp", "core"), [(i, i ^ (1 | (axis << 1))) for i in range(8)])


def along_z(v, pairs):
    return lax.ppermute(v, "z", pairs)


def tie(v, *after):
    return lax.optimization_barrier((v,) + after)[0] if after else v


def small_kernel(fn, *refs):
    out_ref = refs[-1]
    out_ref[...] = fn(*[r[...] for r in refs[:-1]]).astype(out_ref.dtype)


def small(fn, *args, space=pltpu.VMEM, name="small"):
    shape = jax.eval_shape(fn, *args)
    return pl.pallas_call(
        functools.partial(small_kernel, fn),
        in_specs=[resident()] * len(args),
        out_specs=resident(),
        out_shape=pltpu.VMEM(shape.shape, args[0].dtype),
        compiler_params=params(),
        cost_estimate=work(1.0),
        name=name,
    )(*[near(v) for v in args])


def add_f32(a, b):
    return a.astype(f32) + b.astype(f32)


def add(a, b):
    return small(add_f32, a, b, name="add")


def merge_kernel(mine_ref, away_ref, first_ref, second_ref, out_ref):
    n, rows, width = out_ref.shape
    rows -= 16
    d = first_ref.shape[1]
    for k in range(n):
        at = slice(k * rows, (k + 1) * rows)
        out_ref[k, :rows] = (mine_ref[at, :].astype(f32) + away_ref[at, :].astype(f32)).astype(bf16)
        out_ref[k, rows:] = jnp.zeros((16, width), bf16)
    small = jnp.concatenate([first_ref[...], second_ref[...], jnp.zeros((12, d), f32)], axis=0)
    out_ref[0, rows:, :d] = small.astype(bf16)


def merge_small(mine, away, first, second):
    half, width = mine.shape
    return pl.pallas_call(
        merge_kernel,
        in_specs=[resident()] * 4,
        out_specs=resident(),
        out_shape=pltpu.VMEM((4, half // 4 + 16, width), bf16),
        compiler_params=params(),
        cost_estimate=work(1.0),
        name="merge_small",
    )(near(mine), near(away), first, second)


def split_kernel(axis, place_ref, *refs):
    keep_ref, send_ref = refs[-2:]
    bit = place_ref[axis]
    for out_ref, at in ((keep_ref, bit), (send_ref, 1 - bit)):
        v = refs[0][at]
        for r in refs[1:-2]:
            v = v.astype(f32) + r[at].astype(f32)
        out_ref[...] = v.astype(bf16)


def split(place, axis, *v):
    shape = pltpu.VMEM(v[0].shape[1:], bf16)
    return pl.pallas_call(
        functools.partial(split_kernel, axis),
        in_specs=[pl.BlockSpec(memory_space=pltpu.SMEM)] + [resident()] * len(v),
        out_specs=[resident()] * 2,
        out_shape=(shape, shape),
        compiler_params=params(),
        cost_estimate=work(1.0),
        name="split",
    )(place, *[near(x) for x in v])


def total(v):
    return small(lambda x: sum(x[k].astype(f32) for k in range(x.shape[0])), v, name="total")


def stack(*v):
    return small(lambda *x: jnp.stack(x), *v, name="stack")


class Line:
    def __init__(self):
        self.last = ()

    def __call__(self, step, first, *rest):
        out = step(tie(first, *self.last), *rest)
        self.last = (jax.tree.leaves(out)[0],)
        return out


UNIT = 128
QBLOCK = 256
WIN = 512
GROUPS = (3, 3)


def tuned(tokens, cotangent, seg_start, dispatch_slot, ln1_gain, ln1_shift, w_qkv, w_attn_out,
          ln2_gain, ln2_shift, w_in, w_out):
    tok_count, d = tokens.shape
    n_z = lax.axis_size("z")
    n_slots = 2 * n_z * (2 * tok_count // (2 * n_z))
    core, dp = lax.axis_index("core"), lax.axis_index("dp")
    bits = {X: dp & 1, Y: dp >> 1}
    place = jnp.stack([core, bits[X], bits[Y], dp * 2 + core]).astype(jnp.int32)
    line = Line()
    PHASE[0] = "early"

    def around(v):
        return [v, swap(v, X), swap(v, Y), swap(v, X | Y)]

    def exchange(v):
        return lax.all_to_all(v, "dp", split_axis=0, concat_axis=0, tiled=True)

    def merge(a, b):
        return small(add_f32, a, b, name="merge").reshape(4, -1, a.shape[1])

    meta, info, seg_col, seg_row, valid, voice = prelude(place, seg_start, dispatch_slot, n_slots)
    away = swap_core(voice)
    h1_t, qkv = line(ln_qkv, tokens, ln1_gain, ln1_shift, w_qkv)
    voice = line(add, voice, away)
    away = swap(voice, X)
    mixed, mixed_t, lse = line(
        lambda v: attn_fwd(v, meta, seg_col, seg_row, QBLOCK, WIN), qkv
    )
    voice = line(add, voice, away)
    away = swap(voice, Y)
    resid, h2, cotm = line(
        lambda v: proj_ln(tokens, v, cotangent, valid, w_attn_out, ln2_gain, ln2_shift), mixed
    )
    tally = line(add, voice, away)
    voice = tally[0, :8].astype(jnp.int32)

    def expert(p, axis):
        return line(
            lambda v: expert_part(info, place, v, cotm, w_in, w_out, p, axis, UNIT, n_z, 4), h2
        )

    def plane(pieces, axis):
        return [pieces[0], swap_core(pieces[1]), swap(pieces[2], axis), swap_both(pieces[3], axis)]

    hid_b, dpre_b, *out_b = expert(1, X)
    got_b = plane(out_b, X)
    hid_a, dpre_a, out_a = expert(0, None)
    own_a = lax.psum_scatter(out_a, ("z", "core"), scatter_dimension=0, tiled=True)
    hid_c, dpre_c, *out_c = expert(2, Y)
    got_c = plane(out_c, Y)
    d_resid, d_branch, d_mixed, gvec2 = line(
        lambda v: post_ffn(
            info, (dpre_a, v, dpre_c), w_in, resid, cotangent, w_attn_out, ln2_gain, UNIT
        ),
        dpre_b,
    )

    def sides(got, axis):
        return line(lambda v: sum_sides(axis, place, voice, (got[0], got[1], got[2], v)), got[3])

    def bwd(at, nh):
        return line(
            lambda v: attn_bwd(qkv, v, mixed_t, lse, meta, seg_col, seg_row, QBLOCK, WIN, at, nh),
            d_mixed,
        )

    def scatter_z(v):
        return lax.psum_scatter(v, "z", scatter_dimension=0, tiled=True)[0]

    one, two = GROUPS
    keep_b, send_b = sides(got_b, X)
    away_b = swap(send_b, Y)
    d_qkv_1 = bwd(0, one)
    other_1, mine_1 = line(lambda v: weight_grads(place, v, d_qkv_1, (mixed_t, d_branch)), h1_t)
    away_1 = swap_core(other_1)
    keep_c, send_c = sides(got_c, Y)
    away_c = swap(send_c, X)
    both_b = line(add, keep_b, away_b)
    half_b = scatter_z(both_b)
    keep_a, send_a = line(lambda v: split(place, Y, v.reshape((2, 2) + v.shape[1:])), own_a[0])
    away_a = swap(send_a, Y)
    all_1 = exchange(line(merge, mine_1, away_1))
    d_qkv_2 = bwd(one, two)
    PHASE[0] = "late"
    PHASE[0] = "early"
    other_2, mine_2 = line(lambda v: weight_grads(place, v, d_qkv_2), h1_t)
    away_2 = swap_core(other_2)
    PHASE[0] = "late"
    both_c = line(add, keep_c, away_c)
    half_c = scatter_z(both_c)
    keep_a, send_a = line(lambda a, b: split(place, X, a, b), keep_a, away_a)
    away_a = swap(send_a, X)
    piece_1 = line(total, all_1)
    away_1 = along_z(piece_1, NEAR)

    def copies(*v):
        return small(lambda *x: jnp.stack([jnp.stack(x)] * 4), *v, name="copies")

    away_t = along_z(tie(tally, mine_2), NEAR)
    grad_tokens, gvec1 = line(
        lambda v: input_grad((d_qkv_1, d_qkv_2), v, d_resid, w_qkv, ln1_gain), tokens
    )
    all_2 = exchange(line(lambda a, b: merge_small(a, b, gvec1, gvec2), mine_2, away_2))
    piece_1 = line(add, piece_1, away_1)
    away_1 = along_z(piece_1, FAR)
    tally = line(add, tally, away_t)
    away_t = along_z(tally, FAR)
    half_a = line(add, keep_a, away_a)
    around_ab = around(line(stack, half_a, half_b))
    result_out = line(lambda v: result_of(info, (hid_a, hid_b, hid_c), w_out, v, UNIT), resid)
    piece_2 = line(total, all_2)
    away_2 = along_z(piece_2, NEAR)
    PHASE[0] = "tail"
    all_e = exchange(line(copies, half_c))
    block_ab = line(stack, *around_ab)
    piece_2 = line(add, piece_2, away_2)
    away_2 = along_z(piece_2, FAR)
    piece_1 = line(add, piece_1, away_1)
    around_1 = around(piece_1)
    piece_2 = line(add, piece_2, away_2)
    around_2 = around(piece_2)
    whole_1 = line(stack, *around_1)
    other_1 = swap_core(whole_1)
    tally = line(add, tally, away_t)
    grad_w_in, grad_w_out, all_counts = line(
        lambda v: finish_experts((Y, X, Y), place, tie(tally, piece_2), (block_ab, v)), all_e
    )
    whole_2 = line(stack, *around_2)
    other_2 = swap_core(whole_2)
    grad_wqkv, grad_wo, vectors = join_weights(
        place, ((tie(whole_1, *line.last), other_1), (whole_2, other_2)), d
    )
    PHASE[0] = "early"
    return (
        result_out, grad_tokens, vectors[0], vectors[1], grad_wqkv, grad_wo, vectors[2], vectors[3],
        grad_w_in, grad_w_out, all_counts,
    )


def general(tokens, cotangent, seg_start, dispatch_slot, ln1_gain, ln1_shift, w_qkv, w_attn_out,
            ln2_gain, ln2_shift, w_in, w_out):
    tok_count, d = tokens.shape
    n_expert = lax.axis_size("expert")
    n_slots = n_expert * (2 * tok_count // n_expert)
    everywhere = ("dp", "expert")
    first_half = jnp.zeros((1,), jnp.int32)
    meta, info, seg_col, seg_row, valid, _ = prelude(
        jnp.zeros((4,), jnp.int32), seg_start, dispatch_slot, n_slots
    )
    h1_t, qkv = ln_qkv(tokens, ln1_gain, ln1_shift, w_qkv)
    mixed, mixed_t, lse = attn_fwd(qkv, meta, seg_col, seg_row, QBLOCK, WIN)
    resid, h2, cotm = proj_ln(tokens, mixed, cotangent, valid, w_attn_out, ln2_gain, ln2_shift)
    blocks = w_in.shape[2] // (UNIT * 2)
    hidden, d_pre, grads = expert_part(
        info, first_half, h2, cotm, w_in, w_out, 0, None, UNIT, blocks
    )
    grads = jnp.transpose(grads[:, 0], (1, 2, 0, 3, 4)).reshape(2, 2, 2 * blocks * UNIT, d)
    grads = lax.psum_scatter(grads, "expert", scatter_dimension=2, tiled=True)
    grads = lax.psum(grads, "dp").astype(f32)
    d_resid, d_branch, d_mixed, gvec2 = post_ffn(
        info, (d_pre,), w_in, resid, cotangent, w_attn_out, ln2_gain, UNIT
    )
    result_out = result_of(info, (hidden,), w_out, resid, UNIT)
    d_qkv = attn_bwd(qkv, d_mixed, mixed_t, lse, meta, seg_col, seg_row, QBLOCK, WIN)
    bottom, top = weight_grads(first_half, h1_t, d_qkv, (mixed_t, d_branch))
    grad_tokens, gvec1 = input_grad((d_qkv,), tokens, d_resid, w_qkv, ln1_gain)
    weights = lax.psum(jnp.concatenate([top, bottom], axis=0), everywhere).astype(f32)
    grad_wqkv, grad_wo = weights[:, : 3 * d], weights[:, 3 * d:]
    counts, gvec1, gvec2 = lax.psum((info[1:].astype(f32), gvec1, gvec2), everywhere)
    factor = (jnp.sum(counts) / (2.0 * counts))[:, None, None]
    return (
        result_out, grad_tokens, gvec1[0], gvec1[1], grad_wqkv, grad_wo,
        gvec2[0], gvec2[1], jnp.transpose(grads[:, 0], (0, 2, 1)) * factor, grads[:, 1] * factor,
        counts.astype(jnp.int32),
    )


def solution(mesh):
    n_dp, n_expert = mesh.shape["dp"], mesh.shape["expert"]
    if (n_dp, n_expert) == (4, 8):
        mesh = Mesh(mesh.devices.reshape(n_dp, n_expert // 2, 2), ("dp", "z", "core"))
        body, expert = tuned, ("z", "core")
    else:
        body, expert = general, ("expert",)
    everywhere = ("dp",) + expert
    rows = P(everywhere, None)
    flat = P(everywhere)
    rep = P()
    return jax.shard_map(
        body,
        mesh=mesh,
        in_specs=(rows, rows, flat, flat) + (rep,) * 8,
        out_specs=(rows, rows) + (rep,) * 6 + (P(None, None, expert), P(None, expert, None), rep),
        check_vma=False,
    )
```
